32 devices in a mesh: head: 4 (over y, x), seq: 8 (over z, core).
Axes of the slice: x: 2, y: 2, z: 4, core: 2. Of those that a mesh axis runs over, the one named last changes fastest.
Arguments:
- frames: bfloat16 [2, 8, 1024, 512], P(None, 'seq', 'head'), may hold values from -6 to 6
- cotangent: bfloat16 [2, 8, 1024, 512], P(None, 'seq', 'head'), may hold values from -6 to 6
- lengths: int32 [2, 8, 4], P(None, 'seq'), may hold values from 1 to 512, 1024 in all within a row
- gain_first: bfloat16 [512], P(('head', 'seq')), may hold values from 0.3984375 to 1.59375
- first_in: bfloat16 [512, 2048], P(('head', 'seq')), may hold values from -0.25 to 0.25
- first_out: bfloat16 [2048, 512], P(('head', 'seq')), may hold values from -0.125 to 0.125
- gain_attend: bfloat16 [512], P(('head', 'seq')), may hold values from 0.3984375 to 1.59375
- head_projection: bfloat16 [512, 1536], P(('head', 'seq')), may hold values from -0.25 to 0.25
- output_projection: bfloat16 [512, 512], P(('head', 'seq')), may hold values from -2 to 2
- gain_gated: bfloat16 [512], P(('head', 'seq')), may hold values from 0.3984375 to 1.59375
- gated_up: bfloat16 [512, 3072], P(('head', 'seq')), may hold values from -0.25 to 0.25
- gain_gate: bfloat16 [1536], P(('head', 'seq')), may hold values from 0.3984375 to 1.59375
- kernel_gate: bfloat16 [31, 1536], P(None, ('head', 'seq')), may hold values from -1 to 1
- gated_down: bfloat16 [1536, 512], P(('head', 'seq')), may hold values from -0.15625 to 0.15625
- kernel_merge: bfloat16 [31, 1024], P(None, ('head', 'seq')), may hold values from -1 to 1
- merge_weight: bfloat16 [1024, 512], P(('head', 'seq')), may hold values from -0.1875 to 0.1875
- gain_second: bfloat16 [512], P(('head', 'seq')), may hold values from 0.3984375 to 1.59375
- second_in: bfloat16 [512, 2048], P(('head', 'seq')), may hold values from -0.25 to 0.25
- second_out: bfloat16 [2048, 512], P(('head', 'seq')), may hold values from -0.125 to 0.125
- gain_final: bfloat16 [512], P(('head', 'seq')), may hold values from 0.3984375 to 1.59375
Outputs:
- output_frames: bfloat16 [2, 8, 1024, 512], P(None, 'seq', 'head')
- grad_frames: float32 [2, 8, 1024, 512], P(None, 'seq', 'head')
- grad_gain_first: float32 [512], P(('head', 'seq'))
- grad_first_in: float32 [512, 2048], P(('head', 'seq'))
- grad_first_out: float32 [2048, 512], P(('head', 'seq'))
- grad_gain_attend: float32 [512], P(('head', 'seq'))
- grad_head_projection: float32 [512, 1536], P(('head', 'seq'))
- grad_output_projection: float32 [512, 512], P(('head', 'seq'))
- grad_gain_gated: float32 [512], P(('head', 'seq'))
- grad_gated_up: float32 [512, 3072], P(('head', 'seq'))
- grad_gain_gate: float32 [1536], P(('head', 'seq'))
- grad_kernel_gate: float32 [31, 1536], P(None, ('head', 'seq'))
- grad_gated_down: float32 [1536, 512], P(('head', 'seq'))
- grad_kernel_merge: float32 [31, 1024], P(None, ('head', 'seq'))
- grad_merge_weight: float32 [1024, 512], P(('head', 'seq'))
- grad_gain_second: float32 [512], P(('head', 'seq'))
- grad_second_in: float32 [512, 2048], P(('head', 'seq'))
- grad_second_out: float32 [2048, 512], P(('head', 'seq'))
- grad_gain_final: float32 [512], P(('head', 'seq'))
The draws below stay inside these ranges and needn't reach their ends.
Inputs may be any that keep to these rules, and one draw needn't show every extreme that they name: The 4 lengths of a stream sum to 1024, and every stream has one utterance of exactly 512 frames.
All inputs are finite; a program needn't handle non-finite values.
Results may differ from the reference program's by a relative error of at most 0.018.
Values may be sent and summed in bfloat16 or wider, within the bound.
No kernel may reach another device: no remote copies, remote signals or barrier semaphores. Data moves between devices by JAX's collectives and lax.ppermute only.
A program may use at most 120 MiB of HBM per device.

```python
import math
import jax
import jax.numpy as jnp
import numpy as np
from jax import lax

D = 512
HEADS = 8
HD = 64
FF = 2048
CG = 3072
KER = 31
FRAME_DEV = 256
MICRO = 2
STREAMS = 8
STREAM_LEN = 1024
UTTS = 4
LONGEST = 512
N_HEAD = 4


def block_levels(stream_key, shape, cuts, least, high):
    def one(axis_at, shards_of):
        steps = jax.random.uniform(jax.random.fold_in(jax.random.fold_in(stream_key, 6), axis_at), (shards_of,), jnp.float32, least / len(cuts), high / len(cuts))
        return jnp.repeat(jnp.exp(steps), shape[axis_at] // shards_of).reshape((-1,) + (1,) * (len(shape) - axis_at - 1))

    factor_of = one(*cuts[0])
    for cut in cuts[1:]:
        factor_of = factor_of * one(*cut)
    return factor_of


def length_profile(count, total, bound, skew):
    weights = [(1 << 20) // math.isqrt(grade ** skew) + 1 for grade in range(2, count + 1)]
    rest, given = total - bound - (count - 1), [1] * (count - 1)
    while rest > 0:
        movable = [i for i in range(count - 1) if given[i] < bound]
        whole, left = sum([weights[i] for i in movable]), rest
        for i in movable:
            addition = min(bound - given[i], max(1, left * weights[i] // whole), rest)
            given[i] = given[i] + addition
            rest = rest - addition
    return np.array([bound] + given)


def ragged_sizes(own_key, count, total, bound, skew):
    if count == 2:
        one = jax.random.randint(own_key, (), max(1, total - bound), min(bound, total - 1) + 1)
        return jnp.stack([one, total - one])
    sizes = jnp.asarray(length_profile(count, total, bound, skew), jnp.int32)
    pairs = (count - 1) // 2
    source_of, sink = sizes[1:1 + 2 * pairs:2], sizes[2:2 + 2 * pairs:2]
    slack = jnp.minimum(source_of - 1, bound - sink)
    shifted = jax.random.randint(jax.random.fold_in(own_key, 1), (pairs,), 0, 1 << 20) % (slack + 1)
    sizes = sizes.at[1:1 + 2 * pairs:2].set(source_of - shifted).at[2:2 + 2 * pairs:2].set(sink + shifted)
    return sizes[jax.random.permutation(jax.random.fold_in(own_key, 2), count)]


def centred(key, shape, scale, most, pieces=(), kind=jnp.bfloat16):
    gain = block_levels(key, shape, pieces, -0.22, 0.18) if pieces else 1.0
    values = jax.random.normal(key, shape, jnp.float32) * scale * gain
    return jnp.minimum(jnp.maximum(values, -most), most).astype(kind)


def setup_inputs(seed: int = 0) -> dict:
    key_of = jax.random.split(jax.random.key(seed), 21)
    return {
        "frames": centred(key_of[0], (MICRO, STREAMS, STREAM_LEN, D), 1.0, 6.0, ((1, 8), (2, 4))),
        "cotangent": centred(key_of[1], (MICRO, STREAMS, STREAM_LEN, D), 1.0, 6.0, ((1, 8), (2, 4))),
        "lengths": jax.vmap(lambda own: ragged_sizes(own, UTTS, FRAME_DEV * N_HEAD, LONGEST, 2))(jax.random.split(key_of[2], MICRO * STREAMS)).reshape((MICRO, STREAMS, UTTS)).astype(jnp.int32),
        "gain_first": jnp.clip(1.0 + 0.12 * jax.random.normal(key_of[3], (D,), jnp.float32), 0.3984375, 1.59375).astype(jnp.bfloat16),
        "first_in": centred(key_of[4], (D, FF), D ** -0.5, 0.25, ((0, 32),)),
        "first_out": centred(key_of[5], (FF, D), FF ** -0.5, 0.125, ((0, 32),)),
        "gain_attend": jnp.clip(1.0 + 0.12 * jax.random.normal(key_of[6], (D,), jnp.float32), 0.3984375, 1.59375).astype(jnp.bfloat16),
        "head_projection": centred(key_of[7], (D, 3 * D), D ** -0.5, 0.25, ((0, 32),)),
        "output_projection": centred(key_of[8], (D, D), (D // 64) ** -0.5, 2.0, ((0, 32),)),
        "gain_gated": jnp.clip(1.0 + 0.12 * jax.random.normal(key_of[9], (D,), jnp.float32), 0.3984375, 1.59375).astype(jnp.bfloat16),
        "gated_up": centred(key_of[10], (D, CG), D ** -0.5, 0.25, ((0, 32),)),
        "gain_gate": jnp.clip(1.0 + 0.12 * jax.random.normal(key_of[11], (CG // 2,), jnp.float32), 0.3984375, 1.59375).astype(jnp.bfloat16),
        "kernel_gate": centred(key_of[12], (KER, CG // 2), KER ** -0.5, 1.0, ((1, 32),)),
        "gated_down": centred(key_of[13], (CG // 2, D), (CG // 2) ** -0.5, 0.15625, ((0, 32),)),
        "kernel_merge": centred(key_of[14], (KER, 2 * D), KER ** -0.5, 1.0, ((1, 32),)),
        "merge_weight": centred(key_of[15], (2 * D, D), (2 * D) ** -0.5, 0.1875, ((0, 32),)),
        "gain_second": jnp.clip(1.0 + 0.12 * jax.random.normal(key_of[16], (D,), jnp.float32), 0.3984375, 1.59375).astype(jnp.bfloat16),
        "second_in": centred(key_of[17], (D, FF), D ** -0.5, 0.25, ((0, 32),)),
        "second_out": centred(key_of[18], (FF, D), FF ** -0.5, 0.125, ((0, 32),)),
        "gain_final": jnp.clip(1.0 + 0.12 * jax.random.normal(key_of[19], (D,), jnp.float32), 0.3984375, 1.59375).astype(jnp.bfloat16),
    }


@jax.custom_vjp
def low(v):
    return lax.optimization_barrier(v.astype(jnp.bfloat16)).astype(jnp.float32)

@jax.custom_vjp
def low_back(v):
    return v

def low_keep(v):
    return (low(v), None)

def low_pass(kept, grad):
    return (grad,)

def back_keep(v):
    return (v, None)

def back_low(kept, grad):
    return (low(grad),)
low.defvjp(low_keep, low_pass)
low_back.defvjp(back_keep, back_low)
EPSILON = 1e-05

def matmul(left, right):
    return jnp.dot(left, right, precision=lax.Precision.HIGHEST)

def layer_norm(values, gain_vector):
    centre = values - lax.optimization_barrier(jnp.mean(values, axis=-1, keepdims=True))
    scaling = lax.rsqrt(lax.optimization_barrier(jnp.mean(centre * centre, axis=-1, keepdims=True)) + EPSILON)
    return centre * scaling * gain_vector

def exact_gelu(values):
    return jax.nn.gelu(values, approximate=False)

def segment_index(positions, lengths):
    boundary = jnp.cumsum(lengths)
    return lax.optimization_barrier(jnp.sum((positions[:, None] >= boundary[None, :]).astype(jnp.int32), axis=1))

def rotary_tables(frame_count, head_width):
    half_width = head_width // 2
    frequency = jnp.exp(jnp.arange(half_width, dtype=jnp.float32) * (-math.log(10000.0) / half_width))
    angles = jnp.arange(frame_count, dtype=jnp.float32)[:, None] * frequency[None, :]
    return (jnp.cos(angles), jnp.sin(angles))

def rotate(values, cos_table, sin_table, sign):
    half_width = values.shape[1] // 2
    first_half = values[:, :half_width]
    second_half = values[:, half_width:]
    return jnp.concatenate([first_half * cos_table - sign * second_half * sin_table, sign * first_half * sin_table + second_half * cos_table], axis=1)

def block_length(frame_count):
    return min(512, frame_count)

def depthwise(values, kernel, segments):
    frame_count = values.shape[0]
    reach = (KER - 1) // 2
    padded = jnp.pad(values, ((reach, reach), (0, 0)))
    seg_pad = jnp.pad(segments, (reach, reach), constant_values=-1)
    summed = jnp.zeros_like(values)
    for shift in range(KER):
        same_part = (seg_pad[shift:shift + frame_count] == segments).astype(values.dtype)[:, None]
        summed = summed + kernel[shift][None, :] * same_part * padded[shift:shift + frame_count]
    return summed

def macaron(values, gain_vector, weight_in, weight_out):
    normed = low(layer_norm(values, gain_vector))
    pre_act = low_back(matmul(normed, weight_in))
    hidden = low(jax.nn.silu(pre_act))
    return low_back(matmul(hidden, weight_out))

def attention(values, gain_vector, head_projection, output_projection, segments):
    frame_count = values.shape[0]
    scaling = 1.0 / math.sqrt(HD)
    normed = low(layer_norm(values, gain_vector))
    projected = low(low_back(matmul(normed, head_projection)))
    per_head = projected.reshape(frame_count, HEADS, 3 * HD).transpose(1, 0, 2)
    cos_table, sin_table = rotary_tables(frame_count, HD)
    block_rows = block_length(frame_count)

    def one_head(piece):
        queries = low(rotate(piece[:, :HD], cos_table, sin_table, 1.0))
        key_rows = low(rotate(piece[:, HD:2 * HD], cos_table, sin_table, 1.0))
        value_rows = piece[:, 2 * HD:]

        def one_block(element):
            query_rows, segment_rows = element
            raw_scores = low_back(scaling * matmul(query_rows, key_rows.T))
            scores = jnp.where(segment_rows[:, None] == segments[None, :], raw_scores, -1e+30)
            row_peak = lax.optimization_barrier(jnp.max(scores, axis=1, keepdims=True))
            weights = jnp.exp(scores - row_peak)
            probability = weights / lax.optimization_barrier(jnp.sum(weights, axis=1, keepdims=True))
            return matmul(low(probability), value_rows)
        blocks = lax.map(jax.checkpoint(one_block), (queries.reshape(-1, block_rows, HD), segments.reshape(-1, block_rows)))
        return blocks.reshape(frame_count, HD)
    attended = low(low_back(jax.vmap(one_head)(per_head)))
    attended = attended.transpose(1, 0, 2).reshape(frame_count, HEADS * HD)
    return matmul(attended, output_projection)

def gated_mlp(values, gain_vector, up_weight, gain_gate, kernel_gate, down_weight, segments):
    normed = low(layer_norm(values, gain_vector))
    lifted = low_back(matmul(normed, up_weight))
    hidden = exact_gelu(lifted)
    half_width = hidden.shape[1] // 2
    gate_in = low(layer_norm(hidden[:, half_width:], gain_gate))
    gate_values = low_back(depthwise(gate_in, kernel_gate, segments))
    gated_low = low(hidden[:, :half_width] * gate_values)
    return matmul(gated_low, down_weight)

def forward(values, weights, segments):
    gain_first, first_in, first_out, gain_attend, head_projection, output_projection, gain_gated, gated_up, gain_gate, kernel_gate, gated_down, kernel_merge, merge_weight, gain_second, second_in, second_out, gain_final = weights
    first_mid = values + 0.5 * macaron(values, gain_first, first_in, first_out)
    branch_global = attention(first_mid, gain_attend, head_projection, output_projection, segments)
    branch_local = gated_mlp(first_mid, gain_gated, gated_up, gain_gate, kernel_gate, gated_down, segments)
    joined = low(jnp.concatenate([low_back(branch_global), low_back(branch_local)], axis=1))
    mixed = low(low_back(joined + depthwise(joined, kernel_merge, segments)))
    second_mid = first_mid + low_back(matmul(mixed, merge_weight))
    third_mid = second_mid + 0.5 * macaron(second_mid, gain_second, second_in, second_out)
    return layer_norm(third_mid, gain_final)

def reference(frames, cotangent, lengths, gain_first, first_in, first_out, gain_attend, head_projection, output_projection, gain_gated, gated_up, gain_gate, kernel_gate, gated_down, kernel_merge, merge_weight, gain_second, second_in, second_out, gain_final):
    weights = tuple((item.astype(jnp.float32) for item in (gain_first, first_in, first_out, gain_attend, head_projection, output_projection, gain_gated, gated_up, gain_gate, kernel_gate, gated_down, kernel_merge, merge_weight, gain_second, second_in, second_out, gain_final)))
    stream_len = frames.shape[2]
    stream_rows = frames.reshape(-1, stream_len, D)
    stream_grads = cotangent.reshape(-1, stream_len, D)
    stream_lengths = lengths.reshape(-1, lengths.shape[2])
    positions = jnp.arange(stream_len, dtype=jnp.int32)

    def stream_step(summed, element):
        rows_in, rows_grad, lengths_row = element
        segments = segment_index(positions, lengths_row)

        def stream_forward(values, params):
            return forward(values, params, segments)
        result, pullback = jax.vjp(stream_forward, rows_in.astype(jnp.float32), weights)
        grad_rows, grad_weights = pullback(rows_grad.astype(jnp.float32))
        summed = jax.tree.map(jnp.add, summed, grad_weights)
        return (summed, (result.astype(jnp.bfloat16), grad_rows))
    zero_grads = jax.tree.map(jnp.zeros_like, weights)
    summed, (outputs, grad_rows) = lax.scan(stream_step, zero_grads, (stream_rows, stream_grads, stream_lengths))
    return (outputs.reshape(frames.shape), grad_rows.reshape(frames.shape), summed[0], summed[1], summed[2], summed[3], summed[4], summed[5], summed[6], summed[7], summed[8], summed[9], summed[10], summed[11], summed[12], summed[13], summed[14], summed[15], summed[16])
```

```python
import math

import jax
import jax.numpy as jnp
import numpy as np
from jax import lax
from jax.experimental import pallas as pl
from jax.experimental.pallas import tpu as pltpu
from jax.sharding import PartitionSpec as P

D = 512
HD = 64
KER = 31
GAP = 15
PAD = 16
EPSILON = 1e-05
AXES = ("head", "seq")
GROUP = 32
f32 = jnp.float32
bf16 = jnp.bfloat16

ROWS = (
    ("first_in", 64, 4),
    ("first_out", 64, 1),
    ("second_in", 64, 4),
    ("second_out", 64, 1),
    ("merge_weight", 32, 1),
    ("gated_down", 48, 1),
    ("head_projection", 48, 3),
    ("gated_up", 96, 6),
    ("output_projection", 16, 1),
    ("tiny", 16, 1),
)
OFFSET = {}
for _name, _rows, _blocks in ROWS:
    OFFSET[_name] = sum(r for n, r, b in ROWS[: len(OFFSET)])
SIZE = {n: r for n, r, b in ROWS}
BLOCKS = {n: b for n, r, b in ROWS}
TOTAL = sum(SIZE.values())

ORDER = (
    "gain_first",
    "first_in",
    "first_out",
    "gain_attend",
    "head_projection",
    "output_projection",
    "gain_gated",
    "gated_up",
    "gain_gate",
    "kernel_gate",
    "gated_down",
    "kernel_merge",
    "merge_weight",
    "gain_second",
    "second_in",
    "second_out",
    "gain_final",
)
GAINS = ("gain_first", "gain_attend", "gain_gated", "gain_second", "gain_final", "gain_gate")
KERNELS = ("kernel_gate", "kernel_merge")


def mm(a, b):
    return jnp.dot(a, b, preferred_element_type=f32)


def mt(a, b):
    return lax.dot_general(a, b, (((1,), (1,)), ((), ())), preferred_element_type=f32)


def tm(a, b):
    return lax.dot_general(a, b, (((0,), (0,)), ((), ())), preferred_element_type=f32)


def norm(v):
    centre = v - jnp.mean(v, axis=-1, keepdims=True)
    scaling = lax.rsqrt(jnp.mean(centre * centre, axis=-1, keepdims=True) + EPSILON)
    return centre * scaling, scaling


def norm_back(vh, scaling, gain, dz):
    t = dz * gain
    dv = scaling * (
        t - jnp.mean(t, axis=-1, keepdims=True) - vh * jnp.mean(t * vh, axis=-1, keepdims=True)
    )
    return dv, jnp.sum(dz * vh, axis=0, keepdims=True)


def sigmoid(v):
    return 0.5 * jnp.tanh(0.5 * v) + 0.5


def call(kernel, name, out_shape, in_specs, out_specs, scratch=(), grid=(1,), us=10, aliases=None):
    return pl.pallas_call(
        kernel,
        name=name,
        out_shape=out_shape,
        grid=grid,
        in_specs=in_specs,
        out_specs=out_specs,
        scratch_shapes=list(scratch),
        input_output_aliases=aliases or {},
        compiler_params=pltpu.CompilerParams(
            vmem_limit_bytes=60 << 20, dimension_semantics=("arbitrary",) * len(grid)
        ),
        cost_estimate=pl.CostEstimate(
            flops=int(us * 5e8), bytes_accessed=int(us * 2.5e6), transcendentals=0
        ),
    )


def whole(shape):
    zeros = (0,) * len(shape)
    return pl.BlockSpec(shape, lambda *_: zeros)


SMEM = pl.BlockSpec(memory_space=pltpu.SMEM)


def columns_spec(name, pick):
    base = OFFSET[name] // 16
    return pl.BlockSpec((GROUP, 16, D), lambda j: (0, base + pick(j), 0))


def rows_spec(name, pick):
    rows = SIZE[name]
    base = OFFSET[name] // rows
    return pl.BlockSpec((D // rows, rows, D), lambda j: (pick(j), base, 0))


def whole_spec(name):
    rows = SIZE[name]
    base = OFFSET[name] // rows
    return pl.BlockSpec((GROUP, rows, D), lambda *_: (0, base, 0))


def sds(shape, dtype):
    return jax.ShapeDtypeStruct(shape, dtype)


def segments_of(meta, m, count, frames):
    base = meta[meta.shape[0] - 1]
    low, high, offset = [], [], []
    start = jnp.int32(0)
    rank = jnp.int32(0)
    before = jnp.int32(0)
    after = jnp.int32(0)
    for s in range(count):
        end = start + meta[m * count + s]
        lo = jnp.clip(start - base, 0, frames)
        hi = jnp.clip(end - base, 0, frames)
        low.append(lo)
        high.append(hi)
        offset.append(PAD + GAP * rank)
        rank = rank + (hi > lo).astype(jnp.int32)
        first = (start <= base) & (base < end)
        before = jnp.where(first, jnp.minimum(base - start, GAP), before)
        final = base + frames - 1
        last = (start <= final) & (final < end)
        after = jnp.where(last, jnp.minimum(end - final - 1, GAP), after)
        start = end
    return low, high, offset, before, after, frames + GAP * (rank - 1)


def clear(buf):
    def body(i, c):
        buf[pl.ds(pl.multiple_of(i * 64, 64), 64), :] = jnp.zeros((64, 128), f32)
        return c

    lax.fori_loop(0, buf.shape[0] // 64, body, 0)


def stage(seg, src, row0, frames, before, after, dst, blocks, sub0):
    low, high, offset, nb, na, length = seg
    for s in range(len(low)):
        lo, hi, off = low[s], high[s], offset[s]

        @pl.when(hi > lo)
        def _():
            def body(g, c):
                r = pl.multiple_of(g * 16, 16)
                for i, cb in enumerate(blocks):
                    x = src[pl.ds(row0 + r, 16), cb * 128 : (cb + 1) * 128].astype(f32)
                    dst[pl.ds((r + off) * 8 + sub0 + i, 16, stride=8), :] = x
                return c

            lax.fori_loop(lo // 16, (hi + 15) // 16, body, 0)

    n = len(blocks)
    for s in range(len(low) - 1):
        lo, hi, off = low[s], high[s], offset[s]

        @pl.when((hi > lo) & (hi < frames))
        def _():
            def body(i, c):
                q = (hi + off + i) * 8
                if n == 8:
                    dst[pl.ds(pl.multiple_of(q, 8), 8), :] = jnp.zeros((8, 128), f32)
                else:
                    dst[pl.ds(q + sub0, n), :] = jnp.zeros((n, 128), f32)
                return c

            lax.fori_loop(0, GAP, body, 0)

    if before is None:
        xb = jnp.zeros((16, 128), f32)
        for i, cb in enumerate(blocks):
            dst[pl.ds(sub0 + i, 16, stride=8), :] = xb
            dst[pl.ds((PAD + length) * 8 + sub0 + i, 16, stride=8), :] = xb
    else:
        rows = lax.broadcasted_iota(jnp.int32, (16, 128), 0)
        kb = rows >= 16 - nb
        ka = rows < na
        for i, cb in enumerate(blocks):
            xb = jnp.where(kb, before[:, cb * 128 : (cb + 1) * 128].astype(f32), 0.0)
            xa = jnp.where(ka, after[:, cb * 128 : (cb + 1) * 128].astype(f32), 0.0)
            dst[pl.ds(sub0 + i, 16, stride=8), :] = xb
            dst[pl.ds((PAD + length) * 8 + sub0 + i, 16, stride=8), :] = xa


def unstage(seg, src, dst, row0, blocks, sub0):
    low, high, offset = seg[:3]
    rows = lax.broadcasted_iota(jnp.int32, (16, 128), 0)
    for s in range(len(low)):
        lo, hi, off = low[s], high[s], offset[s]

        @pl.when(hi > lo)
        def _():
            def body(g, c):
                r = pl.multiple_of(g * 16, 16)
                keep = rows >= lo - r
                for i, cb in enumerate(blocks):
                    value = src[pl.ds((r + off) * 8 + sub0 + i, 16, stride=8), :]
                    at = (pl.ds(row0 + r, 16), slice(cb * 128, (cb + 1) * 128))
                    dst[at] = jnp.where(keep, value, dst[at])
                return c

            lax.fori_loop(lo // 16, (hi + 15) // 16, body, 0)


def convolve(length, taps, buf, out, flip):
    w = [taps[30 - k if flip else k] for k in range(KER)]

    def body(b, c):
        p0 = PAD + b * 8
        acc = [None] * 8
        for j in range(38):
            v = buf[pl.ds(pl.multiple_of((p0 - 15 + j) * 8, 8), 8), :]
            for o in range(8):
                k = j - o
                if 0 <= k < KER:
                    t = w[k] * v
                    acc[o] = t if acc[o] is None else acc[o] + t
        for o in range(8):
            out[pl.ds(pl.multiple_of((p0 + o) * 8, 8), 8), :] = acc[o]
        return c

    lax.fori_loop(0, (length + 7) // 8, body, 0)


def tap_sums(length, vbuf, gbuf):
    def body(b, acc):
        acc = list(acc)
        p0 = PAD + b * 8
        v = [vbuf[pl.ds(pl.multiple_of((p0 + o) * 8, 8), 8), :] for o in range(8)]
        for j in range(38):
            g = gbuf[pl.ds(pl.multiple_of((p0 - 15 + j) * 8, 8), 8), :]
            for o in range(8):
                k = o - j + 30
                if 0 <= k < KER:
                    acc[k] = acc[k] + v[o] * g
        return tuple(acc)

    zero = tuple(jnp.zeros((8, 128), f32) for _ in range(KER))
    return lax.fori_loop(0, (length + 7) // 8, body, zero)


def channel_groups(channels, micro):
    out = []
    for g in range(channels // 1024):
        for m in range(micro):
            out.append((g, tuple(range(8 * g, 8 * g + 8)), ((m, 0),)))
    if channels % 1024:
        blocks = tuple(range(channels // 1024 * 8, channels // 128))
        for m in range(0, micro, 2):
            out.append((channels // 1024, blocks, ((m, 0), (m + 1, 4))))
    return out


def gapped_rows(frames, count):
    return -(-(frames + GAP * (count - 1) + 2 * PAD + 16) // 8) * 8


def tap_layout(kernel):
    channels = kernel.shape[1]
    out = []
    for g in range(channels // 1024):
        out.append(kernel[:, g * 1024 : (g + 1) * 1024].reshape(KER, 8, 128))
    if channels % 1024:
        half = kernel[:, channels // 1024 * 1024 :].reshape(KER, 4, 128)
        out.append(jnp.concatenate([half, half], axis=1))
    return jnp.stack(out).astype(f32)


def tap_unlayout(taps, channels):
    out = [taps[g].reshape(KER, 1024) for g in range(channels // 1024)]
    if channels % 1024:
        out.append((taps[-1][:, :4] + taps[-1][:, 4:]).reshape(KER, 512))
    return jnp.concatenate(out, axis=1)


def put_edges(value, micro, frames, first_ref, last_ref):
    for m in range(micro):
        first_ref[m] = value[m * frames : m * frames + 16]
        last_ref[m] = value[(m + 1) * frames - 16 : (m + 1) * frames]


def first_kernel(nh, x_ref, gain_ref, win_ref, wout_ref, hp_ref, mid_ref, qkv_ref, n_ref, acc_ref, q_ref):
    j = pl.program_id(0)

    @pl.when(j == 0)
    def _():
        vh, _ = norm(x_ref[...].astype(f32))
        n_ref[...] = (vh * gain_ref[0:1, :]).astype(bf16)
        acc_ref[...] = jnp.zeros_like(acc_ref)

    p = mm(n_ref[...], win_ref[...].reshape(D, D))
    h = (p * sigmoid(p)).astype(bf16)
    acc_ref[...] += mm(h, wout_ref[...].reshape(D, D))

    @pl.when(j == pl.num_programs(0) - 1)
    def _():
        mid = x_ref[...].astype(f32) + 0.5 * acc_ref[...]
        mid_ref[...] = mid
        vh, _ = norm(mid)
        n = (vh * gain_ref[1:2, :]).astype(bf16)
        for b in range(3):
            part = hp_ref[:, 16 * b : 16 * b + 16, :].reshape(D, D)
            q_ref[:, D * b : D * b + D] = mm(n, part).astype(bf16)
        width = 3 * D // nh
        for i in range(nh):
            qkv_ref[i] = q_ref[:, width * i : width * i + width]


def up_kernel(
    micro, frames, mid_ref, gain_ref, ggate_ref, gu_ref,
    zl_ref, gp_ref, gn_ref, rs_ref, fe_ref, le_ref, n_ref, zr_ref,
):
    j = pl.program_id(0)

    @pl.when(j == 0)
    def _():
        vh, _ = norm(mid_ref[...])
        n_ref[...] = (vh * gain_ref[2:3, :]).astype(bf16)

    up = mm(n_ref[...], gu_ref[...].reshape(D, D))
    phi = 0.5 + 0.5 * lax.erf(up * (1.0 / math.sqrt(2.0)))
    z = up * phi
    slope = phi + up * (jnp.exp(-0.5 * up * up) * (1.0 / math.sqrt(2.0 * math.pi)))
    gp_ref[...] = slope.astype(bf16)

    @pl.when(j < 3)
    def _():
        zl_ref[...] = z.astype(bf16)

    @pl.when(j >= 3)
    def _():
        zr_ref[:, pl.ds(pl.multiple_of((j - 3) * D, D), D)] = z

    @pl.when(j == 5)
    def _():
        vh, r = norm(zr_ref[...])
        gn = (vh * ggate_ref[...]).astype(bf16)
        gn_ref[...] = gn
        rs_ref[...] = jnp.broadcast_to(r, rs_ref.shape)
        put_edges(gn, micro, frames, fe_ref, le_ref)


def swap_halves(v):
    half = v.shape[1] // 2
    return jnp.concatenate([v[:, half:], v[:, :half]], axis=1)


def segment_ids(meta, m, count, shape, axis, start):
    pos = lax.broadcasted_iota(jnp.int32, shape, axis) + start
    ids = jnp.zeros(shape, jnp.int32)
    end = jnp.int32(0)
    for s in range(count - 1):
        end = end + meta[m * count + s]
        ids = ids + (pos >= end).astype(jnp.int32)
    return ids


SCALE = 1.0 / math.sqrt(HD)


def attend_kernel(lh, count, meta, qkv_ref, cos_ref, sin_ref, o_ref, l_ref, q_s, k_s, v_s):
    nh, _, frames, width = qkv_ref.shape
    stream = nh * frames
    m = pl.program_id(0)
    x = qkv_ref[...].reshape(stream, width)
    cos, sin = cos_ref[...], sin_ref[...]
    for h in range(lh):
        c0 = h * 3 * HD
        q = x[:, c0 : c0 + HD].astype(f32)
        k = x[:, c0 + HD : c0 + 2 * HD].astype(f32)
        q_s[h] = (q * cos + swap_halves(q) * sin).astype(bf16)
        k_s[h] = (k * cos + swap_halves(k) * sin).astype(bf16)
        v_s[h] = x[:, c0 + 2 * HD : c0 + 3 * HD]
    key_seg = segment_ids(meta, m, count, (1, stream), 1, 0)

    def body(i, c):
        at = pl.multiple_of(i * frames, frames)
        row_seg = segment_ids(meta, m, count, (frames, 1), 0, at)
        same = row_seg == key_seg
        lane = lax.broadcasted_iota(jnp.int32, (frames, 128), 1)
        pieces = []
        logs = jnp.zeros((frames, 128), f32)
        for h in range(lh):
            s = mt(q_s[h, pl.ds(at, frames), :], k_s[h])
            s = jnp.where(same, s, -1e30)
            peak = jnp.max(s, axis=1, keepdims=True)
            p = jnp.exp((s - peak) * SCALE)
            total = jnp.sum(p, axis=1, keepdims=True)
            o = mm(p.astype(bf16), v_s[h]) / total
            pieces.append(o)
            logs = jnp.where(lane == h, peak * SCALE + jnp.log(total), logs)
        o_ref[i, 0] = jnp.concatenate(pieces, axis=1).astype(bf16) if lh > 1 else pieces[0].astype(bf16)
        l_ref[0, pl.ds(at, frames), :] = logs
        return c

    lax.fori_loop(0, nh, body, 0)


def attend_back_kernel(
    lh, count, meta, qkv_ref, cos_ref, sin_ref, o_ref, l_ref, do_ref, d_ref,
    q_s, k_s, v_s, do_s, qt_s, dot_s, dq_s, dk_s, dv_s,
):
    nh, _, frames, width = qkv_ref.shape
    stream = nh * frames
    m = pl.program_id(0)
    x = qkv_ref[...].reshape(stream, width)
    do = do_ref[...].reshape(stream, lh * HD)
    cos, sin = cos_ref[...], sin_ref[...]
    for h in range(lh):
        c0 = h * 3 * HD
        q = x[:, c0 : c0 + HD].astype(f32)
        k = x[:, c0 + HD : c0 + 2 * HD].astype(f32)
        q = q * cos + swap_halves(q) * sin
        q_s[h] = q.astype(bf16)
        qt_s[h] = q.T.astype(bf16)
        k_s[h] = (k * cos + swap_halves(k) * sin).astype(bf16)
        v_s[h] = x[:, c0 + 2 * HD : c0 + 3 * HD]
        piece = do[:, h * HD : (h + 1) * HD]
        do_s[h] = piece
        dot_s[h] = piece.astype(f32).T.astype(bf16)
    dk_s[...] = jnp.zeros_like(dk_s)
    dv_s[...] = jnp.zeros_like(dv_s)
    key_seg = segment_ids(meta, m, count, (1, stream), 1, 0)

    def body(i, c):
        at = pl.multiple_of(i * frames, frames)
        row_seg = segment_ids(meta, m, count, (frames, 1), 0, at)
        same = row_seg == key_seg
        lane = lax.broadcasted_iota(jnp.int32, (frames, 128), 1)
        logs = l_ref[0, pl.ds(at, frames), :]
        o = o_ref[i, 0].astype(f32)
        for h in range(lh):
            log = jnp.sum(jnp.where(lane == h, logs, 0.0), axis=1, keepdims=True)
            dh = do_s[h, pl.ds(at, frames), :]
            delta = jnp.sum(o[:, h * HD : (h + 1) * HD] * dh.astype(f32), axis=1, keepdims=True)
            s = mt(q_s[h, pl.ds(at, frames), :], k_s[h])
            p = jnp.where(same, jnp.exp(s * SCALE - log), 0.0)
            dp = mt(dh, v_s[h])
            dr = (p * (dp - delta)).astype(bf16)
            dq_s[h, pl.ds(at, frames), :] = mm(dr, k_s[h]) * SCALE
            dk_s[h] += mm(qt_s[h, :, pl.ds(at, frames)], dr)
            dv_s[h] += mm(dot_s[h, :, pl.ds(at, frames)], p.astype(bf16))
        return c

    lax.fori_loop(0, nh, body, 0)
    pieces = []
    for h in range(lh):
        dq = dq_s[h]
        dk = dk_s[h].T * SCALE
        pieces.append(dq * cos - swap_halves(dq) * sin)
        pieces.append(dk * cos - swap_halves(dk) * sin)
        pieces.append(dv_s[h].T)
    full = jnp.concatenate(pieces, axis=1).astype(bf16)
    for i in range(nh):
        d_ref[i, 0] = full[i * frames : (i + 1) * frames]


def gate_kernel(micro, frames, count, meta, gn_ref, hb_ref, ha_ref, zl_ref, wk_ref, gd_ref, gate_ref, c_ref, buf, res, out):
    segs = [segments_of(meta, m, count, frames) for m in range(micro)]
    clear(buf)
    for g, blocks, members in channel_groups(gn_ref.shape[1], micro):
        length = segs[members[0][0]][5]
        for m, sub in members:
            stage(segs[m], gn_ref, m * frames, frames, hb_ref.at[m], ha_ref.at[m], buf, blocks, sub)
            length = jnp.maximum(length, segs[m][5])
        convolve(length, wk_ref.at[g], buf, res, False)
        for m, sub in members:
            unstage(segs[m], res, out, m * frames, blocks, sub)
    gd = gd_ref[...].reshape(gn_ref.shape[1], D)
    for m in range(micro):
        at = slice(m * frames, (m + 1) * frames)
        gate = out[at, :]
        gate_ref[at, :] = gate.astype(bf16)
        u = (zl_ref[at, :].astype(f32) * gate).astype(bf16)
        c_ref[at, :] = mm(u, gd).astype(bf16)


def join_kernel(micro, frames, o_ref, c_ref, op_ref, jn_ref, fe_ref, le_ref):
    nh = o_ref.shape[0]
    o = jnp.concatenate([o_ref[i] for i in range(nh)], axis=1)
    a = mm(o, op_ref[...].reshape(D, D)).astype(bf16)
    jn_ref[:, :D] = a
    jn_ref[:, D:] = c_ref[...]
    for m in range(micro):
        first = slice(m * frames, m * frames + 16)
        last = slice((m + 1) * frames - 16, (m + 1) * frames)
        fe_ref[m, :, :D] = a[first]
        fe_ref[m, :, D:] = c_ref[first, :]
        le_ref[m, :, :D] = a[last]
        le_ref[m, :, D:] = c_ref[last, :]


def merge_kernel(micro, frames, count, meta, jn_ref, hb_ref, ha_ref, wk_ref, mw_ref, mid_ref, m_ref, mid2_ref, buf, res, out):
    segs = [segments_of(meta, m, count, frames) for m in range(micro)]
    clear(buf)
    for g, blocks, members in channel_groups(jn_ref.shape[1], micro):
        m = members[0][0]
        stage(segs[m], jn_ref, m * frames, frames, hb_ref.at[m], ha_ref.at[m], buf, blocks, 0)
        convolve(segs[m][5], wk_ref.at[g], buf, res, False)
        unstage(segs[m], res, out, m * frames, blocks, 0)
    mw = mw_ref[...].reshape(2 * D, D)
    for m in range(micro):
        at = slice(m * frames, (m + 1) * frames)
        mixed = (jn_ref[at, :].astype(f32) + out[at, :]).astype(bf16)
        m_ref[at, :] = mixed
        mid2_ref[at, :] = mid_ref[at, :] + mm(mixed, mw)


def silu_back(p, dh):
    s = sigmoid(p)
    return (p * s).astype(bf16), (s * (1.0 + p * (1.0 - s)) * dh).astype(bf16)


def second_kernel(
    micro, frames, mid2_ref, cot_ref, gain_ref, win_ref, wout_ref, mw_ref,
    out_ref, dmid2_ref, dm_ref, dmg_ref, fe_ref, le_ref, dwin_ref, dwout_ref, dgain_ref,
    n_ref, nt_ref, p_ref, acc_ref, dmid3_ref, df_ref,
):
    j = pl.program_id(0)
    nb = pl.num_programs(0) // 2

    @pl.when(j == 0)
    def _():
        vh, _ = norm(mid2_ref[...])
        n = vh * gain_ref[3:4, :]
        n_ref[...] = n.astype(bf16)
        nt_ref[...] = n.T.astype(bf16)
        acc_ref[...] = jnp.zeros_like(acc_ref)

    @pl.when(j < nb)
    def _():
        p = mm(n_ref[...], win_ref[...].reshape(D, D))
        p_ref[j] = p
        h = (p * sigmoid(p)).astype(bf16)
        acc_ref[...] += mm(h, wout_ref[...].reshape(D, D))

    @pl.when(j == nb - 1)
    def _():
        mid3 = mid2_ref[...] + 0.5 * acc_ref[...]
        vh, r = norm(mid3)
        gain = gain_ref[4:5, :]
        out_ref[...] = (vh * gain).astype(bf16)
        dmid3, dgain = norm_back(vh, r, gain, cot_ref[...].astype(f32))
        dgain_ref[1:2, :] = dgain
        dmid3_ref[...] = dmid3
        df_ref[...] = (0.5 * dmid3).astype(bf16)
        acc_ref[...] = jnp.zeros_like(acc_ref)

    @pl.when(j >= nb)
    def _():
        win = win_ref[...].reshape(D, D)
        dh = mt(df_ref[...], wout_ref[...].reshape(D, D))
        h, dp = silu_back(p_ref[2 * nb - 1 - j], dh)
        dwout_ref[...] = tm(h, df_ref[...]).astype(bf16).reshape(dwout_ref.shape)
        dwin_ref[...] = mm(nt_ref[...], dp).astype(bf16).reshape(dwin_ref.shape)
        acc_ref[...] += mt(dp, win)

    @pl.when(j == 2 * nb - 1)
    def _():
        vh, r = norm(mid2_ref[...])
        dv, dgain = norm_back(vh, r, gain_ref[3:4, :], acc_ref[...])
        dgain_ref[0:1, :] = dgain
        dmid2 = dmid3_ref[...] + dv
        dmid2_ref[...] = dmid2
        dmg = dmid2.astype(bf16)
        dmg_ref[...] = dmg
        dm = mt(dmg, mw_ref[...].reshape(2 * D, D)).astype(bf16)
        dm_ref[...] = dm
        put_edges(dm, micro, frames, fe_ref, le_ref)


def outer_kernel(a_ref, b_ref, o_ref):
    o_ref[...] = tm(a_ref[...], b_ref[...]).astype(bf16)


def merge_back_kernel(
    micro, frames, count, meta, dm_ref, hb_ref, ha_ref, jn_ref, wk_ref, op_ref,
    da_ref, dc_ref, do_ref, dk_ref, buf, vbuf, res, out,
):
    segs = [segments_of(meta, m, count, frames) for m in range(micro)]
    clear(buf)
    clear(vbuf)
    total = [None] * KER
    for g, blocks, members in channel_groups(dm_ref.shape[1], micro):
        m = members[0][0]
        stage(segs[m], dm_ref, m * frames, frames, hb_ref.at[m], ha_ref.at[m], buf, blocks, 0)
        stage(segs[m], jn_ref, m * frames, frames, None, None, vbuf, blocks, 0)
        convolve(segs[m][5], wk_ref.at[g], buf, res, True)
        sums = tap_sums(segs[m][5], vbuf, buf)
        for k in range(KER):
            dk_ref[g, k] = sums[k] if m == 0 else dk_ref[g, k] + sums[k]
        unstage(segs[m], res, out, m * frames, blocks, 0)
    nh = do_ref.shape[0]
    width = D // nh
    for m in range(micro):
        at = slice(m * frames, (m + 1) * frames)
        djn = dm_ref[at, :].astype(f32) + out[at, :]
        da = djn[:, :D].astype(bf16)
        da_ref[at, :] = da
        dc_ref[at, :] = djn[:, D:].astype(bf16)
        do = mt(da, op_ref[...].reshape(D, D)).astype(bf16)
        for i in range(nh):
            do_ref[i, at, :] = do[:, i * width : (i + 1) * width]


def gate_pre_kernel(
    micro, frames, dc_ref, da_ref, o_ref, zl_ref, gate_ref, gp_ref, gd_ref,
    dgd_ref, dop_ref, dup_ref, dgate_ref, fe_ref, le_ref, gd_s,
):
    j = pl.program_id(0)

    @pl.when(j == 0)
    def _():
        gd_s[...] = gd_ref[...].reshape(gd_s.shape)
        width = o_ref.shape[2]
        for i in range(o_ref.shape[0]):
            dop_ref[i * width : (i + 1) * width, :] = tm(o_ref[i], da_ref[...]).astype(bf16)

    du = mt(dc_ref[...], gd_s[pl.ds(pl.multiple_of(j * D, D), D), :])
    gate = gate_ref[...].astype(f32)
    left = zl_ref[...].astype(f32)
    u = (left * gate).astype(bf16)
    dgd_ref[...] = tm(u, dc_ref[...]).astype(bf16)
    dup_ref[...] = (gp_ref[...].astype(f32) * (du * gate)).astype(bf16)
    dgate = (du * left).astype(bf16)
    dgate_ref[...] = dgate
    put_edges(dgate, micro, frames, fe_ref, le_ref)


def gate_back_kernel(
    micro, frames, count, meta, dg_ref, hb_ref, ha_ref, gn_ref, rs_ref, ggate_ref, wk_ref, gp_ref,
    dup_ref, dk_ref, dgain_ref, buf, vbuf, res, out,
):
    segs = [segments_of(meta, m, count, frames) for m in range(micro)]
    clear(buf)
    clear(vbuf)
    seen = set()
    for g, blocks, members in channel_groups(dg_ref.shape[1], micro):
        length = segs[members[0][0]][5]
        if len(members) > 1:
            clear(buf)
            clear(vbuf)
        for m, sub in members:
            stage(segs[m], dg_ref, m * frames, frames, hb_ref.at[m], ha_ref.at[m], buf, blocks, sub)
            stage(segs[m], gn_ref, m * frames, frames, None, None, vbuf, blocks, sub)
            length = jnp.maximum(length, segs[m][5])
        convolve(length, wk_ref.at[g], buf, res, True)
        sums = tap_sums(length, vbuf, buf)
        for k in range(KER):
            dk_ref[g, k] = dk_ref[g, k] + sums[k] if g in seen else sums[k]
        seen.add(g)
        for m, sub in members:
            unstage(segs[m], res, out, m * frames, blocks, sub)
    gain = ggate_ref[...]
    inverse = 1.0 / gain
    for m in range(micro):
        at = slice(m * frames, (m + 1) * frames)
        vh = gn_ref[at, :].astype(f32) * inverse
        dv, dgain = norm_back(vh, rs_ref[at, 0:1], gain, out[at, :])
        dgain_ref[...] = dgain if m == 0 else dgain_ref[...] + dgain
        dup_ref[at, :] = (gp_ref[at, :].astype(f32) * dv).astype(bf16)


def up_back_kernel(mid_ref, dmid2_ref, gain_ref, dl_ref, dr_ref, gu_ref, dmid_ref, dgu_ref, dgain_ref, nt_ref, acc_ref):
    j = pl.program_id(0)

    @pl.when(j == 0)
    def _():
        vh, _ = norm(mid_ref[...])
        nt_ref[...] = (vh * gain_ref[2:3, :]).T.astype(bf16)
        acc_ref[...] = jnp.zeros_like(acc_ref)

    dup = jnp.where(j < 3, dl_ref[...], dr_ref[...])
    dgu_ref[...] = mm(nt_ref[...], dup).astype(bf16).reshape(dgu_ref.shape)
    acc_ref[...] += mt(dup, gu_ref[...].reshape(D, D))

    @pl.when(j == pl.num_programs(0) - 1)
    def _():
        vh, r = norm(mid_ref[...])
        dv, dgain = norm_back(vh, r, gain_ref[2:3, :], acc_ref[...])
        dgain_ref[...] = dgain
        dmid_ref[...] = dmid2_ref[...] + dv


def first_back_kernel(
    x_ref, mid_ref, dml_ref, dq_ref, gain_ref, hp_ref, win_ref, wout_ref,
    dx_ref, dhp_ref, dwin_ref, dwout_ref, dgain_ref,
    dq_s, n_ref, nt_ref, dmid_ref, df_ref, acc_ref,
):
    j = pl.program_id(0)

    @pl.when(j == 0)
    def _():
        nh, _, width = dq_ref.shape
        for i in range(nh):
            dq_s[:, i * width : (i + 1) * width] = dq_ref[i]
        vh, r = norm(mid_ref[...])
        gain = gain_ref[1:2, :]
        nt = (vh * gain).T.astype(bf16)
        dn = None
        for b in range(3):
            dq = dq_s[:, b * D : (b + 1) * D]
            dhp_ref[:, 16 * b : 16 * b + 16, :] = mm(nt, dq).astype(bf16).reshape(GROUP, 16, D)
            t = mt(dq, hp_ref[:, 16 * b : 16 * b + 16, :].reshape(D, D))
            dn = t if dn is None else dn + t
        dv, dgain = norm_back(vh, r, gain, dn)
        dgain_ref[1:2, :] = dgain
        dmid = dml_ref[...] + dv
        dmid_ref[...] = dmid
        df_ref[...] = (0.5 * dmid).astype(bf16)
        vh, _ = norm(x_ref[...].astype(f32))
        n = vh * gain_ref[0:1, :]
        n_ref[...] = n.astype(bf16)
        nt_ref[...] = n.T.astype(bf16)
        acc_ref[...] = jnp.zeros_like(acc_ref)

    win = win_ref[...].reshape(D, D)
    p = mm(n_ref[...], win)
    dh = mt(df_ref[...], wout_ref[...].reshape(D, D))
    h, dp = silu_back(p, dh)
    dwout_ref[...] = tm(h, df_ref[...]).astype(bf16).reshape(dwout_ref.shape)
    dwin_ref[...] = mm(nt_ref[...], dp).astype(bf16).reshape(dwin_ref.shape)
    acc_ref[...] += mt(dp, win)

    @pl.when(j == pl.num_programs(0) - 1)
    def _():
        vh, r = norm(x_ref[...].astype(f32))
        dv, dgain = norm_back(vh, r, gain_ref[0:1, :], acc_ref[...])
        dgain_ref[0:1, :] = dgain
        dx_ref[...] = dmid_ref[...] + dv


def to_rows(shard):
    rows, cols = shard.shape
    if cols == D:
        return shard
    return shard.reshape(rows, cols // D, D).transpose(1, 0, 2).reshape(rows * cols // D, D)


def canonical(part, name):
    count = part.shape[0]
    q = count // GROUP
    if q == 1:
        return part
    blocks = BLOCKS[name]
    rows = part.shape[1] // blocks
    part = part.reshape(GROUP, q, blocks, rows, D).transpose(0, 2, 1, 3, 4)
    return part.reshape(GROUP, blocks * q * rows, D)


def by_device(part, name, count):
    q = count // GROUP
    if q == 1:
        return part
    blocks = BLOCKS[name]
    rows = part.shape[1] // blocks // q
    part = part.reshape(GROUP, blocks, q, rows, D).transpose(0, 2, 1, 3, 4)
    return part.reshape(count, blocks * rows, D)


def gather_weights(shards, count):
    q = count // GROUP
    tiny = jnp.concatenate([shards[n].reshape(-1) for n in GAINS + KERNELS])
    tiny = jnp.pad(tiny, (0, SIZE["tiny"] // q * D - tiny.shape[0])).reshape(-1, D)
    packed = jnp.concatenate([to_rows(shards[n]) for n, r, b in ROWS[:-1]] + [tiny], axis=0)
    raw = lax.all_gather(packed, AXES, axis=0, tiled=False)
    if q == 1:
        full = raw
    else:
        full = jnp.concatenate(
            [canonical(raw[:, OFFSET[n] // q : (OFFSET[n] + SIZE[n]) // q], n) for n, r, b in ROWS],
            axis=1,
        )
    tiny = raw[:, OFFSET["tiny"] // q :].reshape(count, -1)
    unit = shards["gain_first"].shape[0]
    gains = tiny[:, : 5 * unit].astype(f32).reshape(count, 5, unit).transpose(1, 0, 2).reshape(5, D)
    gains = jnp.pad(gains, ((0, 3), (0, 0)))
    at = 5 * unit
    size = shards["gain_gate"].shape[0]
    gate_gain = tiny[:, at : at + size].astype(f32).reshape(1, -1)
    at += size
    kernels = []
    for n in KERNELS:
        taps, cols = shards[n].shape
        part = tiny[:, at : at + taps * cols].reshape(count, taps, cols)
        kernels.append(tap_layout(part.transpose(1, 0, 2).reshape(taps, count * cols)))
        at += taps * cols
    return full, gains, gate_gain, kernels


def scatter_pieces(pieces, count):
    q = count // GROUP
    parts = [p if n == "tiny" else by_device(p, n, count) for n, p in pieces]
    rows = sum(p.shape[1] for p in parts)
    want = -(-rows // 48) * 48
    joined = jnp.concatenate(parts, axis=1)
    if want != rows:
        joined = jnp.pad(joined, ((0, 0), (0, want - rows), (0, 0)))
    got = lax.psum_scatter(joined.reshape(-1, D), AXES, scatter_dimension=0, tiled=True)
    out = {}
    at = 0
    for (n, _), p in zip(pieces, parts):
        part = got[at : at + p.shape[1]].astype(f32)
        at += p.shape[1]
        if n != "tiny":
            blocks = BLOCKS[n]
            rows = part.shape[0] // blocks
            part = part.reshape(blocks, rows, D).transpose(1, 0, 2).reshape(rows, blocks * D)
        out[n] = part
    return out


def rope_tables(stream):
    half = HD // 2
    frequency = np.exp(np.arange(half, dtype=np.float32) * np.float32(-math.log(10000.0) / half))
    angles = np.arange(stream, dtype=np.float32)[:, None] * frequency.astype(np.float32)[None, :]
    cos, sin = np.cos(angles), np.sin(angles)
    return (
        jnp.asarray(np.concatenate([cos, cos], axis=1), f32),
        jnp.asarray(np.concatenate([-sin, sin], axis=1), f32),
    )


def on_device(frames, cotangent, lengths, *weights):
    shards = dict(zip(ORDER, weights))
    nh = lax.axis_size("head")
    devices = nh * lax.axis_size("seq")
    micro, _, F, _ = frames.shape
    T = micro * F
    lh = D // HD // nh
    W = 3 * D // nh
    O = lh * HD
    S = nh * F
    U = lengths.shape[2]
    FF = 4 * D
    CH = 3 * D
    meta = jnp.concatenate(
        [lengths.reshape(-1), (lax.axis_index("head") * F).astype(jnp.int32).reshape(1)]
    ).astype(jnp.int32)
    E, gains, gate_gain, (gate_taps, merge_taps) = gather_weights(shards, devices)
    x = frames.reshape(T, D)
    cot = cotangent.reshape(T, D)
    up = [(i, i + 1) for i in range(nh - 1)]
    down = [(i + 1, i) for i in range(nh - 1)]

    def halo(first, last):
        return lax.ppermute(last, "head", up), lax.ppermute(first, "head", down)

    def exchange(v):
        return lax.all_to_all(v, "head", split_axis=0, concat_axis=0, tiled=True)

    def bind(kernel, *args):
        def bound(*refs):
            return kernel(*args, *refs)

        return bound

    rows = lambda c, d: sds((T, c), d)
    full = lambda c: whole((T, c))
    edge = lambda c: sds((micro, 16, c), bf16)
    edge_spec = lambda c: whole((micro, 16, c))
    vm = pltpu.VMEM
    PR = gapped_rows(F, U)
    buf = vm((PR * 8, 128), f32)
    nb = FF // D
    same = lambda j: j

    mid1, qkv = call(
        bind(first_kernel, nh), "first",
        (rows(D, f32), sds((nh, T, W), bf16)),
        [full(D), whole((8, D)), columns_spec("first_in", same), rows_spec("first_out", same), whole_spec("head_projection")],
        (full(D), whole((nh, T, W))),
        [vm((T, D), bf16), vm((T, D), f32), vm((T, 3 * D), bf16)],
        grid=(nb,), us=8,
    )(x, gains, E, E, E)
    qkv_r = exchange(qkv).reshape(nh, micro, F, W)

    zl, gp, gn, rs, fe, le = call(
        bind(up_kernel, micro, F), "up",
        (rows(CH, bf16), rows(2 * CH, bf16), rows(CH, bf16), rows(128, f32), edge(CH), edge(CH)),
        [full(D), whole((8, D)), whole((1, CH)), columns_spec("gated_up", same)],
        (
            pl.BlockSpec((T, D), lambda j: (0, jnp.minimum(j, 2))),
            pl.BlockSpec((T, D), lambda j: (0, j)),
            full(CH), full(128), edge_spec(CH), edge_spec(CH),
        ),
        [vm((T, D), bf16), vm((T, CH), f32)],
        grid=(6,), us=15,
    )(mid1, gains, gate_gain, E)
    gate_b, gate_a = halo(fe, le)

    cos, sin = rope_tables(S)
    qkv_spec = pl.BlockSpec((nh, 1, F, W), lambda m: (0, m, 0, 0))
    o_spec = pl.BlockSpec((nh, 1, F, O), lambda m: (0, m, 0, 0))
    l_spec = pl.BlockSpec((1, S, 128), lambda m: (m, 0, 0))
    head_buf = vm((lh, S, HD), bf16)
    o_own, logs = call(
        bind(attend_kernel, lh, U), "attend",
        (sds((nh, micro, F, O), bf16), sds((micro, S, 128), f32)),
        [SMEM, qkv_spec, whole((S, HD)), whole((S, HD))],
        (o_spec, l_spec),
        [head_buf] * 3,
        grid=(micro,), us=12,
    )(meta, qkv_r, cos, sin)
    o_r = exchange(o_own.reshape(nh, T, O))

    gate, c = call(
        bind(gate_kernel, micro, F, U), "gate",
        (rows(CH, bf16), rows(D, bf16)),
        [SMEM, full(CH), edge_spec(CH), edge_spec(CH), full(CH), whole(gate_taps.shape), whole_spec("gated_down")],
        (full(CH), full(D)),
        [buf, buf, vm((T, CH), f32)],
        us=18,
    )(meta, gn, gate_b, gate_a, zl, gate_taps, E)

    jn, fe, le = call(
        bind(join_kernel, micro, F), "join",
        (rows(2 * D, bf16), edge(2 * D), edge(2 * D)),
        [whole((nh, T, O)), full(D), whole_spec("output_projection")],
        (full(2 * D), edge_spec(2 * D), edge_spec(2 * D)),
        us=2,
    )(o_r, c, E)
    jn_b, jn_a = halo(fe, le)

    mixed, mid2 = call(
        bind(merge_kernel, micro, F, U), "merge",
        (rows(2 * D, bf16), rows(D, f32)),
        [SMEM, full(2 * D), edge_spec(2 * D), edge_spec(2 * D), whole(merge_taps.shape), whole_spec("merge_weight"), full(D)],
        (full(2 * D), full(D)),
        [buf, buf, vm((T, 2 * D), f32)],
        us=12,
    )(meta, jn, jn_b, jn_a, merge_taps, E, mid1)

    there_back = lambda j: jnp.where(j < nb, j, 2 * nb - 1 - j)
    back = lambda j: jnp.where(j < nb, nb - 1, 2 * nb - 1 - j)
    out_rows, dmid2, dm, dmg, fe, le, d_second_in, d_second_out, dgain2 = call(
        bind(second_kernel, micro, F), "second",
        (
            rows(D, bf16), rows(D, f32), rows(2 * D, bf16), rows(D, bf16), edge(2 * D), edge(2 * D),
            sds((GROUP, 64, D), bf16), sds((GROUP, 64, D), bf16), sds((8, D), f32),
        ),
        [full(D), full(D), whole((8, D)), columns_spec("second_in", there_back), rows_spec("second_out", there_back), whole_spec("merge_weight")],
        (
            full(D), full(D), full(2 * D), full(D), edge_spec(2 * D), edge_spec(2 * D),
            pl.BlockSpec((GROUP, 16, D), lambda j: (0, back(j), 0)),
            pl.BlockSpec((D // 64, 64, D), lambda j: (back(j), 0, 0)),
            whole((8, D)),
        ),
        [vm((T, D), bf16), vm((D, T), bf16), vm((nb, T, D), f32), vm((T, D), f32), vm((T, D), f32), vm((T, D), bf16)],
        grid=(2 * nb,), us=25,
    )(mid2, cot, gains, E, E, E)
    dm_b, dm_a = halo(fe, le)

    d_merge = call(
        outer_kernel, "merge_outer", sds((2 * D, D), bf16), [full(2 * D), full(D)], whole((2 * D, D)), us=4
    )(mixed, dmg).reshape(GROUP, 32, D)

    da, dc, do, merge_sums = call(
        bind(merge_back_kernel, micro, F, U), "merge_back",
        (rows(D, bf16), rows(D, bf16), sds((nh, T, O), bf16), sds(merge_taps.shape, f32)),
        [SMEM, full(2 * D), edge_spec(2 * D), edge_spec(2 * D), full(2 * D), whole(merge_taps.shape), whole_spec("output_projection")],
        (full(D), full(D), whole((nh, T, O)), whole(merge_taps.shape)),
        [buf, buf, buf, vm((T, 2 * D), f32)],
        us=20,
    )(meta, dm, dm_b, dm_a, jn, merge_taps, E)
    do_r = exchange(do).reshape(nh, micro, F, O)

    column = pl.BlockSpec((T, D), lambda j: (0, j))
    edge_column = pl.BlockSpec((micro, 16, D), lambda j: (0, 0, j))
    d_down, d_output, dup_l, dgate, fe, le = call(
        bind(gate_pre_kernel, micro, F), "gate_pre",
        (sds((CH, D), bf16), sds((D, D), bf16), rows(CH, bf16), rows(CH, bf16), edge(CH), edge(CH)),
        [full(D), full(D), whole((nh, T, O)), column, column, column, whole_spec("gated_down")],
        (pl.BlockSpec((D, D), lambda j: (j, 0)), whole((D, D)), column, column, edge_column, edge_column),
        [vm((CH, D), bf16)],
        grid=(3,), us=8,
    )(dc, da, o_r, zl, gate, gp, E)
    dg_b, dg_a = halo(fe, le)

    dqkv = call(
        bind(attend_back_kernel, lh, U), "attend_back",
        sds((nh, micro, F, W), bf16),
        [SMEM, qkv_spec, whole((S, HD)), whole((S, HD)), o_spec, l_spec, o_spec],
        qkv_spec,
        [head_buf] * 4 + [vm((lh, HD, S), bf16)] * 2 + [vm((lh, S, HD), f32)] + [vm((lh, HD, S), f32)] * 2,
        grid=(micro,), us=25,
    )(meta, qkv_r, cos, sin, o_own, logs, do_r)
    dqkv_r = exchange(dqkv.reshape(nh, T, W))

    dup_r, gate_sums, dgain_gate = call(
        bind(gate_back_kernel, micro, F, U), "gate_back",
        (rows(CH, bf16), sds(gate_taps.shape, f32), sds((1, CH), f32)),
        [
            SMEM, full(CH), edge_spec(CH), edge_spec(CH), full(CH), full(128), whole((1, CH)), whole(gate_taps.shape),
            pl.BlockSpec((T, CH), lambda *_: (0, 1)),
        ],
        (full(CH), whole(gate_taps.shape), whole((1, CH))),
        [buf, buf, buf, vm((T, CH), f32)],
        us=30,
    )(meta, dgate, dg_b, dg_a, gn, rs, gate_gain, gate_taps, gp)

    dml, d_up, dgain3 = call(
        up_back_kernel, "up_back",
        (rows(D, f32), sds((GROUP, 96, D), bf16), sds((1, D), f32)),
        [
            full(D), full(D), whole((8, D)),
            pl.BlockSpec((T, D), lambda j: (0, jnp.minimum(j, 2))),
            pl.BlockSpec((T, D), lambda j: (0, jnp.maximum(j - 3, 0))),
            columns_spec("gated_up", same),
        ],
        (full(D), pl.BlockSpec((GROUP, 16, D), lambda j: (0, j, 0)), whole((1, D))),
        [vm((D, T), bf16), vm((T, D), f32)],
        grid=(6,), us=8,
    )(mid1, dmid2, gains, dup_l, dup_r, E)

    dx, d_head, d_first_in, d_first_out, dgain1 = call(
        first_back_kernel, "first_back",
        (
            rows(D, f32), sds((GROUP, 48, D), bf16), sds((GROUP, 64, D), bf16), sds((GROUP, 64, D), bf16),
            sds((8, D), f32),
        ),
        [
            full(D), full(D), full(D), whole((nh, T, W)), whole((8, D)),
            whole_spec("head_projection"), columns_spec("first_in", same), rows_spec("first_out", same),
        ],
        (
            full(D), whole((GROUP, 48, D)),
            pl.BlockSpec((GROUP, 16, D), lambda j: (0, j, 0)),
            pl.BlockSpec((D // 64, 64, D), lambda j: (j, 0, 0)),
            whole((8, D)),
        ),
        [vm((T, 3 * D), bf16), vm((T, D), bf16), vm((D, T), bf16), vm((T, D), f32), vm((T, D), bf16), vm((T, D), f32)],
        grid=(nb,), us=15,
    )(x, mid1, dml, dqkv_r, gains, E, E, E)

    early = scatter_pieces(
        [
            ("second_in", d_second_in), ("second_out", d_second_out), ("merge_weight", d_merge),
            ("gated_down", d_down.reshape(GROUP, 48, D)), ("output_projection", d_output.reshape(GROUP, 16, D)),
        ],
        devices,
    )
    grads = {
        "gain_first": dgain1[0],
        "gain_attend": dgain1[1],
        "gain_gated": dgain3[0],
        "gain_second": dgain2[0],
        "gain_final": dgain2[1],
        "gain_gate": dgain_gate[0],
        "kernel_gate": tap_unlayout(gate_sums, CH),
        "kernel_merge": tap_unlayout(merge_sums, 2 * D),
    }
    tiny = [grads[n].reshape(devices, -1) for n in GAINS]
    for n in KERNELS:
        cols = grads[n].shape[1] // devices
        tiny.append(grads[n].reshape(KER, devices, cols).transpose(1, 0, 2).reshape(devices, -1))
    tiny = jnp.concatenate(tiny, axis=1).astype(bf16)
    tiny_rows = SIZE["tiny"] * GROUP // devices
    tiny = jnp.pad(tiny, ((0, 0), (0, tiny_rows * D - tiny.shape[1]))).reshape(devices, tiny_rows, D)
    late = scatter_pieces(
        [
            ("gated_up", d_up), ("head_projection", d_head), ("first_in", d_first_in), ("first_out", d_first_out),
            ("tiny", tiny),
        ],
        devices,
    )
    shares = {**early, **late}
    flat = shares["tiny"].reshape(-1)
    at = 0
    for n in GAINS + KERNELS:
        size = shards[n].size
        shares[n] = flat[at : at + size].reshape(shards[n].shape)
        at += size
    return (
        out_rows.reshape(micro, 1, F, D),
        dx.reshape(micro, 1, F, D),
        *(shares[n] for n in ORDER),
    )


def solution(mesh):
    split = P(AXES)
    split_rows = P(AXES, None)
    split_columns = P(None, AXES)
    spec = {n: split if n in GAINS else split_columns if n in KERNELS else split_rows for n in ORDER}
    weight_specs = tuple(spec[n] for n in ORDER)
    frame_spec = P(None, "seq", "head", None)
    return jax.shard_map(
        on_device,
        mesh=mesh,
        in_specs=(frame_spec, frame_spec, P(None, "seq", None)) + weight_specs,
        out_specs=(frame_spec, frame_spec) + weight_specs,
        check_vma=False,
    )
```

```python
import math

import jax
import jax.numpy as jnp
import numpy as np
from jax import lax
from jax.experimental import pallas as pl
from jax.experimental.pallas import tpu as pltpu
from jax.sharding import PartitionSpec as P

D = 512
HD = 64
KER = 31
GAP = 15
PAD = 16
EPSILON = 1e-05
AXES = ("head", "seq")
GROUP = 32
f32 = jnp.float32
bf16 = jnp.bfloat16

PACKS = {
    "a": (("head_projection", 48, 3), ("first_in", 64, 4)),
    "b": (("first_out", 64, 1), ("tiny", 16, 1)),
    "rest": (("gated_up", 96, 6), ("gated_down", 48, 1), ("output_projection", 16, 1), ("merge_weight", 32, 1)),
    "last": (("second_in", 64, 4), ("second_out", 64, 1)),
}
OFFSET = {}
SIZE = {}
BLOCKS = {}
for _pack in PACKS.values():
    _at = 0
    for _name, _rows, _blocks in _pack:
        OFFSET[_name], SIZE[_name], BLOCKS[_name] = _at, _rows, _blocks
        _at += _rows

ORDER = (
    "gain_first",
    "first_in",
    "first_out",
    "gain_attend",
    "head_projection",
    "output_projection",
    "gain_gated",
    "gated_up",
    "gain_gate",
    "kernel_gate",
    "gated_down",
    "kernel_merge",
    "merge_weight",
    "gain_second",
    "second_in",
    "second_out",
    "gain_final",
)
GAINS = ("gain_first", "gain_attend", "gain_gated", "gain_second", "gain_final", "gain_gate")
KERNELS = ("kernel_gate", "kernel_merge")


def mm(a, b):
    return jnp.dot(a, b, preferred_element_type=f32)


def mt(a, b):
    return lax.dot_general(a, b, (((1,), (1,)), ((), ())), preferred_element_type=f32)


def tm(a, b):
    return lax.dot_general(a, b, (((0,), (0,)), ((), ())), preferred_element_type=f32)


def norm(v):
    centre = v - jnp.mean(v, axis=-1, keepdims=True)
    scaling = lax.rsqrt(jnp.mean(centre * centre, axis=-1, keepdims=True) + EPSILON)
    return centre * scaling, scaling


def norm_back(vh, scaling, gain, dz):
    t = dz * gain
    dv = scaling * (
        t - jnp.mean(t, axis=-1, keepdims=True) - vh * jnp.mean(t * vh, axis=-1, keepdims=True)
    )
    return dv, jnp.sum(dz * vh, axis=0, keepdims=True)


def sigmoid(v):
    return 0.5 * jnp.tanh(0.5 * v) + 0.5


def call(kernel, name, out_shape, in_specs, out_specs, scratch=(), grid=(1,), us=10, aliases=None):
    return pl.pallas_call(
        kernel,
        name=name,
        out_shape=out_shape,
        grid=grid,
        in_specs=in_specs,
        out_specs=out_specs,
        scratch_shapes=list(scratch),
        input_output_aliases=aliases or {},
        compiler_params=pltpu.CompilerParams(
            vmem_limit_bytes=60 << 20, dimension_semantics=("arbitrary",) * len(grid)
        ),
        cost_estimate=pl.CostEstimate(
            flops=int(us * 5e8), bytes_accessed=int(us * 2.5e6), transcendentals=0
        ),
    )


def whole(shape):
    zeros = (0,) * len(shape)
    return pl.BlockSpec(shape, lambda *_: zeros)


SMEM = pl.BlockSpec(memory_space=pltpu.SMEM)


def columns_spec(name, pick):
    base = OFFSET[name] // 16
    return pl.BlockSpec((GROUP, 16, D), lambda j: (0, base + pick(j), 0))


def rows_spec(name, pick):
    rows = SIZE[name]
    base = OFFSET[name] // rows
    return pl.BlockSpec((D // rows, rows, D), lambda j: (pick(j), base, 0))


def whole_spec(name):
    rows = SIZE[name]
    base = OFFSET[name] // rows
    return pl.BlockSpec((GROUP, rows, D), lambda *_: (0, base, 0))


def sds(shape, dtype):
    return jax.ShapeDtypeStruct(shape, dtype)


def segments_of(meta, m, count, frames):
    base = meta[meta.shape[0] - 1]
    low, high, offset = [], [], []
    start = jnp.int32(0)
    rank = jnp.int32(0)
    before = jnp.int32(0)
    after = jnp.int32(0)
    for s in range(count):
        end = start + meta[m * count + s]
        lo = jnp.clip(start - base, 0, frames)
        hi = jnp.clip(end - base, 0, frames)
        low.append(lo)
        high.append(hi)
        offset.append(PAD + GAP * rank)
        rank = rank + (hi > lo).astype(jnp.int32)
        first = (start <= base) & (base < end)
        before = jnp.where(first, jnp.minimum(base - start, GAP), before)
        final = base + frames - 1
        last = (start <= final) & (final < end)
        after = jnp.where(last, jnp.minimum(end - final - 1, GAP), after)
        start = end
    return low, high, offset, before, after, frames + GAP * (rank - 1)


def clear(buf):
    def body(i, c):
        buf[pl.ds(pl.multiple_of(i * 64, 64), 64), :] = jnp.zeros((64, 128), f32)
        return c

    lax.fori_loop(0, buf.shape[0] // 64, body, 0)


def stage(seg, src, row0, frames, before, after, dst, blocks, sub0):
    low, high, offset, nb, na, length = seg
    for s in range(len(low)):
        lo, hi, off = low[s], high[s], offset[s]

        @pl.when(hi > lo)
        def _():
            def body(g, c):
                r = pl.multiple_of(g * 16, 16)
                for i, cb in enumerate(blocks):
                    x = src[pl.ds(row0 + r, 16), cb * 128 : (cb + 1) * 128].astype(f32)
                    dst[pl.ds((r + off) * 8 + sub0 + i, 16, stride=8), :] = x
                return c

            lax.fori_loop(lo // 16, (hi + 15) // 16, body, 0)

    n = len(blocks)
    for s in range(len(low) - 1):
        lo, hi, off = low[s], high[s], offset[s]

        @pl.when((hi > lo) & (hi < frames))
        def _():
            def body(i, c):
                q = (hi + off + i) * 8
                if n == 8:
                    dst[pl.ds(pl.multiple_of(q, 8), 8), :] = jnp.zeros((8, 128), f32)
                else:
                    dst[pl.ds(q + sub0, n), :] = jnp.zeros((n, 128), f32)
                return c

            lax.fori_loop(0, GAP, body, 0)

    if before is None:
        xb = jnp.zeros((16, 128), f32)
        for i, cb in enumerate(blocks):
            dst[pl.ds(sub0 + i, 16, stride=8), :] = xb
            dst[pl.ds((PAD + length) * 8 + sub0 + i, 16, stride=8), :] = xb
    else:
        rows = lax.broadcasted_iota(jnp.int32, (16, 128), 0)
        kb = rows >= 16 - nb
        ka = rows < na
        for i, cb in enumerate(blocks):
            xb = jnp.where(kb, before[:, cb * 128 : (cb + 1) * 128].astype(f32), 0.0)
            xa = jnp.where(ka, after[:, cb * 128 : (cb + 1) * 128].astype(f32), 0.0)
            dst[pl.ds(sub0 + i, 16, stride=8), :] = xb
            dst[pl.ds((PAD + length) * 8 + sub0 + i, 16, stride=8), :] = xa


def unstage(seg, src, dst, row0, blocks, sub0):
    low, high, offset = seg[:3]
    rows = lax.broadcasted_iota(jnp.int32, (16, 128), 0)
    for s in range(len(low)):
        lo, hi, off = low[s], high[s], offset[s]

        @pl.when(hi > lo)
        def _():
            def body(g, c):
                r = pl.multiple_of(g * 16, 16)
                keep = rows >= lo - r
                for i, cb in enumerate(blocks):
                    value = src[pl.ds((r + off) * 8 + sub0 + i, 16, stride=8), :]
                    at = (pl.ds(row0 + r, 16), slice(cb * 128, (cb + 1) * 128))
                    dst[at] = jnp.where(keep, value, dst[at])
                return c

            lax.fori_loop(lo // 16, (hi + 15) // 16, body, 0)


def convolve(length, taps, buf, out, flip):
    w = [taps[30 - k if flip else k] for k in range(KER)]

    def body(b, c):
        p0 = PAD + b * 8
        acc = [None] * 8
        for j in range(38):
            v = buf[pl.ds(pl.multiple_of((p0 - 15 + j) * 8, 8), 8), :]
            for o in range(8):
                k = j - o
                if 0 <= k < KER:
                    t = w[k] * v
                    acc[o] = t if acc[o] is None else acc[o] + t
        for o in range(8):
            out[pl.ds(pl.multiple_of((p0 + o) * 8, 8), 8), :] = acc[o]
        return c

    lax.fori_loop(0, (length + 7) // 8, body, 0)


def tap_sums(length, vbuf, gbuf):
    def body(b, acc):
        acc = list(acc)
        p0 = PAD + b * 8
        v = [vbuf[pl.ds(pl.multiple_of((p0 + o) * 8, 8), 8), :] for o in range(8)]
        for j in range(38):
            g = gbuf[pl.ds(pl.multiple_of((p0 - 15 + j) * 8, 8), 8), :]
            for o in range(8):
                k = o - j + 30
                if 0 <= k < KER:
                    acc[k] = acc[k] + v[o] * g
        return tuple(acc)

    zero = tuple(jnp.zeros((8, 128), f32) for _ in range(KER))
    return lax.fori_loop(0, (length + 7) // 8, body, zero)


def channel_groups(channels, micro):
    out = []
    for g in range(channels // 1024):
        for m in range(micro):
            out.append((g, tuple(range(8 * g, 8 * g + 8)), ((m, 0),)))
    if channels % 1024:
        blocks = tuple(range(channels // 1024 * 8, channels // 128))
        for m in range(0, micro, 2):
            out.append((channels // 1024, blocks, ((m, 0), (m + 1, 4))))
    return out


def gapped_rows(frames, count):
    return -(-(frames + GAP * (count - 1) + 2 * PAD + 16) // 8) * 8


def tap_layout(kernel):
    channels = kernel.shape[1]
    out = []
    for g in range(channels // 1024):
        out.append(kernel[:, g * 1024 : (g + 1) * 1024].reshape(KER, 8, 128))
    if channels % 1024:
        half = kernel[:, channels // 1024 * 1024 :].reshape(KER, 4, 128)
        out.append(jnp.concatenate([half, half], axis=1))
    return jnp.stack(out).astype(f32)


def tap_unlayout(taps, channels):
    out = [taps[g].reshape(KER, 1024) for g in range(channels // 1024)]
    if channels % 1024:
        out.append((taps[-1][:, :4] + taps[-1][:, 4:]).reshape(KER, 512))
    return jnp.concatenate(out, axis=1)


def put_edges(value, micro, frames, first_ref, last_ref):
    for m in range(micro):
        first_ref[m] = value[m * frames : m * frames + 16]
        last_ref[m] = value[(m + 1) * frames - 16 : (m + 1) * frames]


def first_kernel(nh, x_ref, gain_ref, win_ref, wout_ref, hp_ref, mid_ref, qkv_ref, n_ref, acc_ref, q_ref):
    j = pl.program_id(0)

    @pl.when(j == 0)
    def _():
        vh, _ = norm(x_ref[...].astype(f32))
        n_ref[...] = (vh * gain_ref[0:1, :]).astype(bf16)
        acc_ref[...] = jnp.zeros_like(acc_ref)

    p = mm(n_ref[...], win_ref[...].reshape(D, D))
    h = (p * sigmoid(p)).astype(bf16)
    acc_ref[...] += mm(h, wout_ref[...].reshape(D, D))

    @pl.when(j == pl.num_programs(0) - 1)
    def _():
        mid = x_ref[...].astype(f32) + 0.5 * acc_ref[...]
        mid_ref[...] = mid
        vh, _ = norm(mid)
        n = (vh * gain_ref[1:2, :]).astype(bf16)
        for b in range(3):
            part = hp_ref[:, 16 * b : 16 * b + 16, :].reshape(D, D)
            q_ref[:, D * b : D * b + D] = mm(n, part).astype(bf16)
        width = 3 * D // nh
        for i in range(nh):
            qkv_ref[i] = q_ref[:, width * i : width * i + width]


def up_kernel(
    micro, frames, mid_ref, gain_ref, ggate_ref, gu_ref,
    zl_ref, gp_ref, gn_ref, rs_ref, fe_ref, le_ref, n_ref, zr_ref,
):
    j = pl.program_id(0)

    @pl.when(j == 0)
    def _():
        vh, _ = norm(mid_ref[...])
        n_ref[...] = (vh * gain_ref[2:3, :]).astype(bf16)

    up = mm(n_ref[...], gu_ref[...].reshape(D, D))
    phi = 0.5 + 0.5 * lax.erf(up * (1.0 / math.sqrt(2.0)))
    z = up * phi
    slope = phi + up * (jnp.exp(-0.5 * up * up) * (1.0 / math.sqrt(2.0 * math.pi)))
    gp_ref[...] = slope.astype(bf16)

    @pl.when(j < 3)
    def _():
        zl_ref[...] = z.astype(bf16)

    @pl.when(j >= 3)
    def _():
        zr_ref[:, pl.ds(pl.multiple_of((j - 3) * D, D), D)] = z

    @pl.when(j == 5)
    def _():
        vh, r = norm(zr_ref[...])
        gn = (vh * ggate_ref[...]).astype(bf16)
        gn_ref[...] = gn
        rs_ref[...] = jnp.broadcast_to(r, rs_ref.shape)
        put_edges(gn, micro, frames, fe_ref, le_ref)


def swap_halves(v):
    half = v.shape[1] // 2
    return jnp.concatenate([v[:, half:], v[:, :half]], axis=1)


def segment_ids(meta, m, count, shape, axis, start):
    pos = lax.broadcasted_iota(jnp.int32, shape, axis) + start
    ids = jnp.zeros(shape, jnp.int32)
    end = jnp.int32(0)
    for s in range(count - 1):
        end = end + meta[m * count + s]
        ids = ids + (pos >= end).astype(jnp.int32)
    return ids


SCALE = 1.0 / math.sqrt(HD)


def attend_kernel(lh, count, meta, qkv_ref, cos_ref, sin_ref, o_ref, l_ref, q_s, k_s, v_s):
    nh, _, frames, width = qkv_ref.shape
    stream = nh * frames
    m = pl.program_id(0)
    x = qkv_ref[...].reshape(stream, width)
    cos, sin = cos_ref[...], sin_ref[...]
    for h in range(lh):
        c0 = h * 3 * HD
        q = x[:, c0 : c0 + HD].astype(f32)
        k = x[:, c0 + HD : c0 + 2 * HD].astype(f32)
        q_s[h] = (q * cos + swap_halves(q) * sin).astype(bf16)
        k_s[h] = (k * cos + swap_halves(k) * sin).astype(bf16)
        v_s[h] = x[:, c0 + 2 * HD : c0 + 3 * HD]
    key_seg = segment_ids(meta, m, count, (1, stream), 1, 0)

    def body(i, c):
        at = pl.multiple_of(i * frames, frames)
        row_seg = segment_ids(meta, m, count, (frames, 1), 0, at)
        same = row_seg == key_seg
        lane = lax.broadcasted_iota(jnp.int32, (frames, 128), 1)
        pieces = []
        logs = jnp.zeros((frames, 128), f32)
        for h in range(lh):
            s = mt(q_s[h, pl.ds(at, frames), :], k_s[h])
            s = jnp.where(same, s, -1e30)
            peak = jnp.max(s, axis=1, keepdims=True)
            p = jnp.exp((s - peak) * SCALE)
            total = jnp.sum(p, axis=1, keepdims=True)
            o = mm(p.astype(bf16), v_s[h]) / total
            pieces.append(o)
            logs = jnp.where(lane == h, peak * SCALE + jnp.log(total), logs)
        o_ref[i, 0] = jnp.concatenate(pieces, axis=1).astype(bf16) if lh > 1 else pieces[0].astype(bf16)
        l_ref[0, pl.ds(at, frames), :] = logs
        return c

    lax.fori_loop(0, nh, body, 0)


def attend_back_kernel(
    lh, count, meta, qkv_ref, cos_ref, sin_ref, o_ref, l_ref, do_ref, d_ref,
    q_s, k_s, v_s, do_s, qt_s, dot_s, dq_s, dk_s, dv_s,
):
    nh, _, frames, width = qkv_ref.shape
    stream = nh * frames
    m = pl.program_id(0)
    x = qkv_ref[...].reshape(stream, width)
    do = do_ref[...].reshape(stream, lh * HD)
    cos, sin = cos_ref[...], sin_ref[...]
    for h in range(lh):
        c0 = h * 3 * HD
        q = x[:, c0 : c0 + HD].astype(f32)
        k = x[:, c0 + HD : c0 + 2 * HD].astype(f32)
        q = q * cos + swap_halves(q) * sin
        q_s[h] = q.astype(bf16)
        qt_s[h] = q.T.astype(bf16)
        k_s[h] = (k * cos + swap_halves(k) * sin).astype(bf16)
        v_s[h] = x[:, c0 + 2 * HD : c0 + 3 * HD]
        piece = do[:, h * HD : (h + 1) * HD]
        do_s[h] = piece
        dot_s[h] = piece.astype(f32).T.astype(bf16)
    dk_s[...] = jnp.zeros_like(dk_s)
    dv_s[...] = jnp.zeros_like(dv_s)
    key_seg = segment_ids(meta, m, count, (1, stream), 1, 0)

    def body(i, c):
        at = pl.multiple_of(i * frames, frames)
        row_seg = segment_ids(meta, m, count, (frames, 1), 0, at)
        same = row_seg == key_seg
        lane = lax.broadcasted_iota(jnp.int32, (frames, 128), 1)
        logs = l_ref[0, pl.ds(at, frames), :]
        o = o_ref[i, 0].astype(f32)
        for h in range(lh):
            log = jnp.sum(jnp.where(lane == h, logs, 0.0), axis=1, keepdims=True)
            dh = do_s[h, pl.ds(at, frames), :]
            delta = jnp.sum(o[:, h * HD : (h + 1) * HD] * dh.astype(f32), axis=1, keepdims=True)
            s = mt(q_s[h, pl.ds(at, frames), :], k_s[h])
            p = jnp.where(same, jnp.exp(s * SCALE - log), 0.0)
            dp = mt(dh, v_s[h])
            dr = (p * (dp - delta)).astype(bf16)
            dq_s[h, pl.ds(at, frames), :] = mm(dr, k_s[h]) * SCALE
            dk_s[h] += mm(qt_s[h, :, pl.ds(at, frames)], dr)
            dv_s[h] += mm(dot_s[h, :, pl.ds(at, frames)], p.astype(bf16))
        return c

    lax.fori_loop(0, nh, body, 0)
    pieces = []
    for h in range(lh):
        dq = dq_s[h]
        dk = dk_s[h].T * SCALE
        pieces.append(dq * cos - swap_halves(dq) * sin)
        pieces.append(dk * cos - swap_halves(dk) * sin)
        pieces.append(dv_s[h].T)
    full = jnp.concatenate(pieces, axis=1).astype(bf16)
    for i in range(nh):
        d_ref[i, 0] = full[i * frames : (i + 1) * frames]


def gate_kernel(micro, frames, count, meta, gn_ref, hb_ref, ha_ref, zl_ref, wk_ref, gd_ref, gate_ref, c_ref, buf, res, out):
    segs = [segments_of(meta, m, count, frames) for m in range(micro)]
    clear(buf)
    for g, blocks, members in channel_groups(gn_ref.shape[1], micro):
        length = segs[members[0][0]][5]
        for m, sub in members:
            stage(segs[m], gn_ref, m * frames, frames, hb_ref.at[m], ha_ref.at[m], buf, blocks, sub)
            length = jnp.maximum(length, segs[m][5])
        convolve(length, wk_ref.at[g], buf, res, False)
        for m, sub in members:
            unstage(segs[m], res, out, m * frames, blocks, sub)
    gd = gd_ref[...].reshape(gn_ref.shape[1], D)
    for m in range(micro):
        at = slice(m * frames, (m + 1) * frames)
        gate = out[at, :]
        gate_ref[at, :] = gate.astype(bf16)
        u = (zl_ref[at, :].astype(f32) * gate).astype(bf16)
        c_ref[at, :] = mm(u, gd).astype(bf16)


def join_kernel(micro, frames, o_ref, c_ref, op_ref, jn_ref, fe_ref, le_ref):
    nh = o_ref.shape[0]
    o = jnp.concatenate([o_ref[i] for i in range(nh)], axis=1)
    a = mm(o, op_ref[...].reshape(D, D)).astype(bf16)
    jn_ref[:, :D] = a
    jn_ref[:, D:] = c_ref[...]
    for m in range(micro):
        first = slice(m * frames, m * frames + 16)
        last = slice((m + 1) * frames - 16, (m + 1) * frames)
        fe_ref[m, :, :D] = a[first]
        fe_ref[m, :, D:] = c_ref[first, :]
        le_ref[m, :, :D] = a[last]
        le_ref[m, :, D:] = c_ref[last, :]


def merge_kernel(micro, frames, count, meta, jn_ref, hb_ref, ha_ref, wk_ref, mw_ref, mid_ref, m_ref, mid2_ref, buf, res, out):
    segs = [segments_of(meta, m, count, frames) for m in range(micro)]
    clear(buf)
    for g, blocks, members in channel_groups(jn_ref.shape[1], micro):
        m = members[0][0]
        stage(segs[m], jn_ref, m * frames, frames, hb_ref.at[m], ha_ref.at[m], buf, blocks, 0)
        convolve(segs[m][5], wk_ref.at[g], buf, res, False)
        unstage(segs[m], res, out, m * frames, blocks, 0)
    mw = mw_ref[...].reshape(2 * D, D)
    for m in range(micro):
        at = slice(m * frames, (m + 1) * frames)
        mixed = (jn_ref[at, :].astype(f32) + out[at, :]).astype(bf16)
        m_ref[at, :] = mixed
        mid2_ref[at, :] = mid_ref[at, :] + mm(mixed, mw)


def silu_back(p, dh):
    s = sigmoid(p)
    return (p * s).astype(bf16), (s * (1.0 + p * (1.0 - s)) * dh).astype(bf16)


def second_kernel(
    micro, frames, mid2_ref, cot_ref, gain_ref, win_ref, wout_ref, mw_ref, mixed_ref,
    out_ref, dmid2_ref, dm_ref, fe_ref, le_ref, dw_ref, dgain_ref,
    n_ref, nt_ref, p_ref, acc_ref, dmid3_ref, df_ref,
):
    j = pl.program_id(0)
    nb = pl.num_programs(0) // 2

    @pl.when(j == 0)
    def _():
        vh, _ = norm(mid2_ref[...])
        n = vh * gain_ref[3:4, :]
        n_ref[...] = n.astype(bf16)
        nt_ref[...] = n.T.astype(bf16)
        acc_ref[...] = jnp.zeros_like(acc_ref)

    @pl.when(j < nb)
    def _():
        p = mm(n_ref[...], win_ref[...].reshape(D, D))
        p_ref[j] = p
        h = (p * sigmoid(p)).astype(bf16)
        acc_ref[...] += mm(h, wout_ref[...].reshape(D, D))

    @pl.when(j == nb - 1)
    def _():
        mid3 = mid2_ref[...] + 0.5 * acc_ref[...]
        vh, r = norm(mid3)
        gain = gain_ref[4:5, :]
        out_ref[...] = (vh * gain).astype(bf16)
        dmid3, dgain = norm_back(vh, r, gain, cot_ref[...].astype(f32))
        dgain_ref[1:2, :] = dgain
        dmid3_ref[...] = dmid3
        df_ref[...] = (0.5 * dmid3).astype(bf16)
        acc_ref[...] = jnp.zeros_like(acc_ref)

    @pl.when(j >= nb)
    def _():
        win = win_ref[...].reshape(D, D)
        dh = mt(df_ref[...], wout_ref[...].reshape(D, D))
        h, dp = silu_back(p_ref[2 * nb - 1 - j], dh)
        at = 2 * nb - 1 - j
        few = D // 64
        dw_ref[pl.ds(at * few, few), 64:128, :] = tm(h, df_ref[...]).astype(bf16).reshape(few, 64, D)
        dw_ref[:, pl.ds(pl.multiple_of(at * 16, 16), 16), :] = mm(nt_ref[...], dp).astype(bf16).reshape(GROUP, 16, D)
        acc_ref[...] += mt(dp, win)

    @pl.when(j == 2 * nb - 1)
    def _():
        vh, r = norm(mid2_ref[...])
        dv, dgain = norm_back(vh, r, gain_ref[3:4, :], acc_ref[...])
        dgain_ref[0:1, :] = dgain
        dmid2 = dmid3_ref[...] + dv
        dmid2_ref[...] = dmid2
        dmg = dmid2.astype(bf16)
        dw_ref[:, 128:, :] = tm(mixed_ref[...], dmg).astype(bf16).reshape(GROUP, 32, D)
        dm = mt(dmg, mw_ref[...].reshape(2 * D, D)).astype(bf16)
        dm_ref[...] = dm
        put_edges(dm, micro, frames, fe_ref, le_ref)


def merge_back_kernel(
    micro, frames, count, meta, dm_ref, hb_ref, ha_ref, jn_ref, wk_ref, op_ref,
    da_ref, dc_ref, do_ref, dk_ref, buf, vbuf, res, out,
):
    segs = [segments_of(meta, m, count, frames) for m in range(micro)]
    clear(buf)
    clear(vbuf)
    total = [None] * KER
    for g, blocks, members in channel_groups(dm_ref.shape[1], micro):
        m = members[0][0]
        stage(segs[m], dm_ref, m * frames, frames, hb_ref.at[m], ha_ref.at[m], buf, blocks, 0)
        stage(segs[m], jn_ref, m * frames, frames, None, None, vbuf, blocks, 0)
        convolve(segs[m][5], wk_ref.at[g], buf, res, True)
        sums = tap_sums(segs[m][5], vbuf, buf)
        for k in range(KER):
            dk_ref[g, k] = sums[k] if m == 0 else dk_ref[g, k] + sums[k]
        unstage(segs[m], res, out, m * frames, blocks, 0)
    nh = do_ref.shape[0]
    width = D // nh
    for m in range(micro):
        at = slice(m * frames, (m + 1) * frames)
        djn = dm_ref[at, :].astype(f32) + out[at, :]
        da = djn[:, :D].astype(bf16)
        da_ref[at, :] = da
        dc_ref[at, :] = djn[:, D:].astype(bf16)
        do = mt(da, op_ref[...].reshape(D, D)).astype(bf16)
        for i in range(nh):
            do_ref[i, at, :] = do[:, i * width : (i + 1) * width]


def gate_pre_kernel(
    micro, frames, dc_ref, da_ref, o_ref, zl_ref, gate_ref, gp_ref, gd_ref,
    dw_ref, dup_ref, dgate_ref, fe_ref, le_ref, gd_s, dgd_s,
):
    j = pl.program_id(0)

    @pl.when(j == 0)
    def _():
        gd_s[...] = gd_ref[...].reshape(gd_s.shape)
        width = o_ref.shape[2]
        for i in range(o_ref.shape[0]):
            part = tm(o_ref[i], da_ref[...]).astype(bf16)
            few = width // 16
            dw_ref[i * few : (i + 1) * few, :16, :] = part.reshape(few, 16, D)

    du = mt(dc_ref[...], gd_s[pl.ds(pl.multiple_of(j * D, D), D), :])
    gate = gate_ref[...].astype(f32)
    left = zl_ref[...].astype(f32)
    u = (left * gate).astype(bf16)
    dgd_s[pl.ds(pl.multiple_of(j * D, D), D), :] = tm(u, dc_ref[...]).astype(bf16)

    @pl.when(j == pl.num_programs(0) - 1)
    def _():
        dw_ref[:, 16:, :] = dgd_s[...].reshape(GROUP, 48, D)

    dup_ref[...] = (gp_ref[...].astype(f32) * (du * gate)).astype(bf16)
    dgate = (du * left).astype(bf16)
    dgate_ref[...] = dgate
    put_edges(dgate, micro, frames, fe_ref, le_ref)


def gate_back_kernel(
    micro, frames, count, meta, dg_ref, hb_ref, ha_ref, gn_ref, rs_ref, ggate_ref, wk_ref, gp_ref,
    dup_ref, dk_ref, dgain_ref, buf, vbuf, res, out,
):
    segs = [segments_of(meta, m, count, frames) for m in range(micro)]
    clear(buf)
    clear(vbuf)
    seen = set()
    for g, blocks, members in channel_groups(dg_ref.shape[1], micro):
        length = segs[members[0][0]][5]
        if len(members) > 1:
            clear(buf)
            clear(vbuf)
        for m, sub in members:
            stage(segs[m], dg_ref, m * frames, frames, hb_ref.at[m], ha_ref.at[m], buf, blocks, sub)
            stage(segs[m], gn_ref, m * frames, frames, None, None, vbuf, blocks, sub)
            length = jnp.maximum(length, segs[m][5])
        convolve(length, wk_ref.at[g], buf, res, True)
        sums = tap_sums(length, vbuf, buf)
        for k in range(KER):
            dk_ref[g, k] = dk_ref[g, k] + sums[k] if g in seen else sums[k]
        seen.add(g)
        for m, sub in members:
            unstage(segs[m], res, out, m * frames, blocks, sub)
    gain = ggate_ref[...]
    inverse = 1.0 / gain
    for m in range(micro):
        at = slice(m * frames, (m + 1) * frames)
        vh = gn_ref[at, :].astype(f32) * inverse
        dv, dgain = norm_back(vh, rs_ref[at, 0:1], gain, out[at, :])
        dgain_ref[...] = dgain if m == 0 else dgain_ref[...] + dgain
        dup_ref[at, :] = (gp_ref[at, :].astype(f32) * dv).astype(bf16)


def up_back_kernel(mid_ref, dmid2_ref, gain_ref, dl_ref, dr_ref, gu_ref, dmid_ref, dgu_ref, dgain_ref, nt_ref, acc_ref):
    j = pl.program_id(0)

    @pl.when(j == 0)
    def _():
        vh, _ = norm(mid_ref[...])
        nt_ref[...] = (vh * gain_ref[2:3, :]).T.astype(bf16)
        acc_ref[...] = jnp.zeros_like(acc_ref)

    dup = jnp.where(j < 3, dl_ref[...], dr_ref[...])
    dgu_ref[...] = mm(nt_ref[...], dup).astype(bf16).reshape(dgu_ref.shape)
    acc_ref[...] += mt(dup, gu_ref[...].reshape(D, D))

    @pl.when(j == pl.num_programs(0) - 1)
    def _():
        vh, r = norm(mid_ref[...])
        dv, dgain = norm_back(vh, r, gain_ref[2:3, :], acc_ref[...])
        dgain_ref[...] = dgain
        dmid_ref[...] = dmid2_ref[...] + dv


def first_back_kernel(
    x_ref, mid_ref, dml_ref, dq_ref, gain_ref, hp_ref, win_ref, wout_ref,
    dx_ref, dhp_ref, dwin_ref, dwout_ref, dgain_ref,
    dq_s, n_ref, nt_ref, dmid_ref, df_ref, acc_ref,
):
    j = pl.program_id(0)

    @pl.when(j == 0)
    def _():
        nh, _, width = dq_ref.shape
        for i in range(nh):
            dq_s[:, i * width : (i + 1) * width] = dq_ref[i]
        vh, r = norm(mid_ref[...])
        gain = gain_ref[1:2, :]
        nt = (vh * gain).T.astype(bf16)
        dn = None
        for b in range(3):
            dq = dq_s[:, b * D : (b + 1) * D]
            dhp_ref[:, 16 * b : 16 * b + 16, :] = mm(nt, dq).astype(bf16).reshape(GROUP, 16, D)
            t = mt(dq, hp_ref[:, 16 * b : 16 * b + 16, :].reshape(D, D))
            dn = t if dn is None else dn + t
        dv, dgain = norm_back(vh, r, gain, dn)
        dgain_ref[1:2, :] = dgain
        dmid = dml_ref[...] + dv
        dmid_ref[...] = dmid
        df_ref[...] = (0.5 * dmid).astype(bf16)
        vh, _ = norm(x_ref[...].astype(f32))
        n = vh * gain_ref[0:1, :]
        n_ref[...] = n.astype(bf16)
        nt_ref[...] = n.T.astype(bf16)
        acc_ref[...] = jnp.zeros_like(acc_ref)

    win = win_ref[...].reshape(D, D)
    p = mm(n_ref[...], win)
    dh = mt(df_ref[...], wout_ref[...].reshape(D, D))
    h, dp = silu_back(p, dh)
    dwout_ref[...] = tm(h, df_ref[...]).astype(bf16).reshape(dwout_ref.shape)
    dwin_ref[...] = mm(nt_ref[...], dp).astype(bf16).reshape(dwin_ref.shape)
    acc_ref[...] += mt(dp, win)

    @pl.when(j == pl.num_programs(0) - 1)
    def _():
        vh, r = norm(x_ref[...].astype(f32))
        dv, dgain = norm_back(vh, r, gain_ref[0:1, :], acc_ref[...])
        dgain_ref[0:1, :] = dgain
        dx_ref[...] = dmid_ref[...] + dv


def to_rows(shard):
    rows, cols = shard.shape
    if cols == D:
        return shard
    return shard.reshape(rows, cols // D, D).transpose(1, 0, 2).reshape(rows * cols // D, D)


def canonical(part, name):
    count = part.shape[0]
    q = count // GROUP
    if q == 1:
        return part
    blocks = BLOCKS[name]
    rows = part.shape[1] // blocks
    part = part.reshape(GROUP, q, blocks, rows, D).transpose(0, 2, 1, 3, 4)
    return part.reshape(GROUP, blocks * q * rows, D)


def by_device(part, name, count):
    q = count // GROUP
    if q == 1:
        return part
    blocks = BLOCKS[name]
    rows = part.shape[1] // blocks // q
    part = part.reshape(GROUP, blocks, q, rows, D).transpose(0, 2, 1, 3, 4)
    return part.reshape(count, blocks * rows, D)


def bit_of(index, bit):
    return (index >> bit) & 1


def swap(v, bit, count):
    return lax.ppermute(v, AXES, [(i, i ^ (1 << bit)) for i in range(count)])


def exchange_gather(shards, count):
    me = lax.axis_index(AXES)
    bits = count.bit_length() - 1
    top, rest = [bits - 2, bits - 1], list(range(1, bits - 2))
    out = []
    for v, order in zip(shards, (rest[::-1] + top + [0], rest[::-1] + top[::-1] + [0])):
        held = []
        for bit in order:
            other = swap(v, bit, count)
            mine = bit_of(me, bit) == 1
            held = sorted(held + [bit], reverse=True)
            v = jnp.stack([jnp.where(mine, other, v), jnp.where(mine, v, other)], axis=held.index(bit))
        out.append(v.reshape((count,) + v.shape[-2:]))
    return out


def unpack(raw, pack):
    q = raw.shape[0] // GROUP
    if q == 1:
        return raw
    return jnp.concatenate(
        [canonical(raw[:, OFFSET[n] // q : (OFFSET[n] + SIZE[n]) // q], n) for n, r, b in PACKS[pack]], axis=1
    )


def gather_weights(shards, count):
    q = count // GROUP
    tiny = jnp.concatenate([shards[n].reshape(-1) for n in GAINS + KERNELS])
    tiny = jnp.pad(tiny, (0, SIZE["tiny"] // q * D - tiny.shape[0])).reshape(-1, D)
    rows = {n: tiny if n == "tiny" else to_rows(shards[n]) for n in SIZE}
    packed = {k: jnp.concatenate([rows[n] for n, r, b in pack], axis=0) for k, pack in PACKS.items()}
    raw = {"rest": lax.all_gather(packed["rest"], AXES, axis=0, tiled=False)}
    raw["a"], raw["b"] = exchange_gather([packed["a"], packed["b"]], count)
    full = {k: unpack(raw[k], k) for k in raw}
    full["last"] = packed["last"]
    tiny = raw["b"][:, OFFSET["tiny"] // q :].reshape(count, -1)
    unit = shards["gain_first"].shape[0]
    gains = tiny[:, : 5 * unit].astype(f32).reshape(count, 5, unit).transpose(1, 0, 2).reshape(5, D)
    gains = jnp.pad(gains, ((0, 3), (0, 0)))
    at = 5 * unit
    size = shards["gain_gate"].shape[0]
    gate_gain = tiny[:, at : at + size].astype(f32).reshape(1, -1)
    at += size
    kernels = []
    for n in KERNELS:
        taps, cols = shards[n].shape
        part = tiny[:, at : at + taps * cols].reshape(count, taps, cols)
        kernels.append(tap_layout(part.transpose(1, 0, 2).reshape(taps, count * cols)))
        at += taps * cols
    return full, gains, gate_gain, kernels


class Exchange:
    def __init__(self, pieces, count):
        self.pieces, self.count = pieces, count
        self.parts = [p if n == "tiny" else by_device(p, n, count) for n, p in pieces]
        self.me = lax.axis_index(AXES)
        self.bits = count.bit_length() - 1
        core = bit_of(self.me, 0)
        pairs = [p.reshape(count // 2, 2, p.shape[1], D) for p in self.parts]
        self.kept = [self.pick(p, 1, core) for p in pairs]
        self.sent = jnp.concatenate([self.pick(p, 1, 1 - core) for p in pairs], axis=1)

    def pick(self, v, axis, at):
        return lax.dynamic_index_in_dim(v, at, axis, keepdims=False)

    def pair(self):
        other = swap(self.sent, 0, self.count)
        at = 0
        sums = []
        for p in self.kept:
            sums.append(p + other[:, at : at + p.shape[1]])
            at += p.shape[1]
        half = at // 2 // 16 * 16
        rows = jnp.concatenate(sums, axis=1)
        top, rest = [self.bits - 2, self.bits - 1], list(range(1, self.bits - 2))
        self.orders = [top + rest, top[::-1] + rest]
        self.left = [list(range(self.bits - 1, 0, -1)) for _ in range(2)]
        self.lanes = [
            v.reshape((2,) * (self.bits - 1) + v.shape[1:]) for v in (rows[:, :half], rows[:, half:])
        ]

    def step(self):
        for i in range(2):
            bit = self.orders[i].pop(0)
            axis = self.left[i].index(bit)
            self.left[i].remove(bit)
            mine = bit_of(self.me, bit)
            v = self.lanes[i]
            self.lanes[i] = self.pick(v, axis, mine) + swap(self.pick(v, axis, 1 - mine), bit, self.count)

    def finish(self):
        while self.orders[0]:
            self.step()
        return split_rows(jnp.concatenate(self.lanes, axis=0), [n for n, _ in self.pieces], self.count)


def split_rows(got, names, count):
    q = count // GROUP
    out = {}
    at = 0
    for n in names:
        size = SIZE[n] // q
        part = got[at : at + size].astype(f32)
        at += size
        if n != "tiny":
            blocks = BLOCKS[n]
            rows = part.shape[0] // blocks
            part = part.reshape(blocks, rows, D).transpose(1, 0, 2).reshape(rows, blocks * D)
        out[n] = part
    return out


EARLY = ("second_in", "second_out", "merge_weight", "spare")


def by_pieces(packed, names, count):
    if count == GROUP:
        return packed
    parts = []
    at = 0
    for n in names[:-1]:
        parts.append(by_device(packed[:, at : at + SIZE[n]], n, count))
        at += SIZE[n]
    q = count // GROUP
    parts.append(packed[:, at:].reshape(count, -1, D))
    return jnp.concatenate(parts, axis=1)


def rope_tables(stream):
    half = HD // 2
    frequency = np.exp(np.arange(half, dtype=np.float32) * np.float32(-math.log(10000.0) / half))
    angles = np.arange(stream, dtype=np.float32)[:, None] * frequency.astype(np.float32)[None, :]
    cos, sin = np.cos(angles), np.sin(angles)
    return (
        jnp.asarray(np.concatenate([cos, cos], axis=1), f32),
        jnp.asarray(np.concatenate([-sin, sin], axis=1), f32),
    )


def on_device(frames, cotangent, lengths, *weights):
    shards = dict(zip(ORDER, weights))
    nh = lax.axis_size("head")
    devices = nh * lax.axis_size("seq")
    micro, _, F, _ = frames.shape
    T = micro * F
    lh = D // HD // nh
    W = 3 * D // nh
    O = lh * HD
    S = nh * F
    U = lengths.shape[2]
    FF = 4 * D
    CH = 3 * D
    meta = jnp.concatenate(
        [lengths.reshape(-1), (lax.axis_index("head") * F).astype(jnp.int32).reshape(1)]
    ).astype(jnp.int32)
    packs, gains, gate_gain, (gate_taps, merge_taps) = gather_weights(shards, devices)
    EA, EB, E = packs["a"], packs["b"], packs["rest"]
    x = frames.reshape(T, D)
    cot = cotangent.reshape(T, D)
    up = [(i, i + 1) for i in range(nh - 1)]
    down = [(i + 1, i) for i in range(nh - 1)]

    def halo(first, last):
        return lax.ppermute(last, "head", up), lax.ppermute(first, "head", down)

    def exchange(v):
        return lax.all_to_all(v, "head", split_axis=0, concat_axis=0, tiled=True)

    def bind(kernel, *args):
        def bound(*refs):
            return kernel(*args, *refs)

        return bound

    rows = lambda c, d: sds((T, c), d)
    full = lambda c: whole((T, c))
    edge = lambda c: sds((micro, 16, c), bf16)
    edge_spec = lambda c: whole((micro, 16, c))
    vm = pltpu.VMEM
    PR = gapped_rows(F, U)
    buf = vm((PR * 8, 128), f32)
    nb = FF // D
    same = lambda j: j

    mid1, qkv = call(
        bind(first_kernel, nh), "first",
        (rows(D, f32), sds((nh, T, W), bf16)),
        [full(D), whole((8, D)), columns_spec("first_in", same), rows_spec("first_out", same), whole_spec("head_projection")],
        (full(D), whole((nh, T, W))),
        [vm((T, D), bf16), vm((T, D), f32), vm((T, 3 * D), bf16)],
        grid=(nb,), us=8,
    )(x, gains, EA, EB, EA)
    qkv_r = exchange(qkv).reshape(nh, micro, F, W)
    mid1, last = lax.optimization_barrier((mid1, packs["last"]))
    EL = unpack(lax.all_gather(last, AXES, axis=0, tiled=False), "last")

    zl, gp, gn, rs, fe, le = call(
        bind(up_kernel, micro, F), "up",
        (rows(CH, bf16), rows(2 * CH, bf16), rows(CH, bf16), rows(128, f32), edge(CH), edge(CH)),
        [full(D), whole((8, D)), whole((1, CH)), columns_spec("gated_up", same)],
        (
            pl.BlockSpec((T, D), lambda j: (0, jnp.minimum(j, 2))),
            pl.BlockSpec((T, D), lambda j: (0, j)),
            full(CH), full(128), edge_spec(CH), edge_spec(CH),
        ),
        [vm((T, D), bf16), vm((T, CH), f32)],
        grid=(6,), us=15,
    )(mid1, gains, gate_gain, E)
    gate_b, gate_a = halo(fe, le)

    cos, sin = rope_tables(S)
    qkv_spec = pl.BlockSpec((nh, 1, F, W), lambda m: (0, m, 0, 0))
    o_spec = pl.BlockSpec((nh, 1, F, O), lambda m: (0, m, 0, 0))
    l_spec = pl.BlockSpec((1, S, 128), lambda m: (m, 0, 0))
    head_buf = vm((lh, S, HD), bf16)
    o_own, logs = call(
        bind(attend_kernel, lh, U), "attend",
        (sds((nh, micro, F, O), bf16), sds((micro, S, 128), f32)),
        [SMEM, qkv_spec, whole((S, HD)), whole((S, HD))],
        (o_spec, l_spec),
        [head_buf] * 3,
        grid=(micro,), us=12,
    )(meta, qkv_r, cos, sin)
    o_r = exchange(o_own.reshape(nh, T, O))

    gate, c = call(
        bind(gate_kernel, micro, F, U), "gate",
        (rows(CH, bf16), rows(D, bf16)),
        [SMEM, full(CH), edge_spec(CH), edge_spec(CH), full(CH), whole(gate_taps.shape), whole_spec("gated_down")],
        (full(CH), full(D)),
        [buf, buf, vm((T, CH), f32)],
        us=18,
    )(meta, gn, gate_b, gate_a, zl, gate_taps, E)

    jn, fe, le = call(
        bind(join_kernel, micro, F), "join",
        (rows(2 * D, bf16), edge(2 * D), edge(2 * D)),
        [whole((nh, T, O)), full(D), whole_spec("output_projection")],
        (full(2 * D), edge_spec(2 * D), edge_spec(2 * D)),
        us=2,
    )(o_r, c, E)
    jn_b, jn_a = halo(fe, le)

    mixed, mid2 = call(
        bind(merge_kernel, micro, F, U), "merge",
        (rows(2 * D, bf16), rows(D, f32)),
        [SMEM, full(2 * D), edge_spec(2 * D), edge_spec(2 * D), whole(merge_taps.shape), whole_spec("merge_weight"), full(D)],
        (full(2 * D), full(D)),
        [buf, buf, vm((T, 2 * D), f32)],
        us=12,
    )(meta, jn, jn_b, jn_a, merge_taps, E, mid1)

    there_back = lambda j: jnp.where(j < nb, j, 2 * nb - 1 - j)
    out_rows, dmid2, dm, fe, le, d_early, dgain2 = call(
        bind(second_kernel, micro, F), "second",
        (
            rows(D, bf16), rows(D, f32), rows(2 * D, bf16), edge(2 * D), edge(2 * D),
            sds((GROUP, 192, D), bf16), sds((8, D), f32),
        ),
        [full(D), full(D), whole((8, D)), columns_spec("second_in", there_back), rows_spec("second_out", there_back), whole_spec("merge_weight"), full(2 * D)],
        (
            full(D), full(D), full(2 * D), edge_spec(2 * D), edge_spec(2 * D),
            whole((GROUP, 160, D)),
            whole((8, D)),
        ),
        [vm((T, D), bf16), vm((D, T), bf16), vm((nb, T, D), f32), vm((T, D), f32), vm((T, D), f32), vm((T, D), bf16)],
        grid=(2 * nb,), us=25,
    )(mid2, cot, gains, EL, EL, E, mixed)
    early = lax.psum_scatter(
        by_pieces(d_early, EARLY, devices).reshape(-1, D), AXES, scatter_dimension=0, tiled=True
    )
    dm_b, dm_a = halo(fe, le)

    da, dc, do, merge_sums = call(
        bind(merge_back_kernel, micro, F, U), "merge_back",
        (rows(D, bf16), rows(D, bf16), sds((nh, T, O), bf16), sds(merge_taps.shape, f32)),
        [SMEM, full(2 * D), edge_spec(2 * D), edge_spec(2 * D), full(2 * D), whole(merge_taps.shape), whole_spec("output_projection")],
        (full(D), full(D), whole((nh, T, O)), whole(merge_taps.shape)),
        [buf, buf, buf, vm((T, 2 * D), f32)],
        us=20,
    )(meta, dm, dm_b, dm_a, jn, merge_taps, E)
    do_r = exchange(do).reshape(nh, micro, F, O)

    column = pl.BlockSpec((T, D), lambda j: (0, j))
    edge_column = pl.BlockSpec((micro, 16, D), lambda j: (0, 0, j))
    d_down, dup_l, dgate, fe, le = call(
        bind(gate_pre_kernel, micro, F), "gate_pre",
        (sds((GROUP, 64, D), bf16), rows(CH, bf16), rows(CH, bf16), edge(CH), edge(CH)),
        [full(D), full(D), whole((nh, T, O)), column, column, column, whole_spec("gated_down")],
        (whole((GROUP, 64, D)), column, column, edge_column, edge_column),
        [vm((CH, D), bf16), vm((CH, D), bf16)],
        grid=(3,), us=8,
    )(dc, da, o_r, zl, gate, gp, E)
    dg_b, dg_a = halo(fe, le)

    dqkv = call(
        bind(attend_back_kernel, lh, U), "attend_back",
        sds((nh, micro, F, W), bf16),
        [SMEM, qkv_spec, whole((S, HD)), whole((S, HD)), o_spec, l_spec, o_spec],
        qkv_spec,
        [head_buf] * 4 + [vm((lh, HD, S), bf16)] * 2 + [vm((lh, S, HD), f32)] + [vm((lh, HD, S), f32)] * 2,
        grid=(micro,), us=1,
    )(meta, qkv_r, cos, sin, o_own, logs, do_r)
    dgate, dqkv = lax.optimization_barrier((dgate, dqkv))
    dqkv_r = exchange(dqkv.reshape(nh, T, W))

    dup_r, gate_sums, dgain_gate = call(
        bind(gate_back_kernel, micro, F, U), "gate_back",
        (rows(CH, bf16), sds(gate_taps.shape, f32), sds((1, CH), f32)),
        [
            SMEM, full(CH), edge_spec(CH), edge_spec(CH), full(CH), full(128), whole((1, CH)), whole(gate_taps.shape),
            pl.BlockSpec((T, CH), lambda *_: (0, 1)),
        ],
        (full(CH), whole(gate_taps.shape), whole((1, CH))),
        [buf, buf, buf, vm((T, CH), f32)],
        us=1,
    )(meta, dgate, dg_b, dg_a, gn, rs, gate_gain, gate_taps, gp)

    dup_r, dqkv_r = lax.optimization_barrier((dup_r, dqkv_r))
    dml, d_up, dgain3 = call(
        up_back_kernel, "up_back",
        (rows(D, f32), sds((GROUP, 96, D), bf16), sds((1, D), f32)),
        [
            full(D), full(D), whole((8, D)),
            pl.BlockSpec((T, D), lambda j: (0, jnp.minimum(j, 2))),
            pl.BlockSpec((T, D), lambda j: (0, jnp.maximum(j - 3, 0))),
            columns_spec("gated_up", same),
        ],
        (full(D), pl.BlockSpec((GROUP, 16, D), lambda j: (0, j, 0)), whole((1, D))),
        [vm((D, T), bf16), vm((T, D), f32)],
        grid=(6,), us=1,
    )(mid1, dmid2, gains, dup_l, dup_r, E)

    middle = Exchange(
        [("gated_up", d_up), ("output_projection", d_down[:, :16]), ("gated_down", d_down[:, 16:])], devices
    )
    middle.pair()
    dml, middle.lanes, early = lax.optimization_barrier((dml, middle.lanes, early))

    dx, d_head, d_first_in, d_first_out, dgain1 = call(
        first_back_kernel, "first_back",
        (
            rows(D, f32), sds((GROUP, 48, D), bf16), sds((GROUP, 64, D), bf16), sds((GROUP, 64, D), bf16),
            sds((8, D), f32),
        ),
        [
            full(D), full(D), full(D), whole((nh, T, W)), whole((8, D)),
            whole_spec("head_projection"), columns_spec("first_in", same), rows_spec("first_out", same),
        ],
        (
            full(D), whole((GROUP, 48, D)),
            pl.BlockSpec((GROUP, 16, D), lambda j: (0, j, 0)),
            pl.BlockSpec((D // 64, 64, D), lambda j: (j, 0, 0)),
            whole((8, D)),
        ),
        [vm((T, 3 * D), bf16), vm((T, D), bf16), vm((D, T), bf16), vm((T, D), f32), vm((T, D), bf16), vm((T, D), f32)],
        grid=(nb,), us=1,
    )(x, mid1, dml, dqkv_r, gains, EA, EA, EB)

    grads = {
        "gain_first": dgain1[0],
        "gain_attend": dgain1[1],
        "gain_gated": dgain3[0],
        "gain_second": dgain2[0],
        "gain_final": dgain2[1],
        "gain_gate": dgain_gate[0],
        "kernel_gate": tap_unlayout(gate_sums, CH),
        "kernel_merge": tap_unlayout(merge_sums, 2 * D),
    }
    tiny = [grads[n].reshape(devices, -1) for n in GAINS]
    for n in KERNELS:
        cols = grads[n].shape[1] // devices
        tiny.append(grads[n].reshape(KER, devices, cols).transpose(1, 0, 2).reshape(devices, -1))
    tiny = jnp.concatenate(tiny, axis=1).astype(bf16)
    tiny_rows = SIZE["tiny"] * GROUP // devices
    tiny = jnp.pad(tiny, ((0, 0), (0, tiny_rows * D - tiny.shape[1]))).reshape(devices, tiny_rows, D)
    late = Exchange(
        [("head_projection", d_head), ("first_in", d_first_in), ("first_out", d_first_out), ("tiny", tiny)], devices
    )
    middle.step()
    late.sent, middle.lanes = lax.optimization_barrier((late.sent, middle.lanes))
    late.pair()
    late = late.finish()
    middle = middle.finish()
    early = split_rows(early, EARLY[:-1], devices)
    shares = {**early, **middle, **late}
    flat = shares["tiny"].reshape(-1)
    at = 0
    for n in GAINS + KERNELS:
        size = shards[n].size
        shares[n] = flat[at : at + size].reshape(shards[n].shape)
        at += size
    return (
        out_rows.reshape(micro, 1, F, D),
        dx.reshape(micro, 1, F, D),
        *(shares[n] for n in ORDER),
    )


def solution(mesh):
    split = P(AXES)
    split_rows = P(AXES, None)
    split_columns = P(None, AXES)
    spec = {n: split if n in GAINS else split_columns if n in KERNELS else split_rows for n in ORDER}
    weight_specs = tuple(spec[n] for n in ORDER)
    frame_spec = P(None, "seq", "head", None)
    return jax.shard_map(
        on_device,
        mesh=mesh,
        in_specs=(frame_spec, frame_spec, P(None, "seq", None)) + weight_specs,
        out_specs=(frame_spec, frame_spec) + weight_specs,
        check_vma=False,
    )
```

```python
import math

import jax
import jax.numpy as jnp
import numpy as np
from jax import lax
from jax.experimental import pallas as pl
from jax.experimental.pallas import tpu as pltpu
from jax.sharding import PartitionSpec as P

D = 512
HD = 64
KER = 31
GAP = 15
PAD = 16
EPSILON = 1e-05
AXES = ("head", "seq")
GROUP = 32
f32 = jnp.float32
bf16 = jnp.bfloat16

PACKS = {
    "a": (("head_projection", 48, 3), ("first_in", 64, 4)),
    "b": (("first_out", 64, 1), ("tiny", 16, 1)),
    "rest": (("gated_up", 96, 6), ("gated_down", 48, 1), ("output_projection", 16, 1), ("merge_weight", 32, 1)),
    "last": (("second_in", 64, 4), ("second_out", 64, 1)),
}
OFFSET = {}
SIZE = {}
BLOCKS = {}
for _pack in PACKS.values():
    _at = 0
    for _name, _rows, _blocks in _pack:
        OFFSET[_name], SIZE[_name], BLOCKS[_name] = _at, _rows, _blocks
        _at += _rows

ORDER = (
    "gain_first",
    "first_in",
    "first_out",
    "gain_attend",
    "head_projection",
    "output_projection",
    "gain_gated",
    "gated_up",
    "gain_gate",
    "kernel_gate",
    "gated_down",
    "kernel_merge",
    "merge_weight",
    "gain_second",
    "second_in",
    "second_out",
    "gain_final",
)
GAINS = ("gain_first", "gain_attend", "gain_gated", "gain_second", "gain_final", "gain_gate")
KERNELS = ("kernel_gate", "kernel_merge")


def mm(a, b):
    return jnp.dot(a, b, preferred_element_type=f32)


def mt(a, b):
    return lax.dot_general(a, b, (((1,), (1,)), ((), ())), preferred_element_type=f32)


def tm(a, b):
    return lax.dot_general(a, b, (((0,), (0,)), ((), ())), preferred_element_type=f32)


def norm(v):
    centre = v - jnp.mean(v, axis=-1, keepdims=True)
    scaling = lax.rsqrt(jnp.mean(centre * centre, axis=-1, keepdims=True) + EPSILON)
    return centre * scaling, scaling


def norm_back(vh, scaling, gain, dz):
    t = dz * gain
    dv = scaling * (
        t - jnp.mean(t, axis=-1, keepdims=True) - vh * jnp.mean(t * vh, axis=-1, keepdims=True)
    )
    return dv, jnp.sum(dz * vh, axis=0, keepdims=True)


def sigmoid(v):
    return 0.5 * jnp.tanh(0.5 * v) + 0.5


def call(kernel, name, out_shape, in_specs, out_specs, scratch=(), grid=(1,), us=10, aliases=None):
    return pl.pallas_call(
        kernel,
        name=name,
        out_shape=out_shape,
        grid=grid,
        in_specs=in_specs,
        out_specs=out_specs,
        scratch_shapes=list(scratch),
        input_output_aliases=aliases or {},
        compiler_params=pltpu.CompilerParams(
            vmem_limit_bytes=60 << 20, dimension_semantics=("arbitrary",) * len(grid)
        ),
        cost_estimate=pl.CostEstimate(
            flops=int(us * 5e8), bytes_accessed=int(us * 2.5e6), transcendentals=0
        ),
    )


def whole(shape):
    zeros = (0,) * len(shape)
    return pl.BlockSpec(shape, lambda *_: zeros)


SMEM = pl.BlockSpec(memory_space=pltpu.SMEM)


def columns_spec(name, pick, part=1):
    base = OFFSET[name] // 16
    return pl.BlockSpec((GROUP // part, 16, D), lambda j: (0, base + pick(j), 0))


def rows_spec(name, pick, part=1):
    rows = SIZE[name]
    base = OFFSET[name] // rows
    return pl.BlockSpec((D // rows // part, rows, D), lambda j: (pick(j), base, 0))


def whole_spec(name, part=1):
    rows = SIZE[name]
    base = OFFSET[name] // rows
    return pl.BlockSpec((GROUP // part, rows, D), lambda *_: (0, base, 0))


def join(side, pair, own, other):
    core = side[0]
    pair[:, pl.ds(core, 1)] = own[:, None]
    pair[:, pl.ds(1 - core, 1)] = other[:, None]
    return pair[...].reshape(D, D)


def part(side, pair, value):
    core = side[0]
    pair[...] = value.astype(bf16).reshape(pair.shape)
    return pair[:, pl.ds(core, 1)][:, 0], pair[:, pl.ds(1 - core, 1)][:, 0]


def sds(shape, dtype):
    return jax.ShapeDtypeStruct(shape, dtype)


def segments_of(meta, m, count, frames):
    base = meta[meta.shape[0] - 1]
    low, high, offset = [], [], []
    start = jnp.int32(0)
    rank = jnp.int32(0)
    before = jnp.int32(0)
    after = jnp.int32(0)
    for s in range(count):
        end = start + meta[m * count + s]
        lo = jnp.clip(start - base, 0, frames)
        hi = jnp.clip(end - base, 0, frames)
        low.append(lo)
        high.append(hi)
        offset.append(PAD + GAP * rank)
        rank = rank + (hi > lo).astype(jnp.int32)
        first = (start <= base) & (base < end)
        before = jnp.where(first, jnp.minimum(base - start, GAP), before)
        final = base + frames - 1
        last = (start <= final) & (final < end)
        after = jnp.where(last, jnp.minimum(end - final - 1, GAP), after)
        start = end
    return low, high, offset, before, after, frames + GAP * (rank - 1)


def clear(buf):
    def body(i, c):
        buf[pl.ds(pl.multiple_of(i * 64, 64), 64), :] = jnp.zeros((64, 128), f32)
        return c

    lax.fori_loop(0, buf.shape[0] // 64, body, 0)


def stage(seg, src, row0, frames, before, after, dst, blocks, sub0):
    low, high, offset, nb, na, length = seg
    for s in range(len(low)):
        lo, hi, off = low[s], high[s], offset[s]

        @pl.when(hi > lo)
        def _():
            def body(g, c):
                r = pl.multiple_of(g * 16, 16)
                for i, cb in enumerate(blocks):
                    x = src[pl.ds(row0 + r, 16), cb * 128 : (cb + 1) * 128].astype(f32)
                    dst[pl.ds((r + off) * 8 + sub0 + i, 16, stride=8), :] = x
                return c

            lax.fori_loop(lo // 16, (hi + 15) // 16, body, 0)

    n = len(blocks)
    for s in range(len(low) - 1):
        lo, hi, off = low[s], high[s], offset[s]

        @pl.when((hi > lo) & (hi < frames))
        def _():
            def body(i, c):
                q = (hi + off + i) * 8
                if n == 8:
                    dst[pl.ds(pl.multiple_of(q, 8), 8), :] = jnp.zeros((8, 128), f32)
                else:
                    dst[pl.ds(q + sub0, n), :] = jnp.zeros((n, 128), f32)
                return c

            lax.fori_loop(0, GAP, body, 0)

    if before is None:
        xb = jnp.zeros((16, 128), f32)
        for i, cb in enumerate(blocks):
            dst[pl.ds(sub0 + i, 16, stride=8), :] = xb
            dst[pl.ds((PAD + length) * 8 + sub0 + i, 16, stride=8), :] = xb
    else:
        rows = lax.broadcasted_iota(jnp.int32, (16, 128), 0)
        kb = rows >= 16 - nb
        ka = rows < na
        for i, cb in enumerate(blocks):
            xb = jnp.where(kb, before[:, cb * 128 : (cb + 1) * 128].astype(f32), 0.0)
            xa = jnp.where(ka, after[:, cb * 128 : (cb + 1) * 128].astype(f32), 0.0)
            dst[pl.ds(sub0 + i, 16, stride=8), :] = xb
            dst[pl.ds((PAD + length) * 8 + sub0 + i, 16, stride=8), :] = xa


def unstage(seg, src, dst, row0, blocks, sub0):
    low, high, offset = seg[:3]
    rows = lax.broadcasted_iota(jnp.int32, (16, 128), 0)
    for s in range(len(low)):
        lo, hi, off = low[s], high[s], offset[s]

        @pl.when(hi > lo)
        def _():
            def body(g, c):
                r = pl.multiple_of(g * 16, 16)
                keep = rows >= lo - r
                for i, cb in enumerate(blocks):
                    value = src[pl.ds((r + off) * 8 + sub0 + i, 16, stride=8), :]
                    at = (pl.ds(row0 + r, 16), slice(cb * 128, (cb + 1) * 128))
                    dst[at] = jnp.where(keep, value, dst[at])
                return c

            lax.fori_loop(lo // 16, (hi + 15) // 16, body, 0)


def convolve(length, taps, buf, out, flip):
    w = [taps[30 - k if flip else k] for k in range(KER)]

    def body(b, c):
        p0 = PAD + b * 8
        acc = [None] * 8
        for j in range(38):
            v = buf[pl.ds(pl.multiple_of((p0 - 15 + j) * 8, 8), 8), :]
            for o in range(8):
                k = j - o
                if 0 <= k < KER:
                    t = w[k] * v
                    acc[o] = t if acc[o] is None else acc[o] + t
        for o in range(8):
            out[pl.ds(pl.multiple_of((p0 + o) * 8, 8), 8), :] = acc[o]
        return c

    lax.fori_loop(0, (length + 7) // 8, body, 0)


def tap_sums(length, vbuf, gbuf):
    def body(b, acc):
        acc = list(acc)
        p0 = PAD + b * 8
        v = [vbuf[pl.ds(pl.multiple_of((p0 + o) * 8, 8), 8), :] for o in range(8)]
        for j in range(38):
            g = gbuf[pl.ds(pl.multiple_of((p0 - 15 + j) * 8, 8), 8), :]
            for o in range(8):
                k = o - j + 30
                if 0 <= k < KER:
                    acc[k] = acc[k] + v[o] * g
        return tuple(acc)

    zero = tuple(jnp.zeros((8, 128), f32) for _ in range(KER))
    return lax.fori_loop(0, (length + 7) // 8, body, zero)


def channel_groups(channels, micro):
    out = []
    for g in range(channels // 1024):
        for m in range(micro):
            out.append((g, tuple(range(8 * g, 8 * g + 8)), ((m, 0),)))
    if channels % 1024:
        blocks = tuple(range(channels // 1024 * 8, channels // 128))
        for m in range(0, micro, 2):
            out.append((channels // 1024, blocks, ((m, 0), (m + 1, 4))))
    return out


def gapped_rows(frames, count):
    return -(-(frames + GAP * (count - 1) + 2 * PAD + 16) // 8) * 8


def tap_layout(kernel):
    channels = kernel.shape[1]
    out = []
    for g in range(channels // 1024):
        out.append(kernel[:, g * 1024 : (g + 1) * 1024].reshape(KER, 8, 128))
    if channels % 1024:
        half = kernel[:, channels // 1024 * 1024 :].reshape(KER, 4, 128)
        out.append(jnp.concatenate([half, half], axis=1))
    return jnp.stack(out).astype(f32)


def tap_unlayout(taps, channels):
    out = [taps[g].reshape(KER, 1024) for g in range(channels // 1024)]
    if channels % 1024:
        out.append((taps[-1][:, :4] + taps[-1][:, 4:]).reshape(KER, 512))
    return jnp.concatenate(out, axis=1)


def put_edges(value, micro, frames, first_ref, last_ref):
    for m in range(micro):
        first_ref[m] = value[m * frames : m * frames + 16]
        last_ref[m] = value[(m + 1) * frames - 16 : (m + 1) * frames]


def first_kernel(
    nh, side, x_ref, gain_ref, wina_ref, winb_ref, wouta_ref, woutb_ref, hpa_ref, hpb_ref,
    mid_ref, qkv_ref, win_ref, wout_ref, hp_ref, n_ref, acc_ref, q_ref, wi_s, wo_s,
):
    j = pl.program_id(0)

    @pl.when(j == 0)
    def _():
        vh, _ = norm(x_ref[...].astype(f32))
        n_ref[...] = (vh * gain_ref[0:1, :]).astype(bf16)
        acc_ref[...] = jnp.zeros_like(acc_ref)

    win = join(side, wi_s, wina_ref[...], winb_ref[...])
    win_ref[0] = win
    p = mm(n_ref[...], win)
    h = (p * sigmoid(p)).astype(bf16)
    wout = join(side, wo_s, wouta_ref[...], woutb_ref[...])
    wout_ref[0] = wout
    acc_ref[...] += mm(h, wout)

    @pl.when(j == pl.num_programs(0) - 1)
    def _():
        mid = x_ref[...].astype(f32) + 0.5 * acc_ref[...]
        mid_ref[...] = mid
        vh, _ = norm(mid)
        n = (vh * gain_ref[1:2, :]).astype(bf16)
        for b in range(3):
            at = slice(16 * b, 16 * b + 16)
            w = join(side, wi_s, hpa_ref[:, at, :], hpb_ref[:, at, :])
            hp_ref[b] = w
            q_ref[:, D * b : D * b + D] = mm(n, w).astype(bf16)
        width = 3 * D // nh
        for i in range(nh):
            qkv_ref[i] = q_ref[:, width * i : width * i + width]


def up_kernel(
    micro, frames, mid_ref, gain_ref, ggate_ref, gu_ref,
    zl_ref, gp_ref, gn_ref, rs_ref, fe_ref, le_ref, n_ref, zr_ref,
):
    j = pl.program_id(0)

    @pl.when(j == 0)
    def _():
        vh, _ = norm(mid_ref[...])
        n_ref[...] = (vh * gain_ref[2:3, :]).astype(bf16)

    up = mm(n_ref[...], gu_ref[...].reshape(D, D))
    phi = 0.5 + 0.5 * lax.erf(up * (1.0 / math.sqrt(2.0)))
    z = up * phi
    slope = phi + up * (jnp.exp(-0.5 * up * up) * (1.0 / math.sqrt(2.0 * math.pi)))
    gp_ref[...] = slope.astype(bf16)

    @pl.when(j < 3)
    def _():
        zl_ref[...] = z.astype(bf16)

    @pl.when(j >= 3)
    def _():
        zr_ref[:, pl.ds(pl.multiple_of((j - 3) * D, D), D)] = z

    @pl.when(j == 5)
    def _():
        vh, r = norm(zr_ref[...])
        gn = (vh * ggate_ref[...]).astype(bf16)
        gn_ref[...] = gn
        rs_ref[...] = jnp.broadcast_to(r, rs_ref.shape)
        put_edges(gn, micro, frames, fe_ref, le_ref)


def swap_halves(v):
    half = v.shape[1] // 2
    return jnp.concatenate([v[:, half:], v[:, :half]], axis=1)


def segment_ids(meta, m, count, shape, axis, start):
    pos = lax.broadcasted_iota(jnp.int32, shape, axis) + start
    ids = jnp.zeros(shape, jnp.int32)
    end = jnp.int32(0)
    for s in range(count - 1):
        end = end + meta[m * count + s]
        ids = ids + (pos >= end).astype(jnp.int32)
    return ids


SCALE = 1.0 / math.sqrt(HD)


def attend_kernel(lh, count, meta, qkv_ref, cos_ref, sin_ref, o_ref, l_ref, q_s, k_s, v_s):
    nh, _, frames, width = qkv_ref.shape
    stream = nh * frames
    m = pl.program_id(0)
    x = qkv_ref[...].reshape(stream, width)
    cos, sin = cos_ref[...], sin_ref[...]
    for h in range(lh):
        c0 = h * 3 * HD
        q = x[:, c0 : c0 + HD].astype(f32)
        k = x[:, c0 + HD : c0 + 2 * HD].astype(f32)
        q_s[h] = (q * cos + swap_halves(q) * sin).astype(bf16)
        k_s[h] = (k * cos + swap_halves(k) * sin).astype(bf16)
        v_s[h] = x[:, c0 + 2 * HD : c0 + 3 * HD]
    key_seg = segment_ids(meta, m, count, (1, stream), 1, 0)

    def body(i, c):
        at = pl.multiple_of(i * frames, frames)
        row_seg = segment_ids(meta, m, count, (frames, 1), 0, at)
        same = row_seg == key_seg
        lane = lax.broadcasted_iota(jnp.int32, (frames, 128), 1)
        pieces = []
        logs = jnp.zeros((frames, 128), f32)
        for h in range(lh):
            s = mt(q_s[h, pl.ds(at, frames), :], k_s[h])
            s = jnp.where(same, s, -1e30)
            peak = jnp.max(s, axis=1, keepdims=True)
            p = jnp.exp((s - peak) * SCALE)
            total = jnp.sum(p, axis=1, keepdims=True)
            o = mm(p.astype(bf16), v_s[h]) / total
            pieces.append(o)
            logs = jnp.where(lane == h, peak * SCALE + jnp.log(total), logs)
        o_ref[i, 0] = jnp.concatenate(pieces, axis=1).astype(bf16) if lh > 1 else pieces[0].astype(bf16)
        l_ref[0, pl.ds(at, frames), :] = logs
        return c

    lax.fori_loop(0, nh, body, 0)


def attend_back_kernel(
    lh, count, meta, qkv_ref, cos_ref, sin_ref, o_ref, l_ref, do_ref, d_ref,
    q_s, k_s, v_s, do_s, qt_s, dot_s, dq_s, dk_s, dv_s,
):
    nh, _, frames, width = qkv_ref.shape
    stream = nh * frames
    m = pl.program_id(0)
    x = qkv_ref[...].reshape(stream, width)
    do = do_ref[...].reshape(stream, lh * HD)
    cos, sin = cos_ref[...], sin_ref[...]
    for h in range(lh):
        c0 = h * 3 * HD
        q = x[:, c0 : c0 + HD].astype(f32)
        k = x[:, c0 + HD : c0 + 2 * HD].astype(f32)
        q = q * cos + swap_halves(q) * sin
        q_s[h] = q.astype(bf16)
        qt_s[h] = q.T.astype(bf16)
        k_s[h] = (k * cos + swap_halves(k) * sin).astype(bf16)
        v_s[h] = x[:, c0 + 2 * HD : c0 + 3 * HD]
        piece = do[:, h * HD : (h + 1) * HD]
        do_s[h] = piece
        dot_s[h] = piece.astype(f32).T.astype(bf16)
    dk_s[...] = jnp.zeros_like(dk_s)
    dv_s[...] = jnp.zeros_like(dv_s)
    key_seg = segment_ids(meta, m, count, (1, stream), 1, 0)

    def body(i, c):
        at = pl.multiple_of(i * frames, frames)
        row_seg = segment_ids(meta, m, count, (frames, 1), 0, at)
        same = row_seg == key_seg
        lane = lax.broadcasted_iota(jnp.int32, (frames, 128), 1)
        logs = l_ref[0, pl.ds(at, frames), :]
        o = o_ref[i, 0].astype(f32)
        for h in range(lh):
            log = jnp.sum(jnp.where(lane == h, logs, 0.0), axis=1, keepdims=True)
            dh = do_s[h, pl.ds(at, frames), :]
            delta = jnp.sum(o[:, h * HD : (h + 1) * HD] * dh.astype(f32), axis=1, keepdims=True)
            s = mt(q_s[h, pl.ds(at, frames), :], k_s[h])
            p = jnp.where(same, jnp.exp(s * SCALE - log), 0.0)
            dp = mt(dh, v_s[h])
            dr = (p * (dp - delta)).astype(bf16)
            dq_s[h, pl.ds(at, frames), :] = mm(dr, k_s[h]) * SCALE
            dk_s[h] += mm(qt_s[h, :, pl.ds(at, frames)], dr)
            dv_s[h] += mm(dot_s[h, :, pl.ds(at, frames)], p.astype(bf16))
        return c

    lax.fori_loop(0, nh, body, 0)
    pieces = []
    for h in range(lh):
        dq = dq_s[h]
        dk = dk_s[h].T * SCALE
        pieces.append(dq * cos - swap_halves(dq) * sin)
        pieces.append(dk * cos - swap_halves(dk) * sin)
        pieces.append(dv_s[h].T)
    full = jnp.concatenate(pieces, axis=1).astype(bf16)
    for i in range(nh):
        d_ref[i, 0] = full[i * frames : (i + 1) * frames]


def gate_kernel(micro, frames, count, meta, gn_ref, hb_ref, ha_ref, zl_ref, wk_ref, gd_ref, gate_ref, c_ref, buf, res, out):
    segs = [segments_of(meta, m, count, frames) for m in range(micro)]
    clear(buf)
    for g, blocks, members in channel_groups(gn_ref.shape[1], micro):
        length = segs[members[0][0]][5]
        for m, sub in members:
            stage(segs[m], gn_ref, m * frames, frames, hb_ref.at[m], ha_ref.at[m], buf, blocks, sub)
            length = jnp.maximum(length, segs[m][5])
        convolve(length, wk_ref.at[g], buf, res, False)
        for m, sub in members:
            unstage(segs[m], res, out, m * frames, blocks, sub)
    gd = gd_ref[...].reshape(gn_ref.shape[1], D)
    for m in range(micro):
        at = slice(m * frames, (m + 1) * frames)
        gate = out[at, :]
        gate_ref[at, :] = gate.astype(bf16)
        u = (zl_ref[at, :].astype(f32) * gate).astype(bf16)
        c_ref[at, :] = mm(u, gd).astype(bf16)


def join_kernel(micro, frames, o_ref, c_ref, op_ref, jn_ref, fe_ref, le_ref):
    nh = o_ref.shape[0]
    o = jnp.concatenate([o_ref[i] for i in range(nh)], axis=1)
    a = mm(o, op_ref[...].reshape(D, D)).astype(bf16)
    jn_ref[:, :D] = a
    jn_ref[:, D:] = c_ref[...]
    for m in range(micro):
        first = slice(m * frames, m * frames + 16)
        last = slice((m + 1) * frames - 16, (m + 1) * frames)
        fe_ref[m, :, :D] = a[first]
        fe_ref[m, :, D:] = c_ref[first, :]
        le_ref[m, :, :D] = a[last]
        le_ref[m, :, D:] = c_ref[last, :]


def merge_kernel(micro, frames, count, meta, jn_ref, hb_ref, ha_ref, wk_ref, mw_ref, mid_ref, m_ref, mid2_ref, buf, res, out):
    segs = [segments_of(meta, m, count, frames) for m in range(micro)]
    clear(buf)
    for g, blocks, members in channel_groups(jn_ref.shape[1], micro):
        m = members[0][0]
        stage(segs[m], jn_ref, m * frames, frames, hb_ref.at[m], ha_ref.at[m], buf, blocks, 0)
        convolve(segs[m][5], wk_ref.at[g], buf, res, False)
        unstage(segs[m], res, out, m * frames, blocks, 0)
    mw = mw_ref[...].reshape(2 * D, D)
    for m in range(micro):
        at = slice(m * frames, (m + 1) * frames)
        mixed = (jn_ref[at, :].astype(f32) + out[at, :]).astype(bf16)
        m_ref[at, :] = mixed
        mid2_ref[at, :] = mid_ref[at, :] + mm(mixed, mw)


def silu_back(p, dh):
    s = sigmoid(p)
    return (p * s).astype(bf16), (s * (1.0 + p * (1.0 - s)) * dh).astype(bf16)


def second_kernel(
    micro, frames, mid2_ref, cot_ref, gain_ref, win_ref, wout_ref, mw_ref, mixed_ref,
    out_ref, dmid2_ref, dm_ref, fe_ref, le_ref, dw_ref, dgain_ref,
    n_ref, nt_ref, p_ref, acc_ref, dmid3_ref, df_ref,
):
    j = pl.program_id(0)
    nb = pl.num_programs(0) // 2

    @pl.when(j == 0)
    def _():
        vh, _ = norm(mid2_ref[...])
        n = vh * gain_ref[3:4, :]
        n_ref[...] = n.astype(bf16)
        nt_ref[...] = n.T.astype(bf16)
        acc_ref[...] = jnp.zeros_like(acc_ref)

    @pl.when(j < nb)
    def _():
        p = mm(n_ref[...], win_ref[...].reshape(D, D))
        p_ref[j] = p
        h = (p * sigmoid(p)).astype(bf16)
        acc_ref[...] += mm(h, wout_ref[...].reshape(D, D))

    @pl.when(j == nb - 1)
    def _():
        mid3 = mid2_ref[...] + 0.5 * acc_ref[...]
        vh, r = norm(mid3)
        gain = gain_ref[4:5, :]
        out_ref[...] = (vh * gain).astype(bf16)
        dmid3, dgain = norm_back(vh, r, gain, cot_ref[...].astype(f32))
        dgain_ref[1:2, :] = dgain
        dmid3_ref[...] = dmid3
        df_ref[...] = (0.5 * dmid3).astype(bf16)
        acc_ref[...] = jnp.zeros_like(acc_ref)

    @pl.when(j >= nb)
    def _():
        win = win_ref[...].reshape(D, D)
        dh = mt(df_ref[...], wout_ref[...].reshape(D, D))
        h, dp = silu_back(p_ref[2 * nb - 1 - j], dh)
        at = 2 * nb - 1 - j
        few = D // 64
        dw_ref[pl.ds(at * few, few), 64:128, :] = tm(h, df_ref[...]).astype(bf16).reshape(few, 64, D)
        dw_ref[:, pl.ds(pl.multiple_of(at * 16, 16), 16), :] = mm(nt_ref[...], dp).astype(bf16).reshape(GROUP, 16, D)
        acc_ref[...] += mt(dp, win)

    @pl.when(j == 2 * nb - 1)
    def _():
        vh, r = norm(mid2_ref[...])
        dv, dgain = norm_back(vh, r, gain_ref[3:4, :], acc_ref[...])
        dgain_ref[0:1, :] = dgain
        dmid2 = dmid3_ref[...] + dv
        dmid2_ref[...] = dmid2
        dmg = dmid2.astype(bf16)
        dw_ref[:, 128:, :] = tm(mixed_ref[...], dmg).astype(bf16).reshape(GROUP, 32, D)
        dm = mt(dmg, mw_ref[...].reshape(2 * D, D)).astype(bf16)
        dm_ref[...] = dm
        put_edges(dm, micro, frames, fe_ref, le_ref)


def merge_back_kernel(
    micro, frames, count, meta, dm_ref, hb_ref, ha_ref, jn_ref, wk_ref, op_ref,
    da_ref, dc_ref, do_ref, dk_ref, buf, vbuf, res, out,
):
    segs = [segments_of(meta, m, count, frames) for m in range(micro)]
    clear(buf)
    clear(vbuf)
    total = [None] * KER
    for g, blocks, members in channel_groups(dm_ref.shape[1], micro):
        m = members[0][0]
        stage(segs[m], dm_ref, m * frames, frames, hb_ref.at[m], ha_ref.at[m], buf, blocks, 0)
        stage(segs[m], jn_ref, m * frames, frames, None, None, vbuf, blocks, 0)
        convolve(segs[m][5], wk_ref.at[g], buf, res, True)
        sums = tap_sums(segs[m][5], vbuf, buf)
        for k in range(KER):
            dk_ref[g, k] = sums[k] if m == 0 else dk_ref[g, k] + sums[k]
        unstage(segs[m], res, out, m * frames, blocks, 0)
    nh = do_ref.shape[0]
    width = D // nh
    for m in range(micro):
        at = slice(m * frames, (m + 1) * frames)
        djn = dm_ref[at, :].astype(f32) + out[at, :]
        da = djn[:, :D].astype(bf16)
        da_ref[at, :] = da
        dc_ref[at, :] = djn[:, D:].astype(bf16)
        do = mt(da, op_ref[...].reshape(D, D)).astype(bf16)
        for i in range(nh):
            do_ref[i, at, :] = do[:, i * width : (i + 1) * width]


def gate_pre_kernel(
    micro, frames, side, dc_ref, da_ref, o_ref, zl_ref, gate_ref, gp_ref, gd_ref,
    kept_ref, sent_ref, dup_ref, dgate_ref, fe_ref, le_ref, gd_s, dgd_s, dop_s,
):
    j = pl.program_id(0)

    @pl.when(j == 0)
    def _():
        gd_s[...] = gd_ref[...].reshape(gd_s.shape)
        width = o_ref.shape[2]
        for i in range(o_ref.shape[0]):
            few = width // 32
            at = slice(i * few, (i + 1) * few)
            kept_ref[at, :16, :], sent_ref[at, :16, :] = part(side, dop_s, tm(o_ref[i], da_ref[...]))

    du = mt(dc_ref[...], gd_s[pl.ds(pl.multiple_of(j * D, D), D), :])
    gate = gate_ref[...].astype(f32)
    left = zl_ref[...].astype(f32)
    u = (left * gate).astype(bf16)
    dgd_s[pl.ds(pl.multiple_of(j * D, D), D), :] = tm(u, dc_ref[...]).astype(bf16)

    @pl.when(j == pl.num_programs(0) - 1)
    def _():
        for i in range(GROUP // 2):
            for ref, core in ((kept_ref, side[0]), (sent_ref, 1 - side[0])):
                ref[i, 16:, :] = dgd_s[pl.ds(pl.multiple_of((2 * i + core) * 48, 16), 48), :]

    dup_ref[...] = (gp_ref[...].astype(f32) * (du * gate)).astype(bf16)
    dgate = (du * left).astype(bf16)
    dgate_ref[...] = dgate
    put_edges(dgate, micro, frames, fe_ref, le_ref)


def gate_back_kernel(
    micro, frames, count, meta, dg_ref, hb_ref, ha_ref, gn_ref, rs_ref, ggate_ref, wk_ref, gp_ref,
    dup_ref, dk_ref, dgain_ref, buf, vbuf, res, out,
):
    segs = [segments_of(meta, m, count, frames) for m in range(micro)]
    clear(buf)
    clear(vbuf)
    seen = set()
    for g, blocks, members in channel_groups(dg_ref.shape[1], micro):
        length = segs[members[0][0]][5]
        if len(members) > 1:
            clear(buf)
            clear(vbuf)
        for m, sub in members:
            stage(segs[m], dg_ref, m * frames, frames, hb_ref.at[m], ha_ref.at[m], buf, blocks, sub)
            stage(segs[m], gn_ref, m * frames, frames, None, None, vbuf, blocks, sub)
            length = jnp.maximum(length, segs[m][5])
        convolve(length, wk_ref.at[g], buf, res, True)
        sums = tap_sums(length, vbuf, buf)
        for k in range(KER):
            dk_ref[g, k] = dk_ref[g, k] + sums[k] if g in seen else sums[k]
        seen.add(g)
        for m, sub in members:
            unstage(segs[m], res, out, m * frames, blocks, sub)
    gain = ggate_ref[...]
    inverse = 1.0 / gain
    for m in range(micro):
        at = slice(m * frames, (m + 1) * frames)
        vh = gn_ref[at, :].astype(f32) * inverse
        dv, dgain = norm_back(vh, rs_ref[at, 0:1], gain, out[at, :])
        dgain_ref[...] = dgain if m == 0 else dgain_ref[...] + dgain
        dup_ref[at, :] = (gp_ref[at, :].astype(f32) * dv).astype(bf16)


def up_back_kernel(
    side, mid_ref, dmid2_ref, gain_ref, dl_ref, dr_ref, gu_ref,
    dmid_ref, kept_ref, sent_ref, dgain_ref, nt_ref, acc_ref, pair_s,
):
    j = pl.program_id(0)

    @pl.when(j == 0)
    def _():
        vh, _ = norm(mid_ref[...])
        nt_ref[...] = (vh * gain_ref[2:3, :]).T.astype(bf16)
        acc_ref[...] = jnp.zeros_like(acc_ref)

    dup = jnp.where(j < 3, dl_ref[...], dr_ref[...])
    kept_ref[...], sent_ref[...] = part(side, pair_s, mm(nt_ref[...], dup))
    acc_ref[...] += mt(dup, gu_ref[...].reshape(D, D))

    @pl.when(j == pl.num_programs(0) - 1)
    def _():
        vh, r = norm(mid_ref[...])
        dv, dgain = norm_back(vh, r, gain_ref[2:3, :], acc_ref[...])
        dgain_ref[...] = dgain
        dmid_ref[...] = dmid2_ref[...] + dv


def first_back_kernel(
    side, x_ref, mid_ref, dml_ref, dq_ref, gain_ref, hp_ref, win_ref, wout_ref,
    dx_ref, dhpk_ref, dhps_ref, dwik_ref, dwis_ref, dwok_ref, dwos_ref, dgain_ref,
    dq_s, n_ref, nt_ref, dmid_ref, df_ref, acc_ref, pi_s, po_s,
):
    j = pl.program_id(0)

    @pl.when(j == 0)
    def _():
        nh, _, width = dq_ref.shape
        for i in range(nh):
            dq_s[:, i * width : (i + 1) * width] = dq_ref[i]
        vh, r = norm(mid_ref[...])
        gain = gain_ref[1:2, :]
        nt = (vh * gain).T.astype(bf16)
        dn = None
        for b in range(3):
            dq = dq_s[:, b * D : (b + 1) * D]
            at = slice(16 * b, 16 * b + 16)
            dhpk_ref[:, at, :], dhps_ref[:, at, :] = part(side, pi_s, mm(nt, dq))
            t = mt(dq, hp_ref[b])
            dn = t if dn is None else dn + t
        dv, dgain = norm_back(vh, r, gain, dn)
        dgain_ref[1:2, :] = dgain
        dmid = dml_ref[...] + dv
        dmid_ref[...] = dmid
        df_ref[...] = (0.5 * dmid).astype(bf16)
        vh, _ = norm(x_ref[...].astype(f32))
        n = vh * gain_ref[0:1, :]
        n_ref[...] = n.astype(bf16)
        nt_ref[...] = n.T.astype(bf16)
        acc_ref[...] = jnp.zeros_like(acc_ref)

    win = win_ref[0]
    p = mm(n_ref[...], win)
    dh = mt(df_ref[...], wout_ref[0])
    h, dp = silu_back(p, dh)
    dwok_ref[...], dwos_ref[...] = part(side, po_s, tm(h, df_ref[...]))
    dwik_ref[...], dwis_ref[...] = part(side, pi_s, mm(nt_ref[...], dp))
    acc_ref[...] += mt(dp, win)

    @pl.when(j == pl.num_programs(0) - 1)
    def _():
        vh, r = norm(x_ref[...].astype(f32))
        dv, dgain = norm_back(vh, r, gain_ref[0:1, :], acc_ref[...])
        dgain_ref[0:1, :] = dgain
        dx_ref[...] = dmid_ref[...] + dv


def to_rows(shard):
    rows, cols = shard.shape
    if cols == D:
        return shard
    return shard.reshape(rows, cols // D, D).transpose(1, 0, 2).reshape(rows * cols // D, D)


def canonical(part, name):
    count = part.shape[0]
    q = count // GROUP
    if q == 1:
        return part
    blocks = BLOCKS[name]
    rows = part.shape[1] // blocks
    part = part.reshape(GROUP, q, blocks, rows, D).transpose(0, 2, 1, 3, 4)
    return part.reshape(GROUP, blocks * q * rows, D)


def by_device(part, name, count):
    q = count // GROUP
    if q == 1:
        return part
    blocks = BLOCKS[name]
    rows = part.shape[1] // blocks // q
    part = part.reshape(GROUP, blocks, q, rows, D).transpose(0, 2, 1, 3, 4)
    return part.reshape(count, blocks * rows, D)


def bit_of(index, bit):
    return (index >> bit) & 1


def swap(v, bit, count):
    return lax.ppermute(v, AXES, [(i, i ^ (1 << bit)) for i in range(count)])


def exchange_gather(shards, count):
    me = lax.axis_index(AXES)
    bits = count.bit_length() - 1
    top, rest = [bits - 2, bits - 1], list(range(1, bits - 2))
    out = []
    for v, order in zip(shards, (rest[::-1] + top, rest[::-1] + top[::-1])):
        held = []
        for bit in order:
            other = swap(v, bit, count)
            mine = bit_of(me, bit) == 1
            held = sorted(held + [bit], reverse=True)
            v = jnp.stack([jnp.where(mine, other, v), jnp.where(mine, v, other)], axis=held.index(bit))
        v = v.reshape((count // 2,) + v.shape[-2:])
        out.append((v, swap(v, 0, count)))
    return out


def whole_pack(own, other):
    mine = bit_of(lax.axis_index(AXES), 0) == 1
    both = jnp.stack([jnp.where(mine, other, own), jnp.where(mine, own, other)], axis=1)
    return both.reshape((-1,) + own.shape[1:])


def unpack(raw, pack):
    q = raw.shape[0] // GROUP
    if q == 1:
        return raw
    return jnp.concatenate(
        [canonical(raw[:, OFFSET[n] // q : (OFFSET[n] + SIZE[n]) // q], n) for n, r, b in PACKS[pack]], axis=1
    )


def gather_weights(shards, count):
    q = count // GROUP
    tiny = jnp.concatenate([shards[n].reshape(-1) for n in GAINS + KERNELS])
    tiny = jnp.pad(tiny, (0, SIZE["tiny"] // q * D - tiny.shape[0])).reshape(-1, D)
    rows = {n: tiny if n == "tiny" else to_rows(shards[n]) for n in SIZE}
    packed = {k: jnp.concatenate([rows[n] for n, r, b in pack], axis=0) for k, pack in PACKS.items()}
    raw = {"rest": lax.all_gather(packed["rest"], AXES, axis=0, tiled=False)}
    full = {"rest": unpack(raw["rest"], "rest"), "last": packed["last"]}
    pairs = dict(zip("ab", exchange_gather([packed["a"], packed["b"]], count)))
    for k in pairs:
        if q == 1:
            full[k] = pairs[k]
        else:
            v = unpack(whole_pack(*pairs[k]), k)
            full[k] = (v[0::2], v[1::2])
    tiny = whole_pack(*(v[:, OFFSET["tiny"] // q :] for v in pairs["b"])).reshape(count, -1)
    unit = shards["gain_first"].shape[0]
    gains = tiny[:, : 5 * unit].astype(f32).reshape(count, 5, unit).transpose(1, 0, 2).reshape(5, D)
    gains = jnp.pad(gains, ((0, 3), (0, 0)))
    at = 5 * unit
    size = shards["gain_gate"].shape[0]
    gate_gain = tiny[:, at : at + size].astype(f32).reshape(1, -1)
    at += size
    kernels = []
    for n in KERNELS:
        taps, cols = shards[n].shape
        part = tiny[:, at : at + taps * cols].reshape(count, taps, cols)
        kernels.append(tap_layout(part.transpose(1, 0, 2).reshape(taps, count * cols)))
        at += taps * cols
    return full, gains, gate_gain, kernels


class Exchange:
    def __init__(self, pieces, count):
        self.count = count
        self.names = [n for names, _ in pieces for n in names]
        self.me = lax.axis_index(AXES)
        self.bits = count.bit_length() - 1
        core = bit_of(self.me, 0)
        self.kept, self.sent = [], []
        for names, arrays in pieces:
            if names == ("tiny",):
                arrays = [arrays]
            elif count == GROUP:
                self.kept.append(arrays[0])
                self.sent.append(arrays[1])
                continue
            else:
                packed = jnp.stack(arrays, axis=1).reshape(GROUP, -1, D)
                arrays = [by_pieces(packed, names, count)]
            for p in arrays:
                p = p.reshape(count // 2, 2, p.shape[1], D)
                self.kept.append(self.pick(p, 1, core))
                self.sent.append(self.pick(p, 1, 1 - core))

    def pick(self, v, axis, at):
        return lax.dynamic_index_in_dim(v, at, axis, keepdims=False)

    def pair(self):
        sums = [p + swap(v, 0, self.count) for p, v in zip(self.kept, self.sent)]
        at = sum(p.shape[1] for p in sums)
        half = at // 2 // 16 * 16
        rows = jnp.concatenate(sums, axis=1)
        top, rest = [self.bits - 2, self.bits - 1], list(range(1, self.bits - 2))
        self.orders = [top + rest, top[::-1] + rest]
        self.left = [list(range(self.bits - 1, 0, -1)) for _ in range(2)]
        self.lanes = [
            v.reshape((2,) * (self.bits - 1) + v.shape[1:]) for v in (rows[:, :half], rows[:, half:])
        ]

    def step(self):
        for i in range(2):
            bit = self.orders[i].pop(0)
            axis = self.left[i].index(bit)
            self.left[i].remove(bit)
            mine = bit_of(self.me, bit)
            v = self.lanes[i]
            self.lanes[i] = self.pick(v, axis, mine) + swap(self.pick(v, axis, 1 - mine), bit, self.count)

    def finish(self):
        while self.orders[0]:
            self.step()
        return split_rows(jnp.concatenate(self.lanes, axis=0), self.names, self.count)


def split_rows(got, names, count):
    q = count // GROUP
    out = {}
    at = 0
    for n in names:
        size = SIZE[n] // q
        part = got[at : at + size].astype(f32)
        at += size
        if n != "tiny":
            blocks = BLOCKS[n]
            rows = part.shape[0] // blocks
            part = part.reshape(blocks, rows, D).transpose(1, 0, 2).reshape(rows, blocks * D)
        out[n] = part
    return out


EARLY = ("second_in", "second_out", "merge_weight")


def by_pieces(packed, names, count):
    if count == GROUP:
        return packed
    parts = []
    at = 0
    for n in names:
        parts.append(by_device(packed[:, at : at + SIZE[n]], n, count))
        at += SIZE[n]
    if at < packed.shape[1]:
        parts.append(packed[:, at:].reshape(count, -1, D))
    return jnp.concatenate(parts, axis=1)


def rope_tables(stream):
    half = HD // 2
    frequency = np.exp(np.arange(half, dtype=np.float32) * np.float32(-math.log(10000.0) / half))
    angles = np.arange(stream, dtype=np.float32)[:, None] * frequency.astype(np.float32)[None, :]
    cos, sin = np.cos(angles), np.sin(angles)
    return (
        jnp.asarray(np.concatenate([cos, cos], axis=1), f32),
        jnp.asarray(np.concatenate([-sin, sin], axis=1), f32),
    )


def on_device(frames, cotangent, lengths, *weights):
    shards = dict(zip(ORDER, weights))
    nh = lax.axis_size("head")
    devices = nh * lax.axis_size("seq")
    micro, _, F, _ = frames.shape
    T = micro * F
    lh = D // HD // nh
    W = 3 * D // nh
    O = lh * HD
    S = nh * F
    U = lengths.shape[2]
    FF = 4 * D
    CH = 3 * D
    meta = jnp.concatenate(
        [lengths.reshape(-1), (lax.axis_index("head") * F).astype(jnp.int32).reshape(1)]
    ).astype(jnp.int32)
    packs, gains, gate_gain, (gate_taps, merge_taps) = gather_weights(shards, devices)
    EA, EB, E = packs["a"], packs["b"], packs["rest"]
    core = lax.axis_index(AXES) & 1 if devices == GROUP else 0
    side = jnp.asarray(core, jnp.int32).reshape(1)
    x = frames.reshape(T, D)
    cot = cotangent.reshape(T, D)
    up = [(i, i + 1) for i in range(nh - 1)]
    down = [(i + 1, i) for i in range(nh - 1)]

    def halo(first, last):
        return lax.ppermute(last, "head", up), lax.ppermute(first, "head", down)

    def exchange(v):
        return lax.all_to_all(v, "head", split_axis=0, concat_axis=0, tiled=True)

    def bind(kernel, *args):
        def bound(*refs):
            return kernel(*args, *refs)

        return bound

    rows = lambda c, d: sds((T, c), d)
    full = lambda c: whole((T, c))
    edge = lambda c: sds((micro, 16, c), bf16)
    edge_spec = lambda c: whole((micro, 16, c))
    vm = pltpu.VMEM
    PR = gapped_rows(F, U)
    buf = vm((PR * 8, 128), f32)
    nb = FF // D
    same = lambda j: j

    first_in_specs = [columns_spec("first_in", same, 2)] * 2
    first_out_specs = [rows_spec("first_out", same, 2)] * 2
    head_specs = [whole_spec("head_projection", 2)] * 2
    columns_pair = vm((GROUP // 2, 2, 16, D), bf16)
    rows_pair = vm((D // 128, 2, 64, D), bf16)
    half_columns = pl.BlockSpec((GROUP // 2, 16, D), lambda j: (0, j, 0))
    half_rows = pl.BlockSpec((D // 128, 64, D), lambda j: (j, 0, 0))
    half = lambda r: sds((GROUP // 2, r, D), bf16)

    square = pl.BlockSpec((1, D, D), lambda j: (j, 0, 0))
    mid1, qkv, first_in, first_out, head = call(
        bind(first_kernel, nh), "first",
        (
            rows(D, f32), sds((nh, T, W), bf16),
            sds((nb, D, D), bf16), sds((nb, D, D), bf16), sds((3, D, D), bf16),
        ),
        [SMEM, full(D), whole((8, D)), *first_in_specs, *first_out_specs, *head_specs],
        (full(D), whole((nh, T, W)), square, square, whole((3, D, D))),
        [vm((T, D), bf16), vm((T, D), f32), vm((T, 3 * D), bf16), columns_pair, rows_pair],
        grid=(nb,), us=8,
    )(side, x, gains, *EA, *EB, *EA)
    qkv_r = exchange(qkv).reshape(nh, micro, F, W)
    mid1, last = lax.optimization_barrier((mid1, packs["last"]))
    EL = unpack(lax.all_gather(last, AXES, axis=0, tiled=False), "last")

    zl, gp, gn, rs, fe, le = call(
        bind(up_kernel, micro, F), "up",
        (rows(CH, bf16), rows(2 * CH, bf16), rows(CH, bf16), rows(128, f32), edge(CH), edge(CH)),
        [full(D), whole((8, D)), whole((1, CH)), columns_spec("gated_up", same)],
        (
            pl.BlockSpec((T, D), lambda j: (0, jnp.minimum(j, 2))),
            pl.BlockSpec((T, D), lambda j: (0, j)),
            full(CH), full(128), edge_spec(CH), edge_spec(CH),
        ),
        [vm((T, D), bf16), vm((T, CH), f32)],
        grid=(6,), us=15,
    )(mid1, gains, gate_gain, E)
    gate_b, gate_a = halo(fe, le)

    cos, sin = rope_tables(S)
    qkv_spec = pl.BlockSpec((nh, 1, F, W), lambda m: (0, m, 0, 0))
    o_spec = pl.BlockSpec((nh, 1, F, O), lambda m: (0, m, 0, 0))
    l_spec = pl.BlockSpec((1, S, 128), lambda m: (m, 0, 0))
    head_buf = vm((lh, S, HD), bf16)
    o_own, logs = call(
        bind(attend_kernel, lh, U), "attend",
        (sds((nh, micro, F, O), bf16), sds((micro, S, 128), f32)),
        [SMEM, qkv_spec, whole((S, HD)), whole((S, HD))],
        (o_spec, l_spec),
        [head_buf] * 3,
        grid=(micro,), us=12,
    )(meta, qkv_r, cos, sin)
    o_r = exchange(o_own.reshape(nh, T, O))

    gate, c = call(
        bind(gate_kernel, micro, F, U), "gate",
        (rows(CH, bf16), rows(D, bf16)),
        [SMEM, full(CH), edge_spec(CH), edge_spec(CH), full(CH), whole(gate_taps.shape), whole_spec("gated_down")],
        (full(CH), full(D)),
        [buf, buf, vm((T, CH), f32)],
        us=18,
    )(meta, gn, gate_b, gate_a, zl, gate_taps, E)

    jn, fe, le = call(
        bind(join_kernel, micro, F), "join",
        (rows(2 * D, bf16), edge(2 * D), edge(2 * D)),
        [whole((nh, T, O)), full(D), whole_spec("output_projection")],
        (full(2 * D), edge_spec(2 * D), edge_spec(2 * D)),
        us=2,
    )(o_r, c, E)
    jn_b, jn_a = halo(fe, le)

    mixed, mid2 = call(
        bind(merge_kernel, micro, F, U), "merge",
        (rows(2 * D, bf16), rows(D, f32)),
        [SMEM, full(2 * D), edge_spec(2 * D), edge_spec(2 * D), whole(merge_taps.shape), whole_spec("merge_weight"), full(D)],
        (full(2 * D), full(D)),
        [buf, buf, vm((T, 2 * D), f32)],
        us=12,
    )(meta, jn, jn_b, jn_a, merge_taps, E, mid1)

    there_back = lambda j: jnp.where(j < nb, j, 2 * nb - 1 - j)
    out_rows, dmid2, dm, fe, le, d_early, dgain2 = call(
        bind(second_kernel, micro, F), "second",
        (
            rows(D, bf16), rows(D, f32), rows(2 * D, bf16), edge(2 * D), edge(2 * D),
            sds((GROUP, 192, D), bf16), sds((8, D), f32),
        ),
        [full(D), full(D), whole((8, D)), columns_spec("second_in", there_back), rows_spec("second_out", there_back), whole_spec("merge_weight"), full(2 * D)],
        (
            full(D), full(D), full(2 * D), edge_spec(2 * D), edge_spec(2 * D),
            whole((GROUP, 160, D)),
            whole((8, D)),
        ),
        [vm((T, D), bf16), vm((D, T), bf16), vm((nb, T, D), f32), vm((T, D), f32), vm((T, D), f32), vm((T, D), bf16)],
        grid=(2 * nb,), us=25,
    )(mid2, cot, gains, EL, EL, E, mixed)
    early = lax.psum_scatter(
        by_pieces(d_early, EARLY, devices).reshape(-1, D), AXES, scatter_dimension=0, tiled=True
    )
    dm_b, dm_a = halo(fe, le)

    da, dc, do, merge_sums = call(
        bind(merge_back_kernel, micro, F, U), "merge_back",
        (rows(D, bf16), rows(D, bf16), sds((nh, T, O), bf16), sds(merge_taps.shape, f32)),
        [SMEM, full(2 * D), edge_spec(2 * D), edge_spec(2 * D), full(2 * D), whole(merge_taps.shape), whole_spec("output_projection")],
        (full(D), full(D), whole((nh, T, O)), whole(merge_taps.shape)),
        [buf, buf, buf, vm((T, 2 * D), f32)],
        us=20,
    )(meta, dm, dm_b, dm_a, jn, merge_taps, E)
    do_r = exchange(do).reshape(nh, micro, F, O)

    column = pl.BlockSpec((T, D), lambda j: (0, j))
    edge_column = pl.BlockSpec((micro, 16, D), lambda j: (0, 0, j))
    *d_down, dup_l, dgate, fe, le = call(
        bind(gate_pre_kernel, micro, F), "gate_pre",
        (half(64), half(64), rows(CH, bf16), rows(CH, bf16), edge(CH), edge(CH)),
        [SMEM, full(D), full(D), whole((nh, T, O)), column, column, column, whole_spec("gated_down")],
        (whole((GROUP // 2, 64, D)), whole((GROUP // 2, 64, D)), column, column, edge_column, edge_column),
        [vm((CH, D), bf16), vm((CH, D), bf16), vm((O // 32, 2, 16, D), bf16)],
        grid=(3,), us=8,
    )(side, dc, da, o_r, zl, gate, gp, E)
    dg_b, dg_a = halo(fe, le)

    dqkv = call(
        bind(attend_back_kernel, lh, U), "attend_back",
        sds((nh, micro, F, W), bf16),
        [SMEM, qkv_spec, whole((S, HD)), whole((S, HD)), o_spec, l_spec, o_spec],
        qkv_spec,
        [head_buf] * 4 + [vm((lh, HD, S), bf16)] * 2 + [vm((lh, S, HD), f32)] + [vm((lh, HD, S), f32)] * 2,
        grid=(micro,), us=1,
    )(meta, qkv_r, cos, sin, o_own, logs, do_r)
    dgate, dqkv, dg_b, dg_a = lax.optimization_barrier((dgate, dqkv, dg_b, dg_a))
    dqkv_r = exchange(dqkv.reshape(nh, T, W))

    dup_r, gate_sums, dgain_gate = call(
        bind(gate_back_kernel, micro, F, U), "gate_back",
        (rows(CH, bf16), sds(gate_taps.shape, f32), sds((1, CH), f32)),
        [
            SMEM, full(CH), edge_spec(CH), edge_spec(CH), full(CH), full(128), whole((1, CH)), whole(gate_taps.shape),
            pl.BlockSpec((T, CH), lambda *_: (0, 1)),
        ],
        (full(CH), whole(gate_taps.shape), whole((1, CH))),
        [buf, buf, buf, vm((T, CH), f32)],
        us=1,
    )(meta, dgate, dg_b, dg_a, gn, rs, gate_gain, gate_taps, gp)

    dup_r, dqkv_r = lax.optimization_barrier((dup_r, dqkv_r))
    dml, *d_up, dgain3 = call(
        up_back_kernel, "up_back",
        (rows(D, f32), half(96), half(96), sds((1, D), f32)),
        [
            SMEM, full(D), full(D), whole((8, D)),
            pl.BlockSpec((T, D), lambda j: (0, jnp.minimum(j, 2))),
            pl.BlockSpec((T, D), lambda j: (0, jnp.maximum(j - 3, 0))),
            columns_spec("gated_up", same),
        ],
        (full(D), half_columns, half_columns, whole((1, D))),
        [vm((D, T), bf16), vm((T, D), f32), columns_pair],
        grid=(6,), us=1,
    )(side, mid1, dmid2, gains, dup_l, dup_r, E)

    middle = Exchange([(("gated_up",), d_up), (("output_projection", "gated_down"), d_down)], devices)
    middle.pair()
    dml, middle.lanes, early = lax.optimization_barrier((dml, middle.lanes, early))

    dx, d_head_k, d_head_s, d_in_k, d_in_s, d_out_k, d_out_s, dgain1 = call(
        first_back_kernel, "first_back",
        (
            rows(D, f32), half(48), half(48), half(64), half(64), half(64), half(64), sds((8, D), f32),
        ),
        [
            SMEM, full(D), full(D), full(D), whole((nh, T, W)), whole((8, D)),
            whole((3, D, D)), square, square,
        ],
        (
            full(D), whole((GROUP // 2, 48, D)), whole((GROUP // 2, 48, D)),
            half_columns, half_columns, half_rows, half_rows, whole((8, D)),
        ),
        [
            vm((T, 3 * D), bf16), vm((T, D), bf16), vm((D, T), bf16), vm((T, D), f32), vm((T, D), bf16), vm((T, D), f32),
            columns_pair, rows_pair,
        ],
        grid=(nb,), us=1,
    )(side, x, mid1, dml, dqkv_r, gains, head, first_in, first_out)

    grads = {
        "gain_first": dgain1[0],
        "gain_attend": dgain1[1],
        "gain_gated": dgain3[0],
        "gain_second": dgain2[0],
        "gain_final": dgain2[1],
        "gain_gate": dgain_gate[0],
        "kernel_gate": tap_unlayout(gate_sums, CH),
        "kernel_merge": tap_unlayout(merge_sums, 2 * D),
    }
    tiny = [grads[n].reshape(devices, -1) for n in GAINS]
    for n in KERNELS:
        cols = grads[n].shape[1] // devices
        tiny.append(grads[n].reshape(KER, devices, cols).transpose(1, 0, 2).reshape(devices, -1))
    tiny = jnp.concatenate(tiny, axis=1).astype(bf16)
    tiny_rows = SIZE["tiny"] * GROUP // devices
    tiny = jnp.pad(tiny, ((0, 0), (0, tiny_rows * D - tiny.shape[1]))).reshape(devices, tiny_rows, D)
    late = Exchange(
        [
            (("head_projection",), (d_head_k, d_head_s)), (("first_in",), (d_in_k, d_in_s)),
            (("first_out",), (d_out_k, d_out_s)), (("tiny",), tiny),
        ],
        devices,
    )
    middle.step()
    late.sent, middle.lanes = lax.optimization_barrier((late.sent, middle.lanes))
    middle.step()
    late.pair()
    late.lanes, middle.lanes = lax.optimization_barrier((late.lanes, middle.lanes))
    late.step()
    while middle.orders[0]:
        middle.step()
    late.lanes, middle.lanes = lax.optimization_barrier((late.lanes, middle.lanes))
    late = late.finish()
    middle = middle.finish()
    early = split_rows(early, EARLY, devices)
    shares = {**early, **middle, **late}
    flat = shares["tiny"].reshape(-1)
    at = 0
    for n in GAINS + KERNELS:
        size = shards[n].size
        shares[n] = flat[at : at + size].reshape(shards[n].shape)
        at += size
    return (
        out_rows.reshape(micro, 1, F, D),
        dx.reshape(micro, 1, F, D),
        *(shares[n] for n in ORDER),
    )


def solution(mesh):
    split = P(AXES)
    split_rows = P(AXES, None)
    split_columns = P(None, AXES)
    spec = {n: split if n in GAINS else split_columns if n in KERNELS else split_rows for n in ORDER}
    weight_specs = tuple(spec[n] for n in ORDER)
    frame_spec = P(None, "seq", "head", None)
    return jax.shard_map(
        on_device,
        mesh=mesh,
        in_specs=(frame_spec, frame_spec, P(None, "seq", None)) + weight_specs,
        out_specs=(frame_spec, frame_spec) + weight_specs,
        check_vma=False,
    )
```

```python
import math

import jax
import jax.numpy as jnp
import numpy as np
from jax import lax
from jax.experimental import pallas as pl
from jax.experimental.pallas import tpu as pltpu
from jax.sharding import PartitionSpec as P

D = 512
HD = 64
KER = 31
GAP = 15
PAD = 16
EPSILON = 1e-05
AXES = ("head", "seq")
GROUP = 32
f32 = jnp.float32
bf16 = jnp.bfloat16

PACKS = {
    "a": (("head_projection", 48, 3), ("first_in", 64, 4)),
    "b": (("first_out", 64, 1), ("tiny", 16, 1)),
    "rest": (("gated_up", 96, 6), ("gated_down", 48, 1), ("output_projection", 16, 1), ("merge_weight", 32, 1)),
    "last": (("second_in", 64, 4), ("second_out", 64, 1)),
}
OFFSET = {}
SIZE = {}
BLOCKS = {}
for _pack in PACKS.values():
    _at = 0
    for _name, _rows, _blocks in _pack:
        OFFSET[_name], SIZE[_name], BLOCKS[_name] = _at, _rows, _blocks
        _at += _rows

ORDER = (
    "gain_first",
    "first_in",
    "first_out",
    "gain_attend",
    "head_projection",
    "output_projection",
    "gain_gated",
    "gated_up",
    "gain_gate",
    "kernel_gate",
    "gated_down",
    "kernel_merge",
    "merge_weight",
    "gain_second",
    "second_in",
    "second_out",
    "gain_final",
)
GAINS = ("gain_first", "gain_attend", "gain_gated", "gain_second", "gain_final", "gain_gate")
KERNELS = ("kernel_gate", "kernel_merge")


def mm(a, b):
    return jnp.dot(a, b, preferred_element_type=f32)


def mt(a, b):
    return lax.dot_general(a, b, (((1,), (1,)), ((), ())), preferred_element_type=f32)


def tm(a, b):
    return lax.dot_general(a, b, (((0,), (0,)), ((), ())), preferred_element_type=f32)


def norm(v):
    centre = v - jnp.mean(v, axis=-1, keepdims=True)
    scaling = lax.rsqrt(jnp.mean(centre * centre, axis=-1, keepdims=True) + EPSILON)
    return centre * scaling, scaling


def norm_back(vh, scaling, gain, dz):
    t = dz * gain
    dv = scaling * (
        t - jnp.mean(t, axis=-1, keepdims=True) - vh * jnp.mean(t * vh, axis=-1, keepdims=True)
    )
    return dv, jnp.sum(dz * vh, axis=0, keepdims=True)


def sigmoid(v):
    return 0.5 * jnp.tanh(0.5 * v) + 0.5


def call(kernel, name, out_shape, in_specs, out_specs, scratch=(), grid=(1,), us=10, aliases=None):
    return pl.pallas_call(
        kernel,
        name=name,
        out_shape=out_shape,
        grid=grid,
        in_specs=in_specs,
        out_specs=out_specs,
        scratch_shapes=list(scratch),
        input_output_aliases=aliases or {},
        compiler_params=pltpu.CompilerParams(
            vmem_limit_bytes=60 << 20, dimension_semantics=("arbitrary",) * len(grid)
        ),
        cost_estimate=pl.CostEstimate(
            flops=int(us * 5e8), bytes_accessed=int(us * 2.5e6), transcendentals=0
        ),
    )


def whole(shape):
    zeros = (0,) * len(shape)
    return pl.BlockSpec(shape, lambda *_: zeros)


SMEM = pl.BlockSpec(memory_space=pltpu.SMEM)


def columns_spec(name, pick, part=1):
    base = OFFSET[name] // 16
    return pl.BlockSpec((GROUP // part, 16, D), lambda j: (0, base + pick(j), 0))


def rows_spec(name, pick, part=1):
    rows = SIZE[name]
    base = OFFSET[name] // rows
    return pl.BlockSpec((D // rows // part, rows, D), lambda j: (pick(j), base, 0))


def whole_spec(name, part=1):
    rows = SIZE[name]
    base = OFFSET[name] // rows
    return pl.BlockSpec((GROUP // part, rows, D), lambda *_: (0, base, 0))


def join(side, pair, own, other):
    core = side[0]
    pair[:, pl.ds(core, 1)] = own[:, None]
    pair[:, pl.ds(1 - core, 1)] = other[:, None]
    return pair[...].reshape(D, D)


def part(side, pair, value):
    core = side[0]
    pair[...] = value.astype(bf16).reshape(pair.shape)
    return pair[:, pl.ds(core, 1)][:, 0], pair[:, pl.ds(1 - core, 1)][:, 0]


def sds(shape, dtype):
    return jax.ShapeDtypeStruct(shape, dtype)


def segments_of(meta, m, count, frames):
    base = meta[meta.shape[0] - 1]
    low, high, offset = [], [], []
    start = jnp.int32(0)
    rank = jnp.int32(0)
    before = jnp.int32(0)
    after = jnp.int32(0)
    for s in range(count):
        end = start + meta[m * count + s]
        lo = jnp.clip(start - base, 0, frames)
        hi = jnp.clip(end - base, 0, frames)
        low.append(lo)
        high.append(hi)
        offset.append(PAD + GAP * rank)
        rank = rank + (hi > lo).astype(jnp.int32)
        first = (start <= base) & (base < end)
        before = jnp.where(first, jnp.minimum(base - start, GAP), before)
        final = base + frames - 1
        last = (start <= final) & (final < end)
        after = jnp.where(last, jnp.minimum(end - final - 1, GAP), after)
        start = end
    return low, high, offset, before, after, frames + GAP * (rank - 1)


def clear(buf):
    def body(i, c):
        buf[pl.ds(pl.multiple_of(i * 64, 64), 64), :] = jnp.zeros((64, 128), f32)
        return c

    lax.fori_loop(0, buf.shape[0] // 64, body, 0)


def stage(seg, src, row0, frames, before, after, dst, blocks, sub0):
    low, high, offset, nb, na, length = seg
    for s in range(len(low)):
        lo, hi, off = low[s], high[s], offset[s]

        @pl.when(hi > lo)
        def _():
            def body(g, c):
                r = pl.multiple_of(g * 16, 16)
                for i, cb in enumerate(blocks):
                    x = src[pl.ds(row0 + r, 16), cb * 128 : (cb + 1) * 128].astype(f32)
                    dst[pl.ds((r + off) * 8 + sub0 + i, 16, stride=8), :] = x
                return c

            lax.fori_loop(lo // 16, (hi + 15) // 16, body, 0)

    n = len(blocks)
    for s in range(len(low) - 1):
        lo, hi, off = low[s], high[s], offset[s]

        @pl.when((hi > lo) & (hi < frames))
        def _():
            def body(i, c):
                q = (hi + off + i) * 8
                if n == 8:
                    dst[pl.ds(pl.multiple_of(q, 8), 8), :] = jnp.zeros((8, 128), f32)
                else:
                    dst[pl.ds(q + sub0, n), :] = jnp.zeros((n, 128), f32)
                return c

            lax.fori_loop(0, GAP, body, 0)

    if before is None:
        xb = jnp.zeros((16, 128), f32)
        for i, cb in enumerate(blocks):
            dst[pl.ds(sub0 + i, 16, stride=8), :] = xb
            dst[pl.ds((PAD + length) * 8 + sub0 + i, 16, stride=8), :] = xb
    else:
        rows = lax.broadcasted_iota(jnp.int32, (16, 128), 0)
        kb = rows >= 16 - nb
        ka = rows < na
        for i, cb in enumerate(blocks):
            xb = jnp.where(kb, before[:, cb * 128 : (cb + 1) * 128].astype(f32), 0.0)
            xa = jnp.where(ka, after[:, cb * 128 : (cb + 1) * 128].astype(f32), 0.0)
            dst[pl.ds(sub0 + i, 16, stride=8), :] = xb
            dst[pl.ds((PAD + length) * 8 + sub0 + i, 16, stride=8), :] = xa


def unstage(seg, src, dst, row0, blocks, sub0):
    low, high, offset = seg[:3]
    rows = lax.broadcasted_iota(jnp.int32, (16, 128), 0)
    for s in range(len(low)):
        lo, hi, off = low[s], high[s], offset[s]

        @pl.when(hi > lo)
        def _():
            def body(g, c):
                r = pl.multiple_of(g * 16, 16)
                keep = rows >= lo - r
                for i, cb in enumerate(blocks):
                    value = src[pl.ds((r + off) * 8 + sub0 + i, 16, stride=8), :]
                    at = (pl.ds(row0 + r, 16), slice(cb * 128, (cb + 1) * 128))
                    dst[at] = jnp.where(keep, value, dst[at])
                return c

            lax.fori_loop(lo // 16, (hi + 15) // 16, body, 0)


def convolve(length, taps, buf, out, flip):
    w = [taps[30 - k if flip else k] for k in range(KER)]

    def body(b, c):
        p0 = PAD + b * 8
        acc = [None] * 8
        for j in range(38):
            v = buf[pl.ds(pl.multiple_of((p0 - 15 + j) * 8, 8), 8), :]
            for o in range(8):
                k = j - o
                if 0 <= k < KER:
                    t = w[k] * v
                    acc[o] = t if acc[o] is None else acc[o] + t
        for o in range(8):
            out[pl.ds(pl.multiple_of((p0 + o) * 8, 8), 8), :] = acc[o]
        return c

    lax.fori_loop(0, (length + 7) // 8, body, 0)


def tap_sums(length, vbuf, gbuf):
    def body(b, acc):
        acc = list(acc)
        p0 = PAD + b * 8
        v = [vbuf[pl.ds(pl.multiple_of((p0 + o) * 8, 8), 8), :] for o in range(8)]
        for j in range(38):
            g = gbuf[pl.ds(pl.multiple_of((p0 - 15 + j) * 8, 8), 8), :]
            for o in range(8):
                k = o - j + 30
                if 0 <= k < KER:
                    acc[k] = acc[k] + v[o] * g
        return tuple(acc)

    zero = tuple(jnp.zeros((8, 128), f32) for _ in range(KER))
    return lax.fori_loop(0, (length + 7) // 8, body, zero)


def channel_groups(channels, micro):
    out = []
    for g in range(channels // 1024):
        for m in range(micro):
            out.append((g, tuple(range(8 * g, 8 * g + 8)), ((m, 0),)))
    if channels % 1024:
        blocks = tuple(range(channels // 1024 * 8, channels // 128))
        for m in range(0, micro, 2):
            out.append((channels // 1024, blocks, ((m, 0), (m + 1, 4))))
    return out


def gapped_rows(frames, count):
    return -(-(frames + GAP * (count - 1) + 2 * PAD + 16) // 8) * 8


def tap_layout(kernel):
    channels = kernel.shape[1]
    out = []
    for g in range(channels // 1024):
        out.append(kernel[:, g * 1024 : (g + 1) * 1024].reshape(KER, 8, 128))
    if channels % 1024:
        half = kernel[:, channels // 1024 * 1024 :].reshape(KER, 4, 128)
        out.append(jnp.concatenate([half, half], axis=1))
    return jnp.stack(out).astype(f32)


def tap_unlayout(taps, channels):
    out = [taps[g].reshape(KER, 1024) for g in range(channels // 1024)]
    if channels % 1024:
        out.append((taps[-1][:, :4] + taps[-1][:, 4:]).reshape(KER, 512))
    return jnp.concatenate(out, axis=1)


def put_edges(value, micro, frames, first_ref, last_ref):
    for m in range(micro):
        first_ref[m] = value[m * frames : m * frames + 16]
        last_ref[m] = value[(m + 1) * frames - 16 : (m + 1) * frames]


def first_kernel(
    nh, side, x_ref, gain_ref, wina_ref, winb_ref, wouta_ref, woutb_ref, hpa_ref, hpb_ref,
    mid_ref, qkv_ref, win_ref, wout_ref, hp_ref, n_ref, acc_ref, q_ref, wi_s, wo_s,
):
    j = pl.program_id(0)

    @pl.when(j == 0)
    def _():
        vh, _ = norm(x_ref[...].astype(f32))
        n_ref[...] = (vh * gain_ref[0:1, :]).astype(bf16)
        acc_ref[...] = jnp.zeros_like(acc_ref)

    win = join(side, wi_s, wina_ref[...], winb_ref[...])
    win_ref[0] = win
    p = mm(n_ref[...], win)
    h = (p * sigmoid(p)).astype(bf16)
    wout = join(side, wo_s, wouta_ref[...], woutb_ref[...])
    wout_ref[0] = wout
    acc_ref[...] += mm(h, wout)

    @pl.when(j == pl.num_programs(0) - 1)
    def _():
        mid = x_ref[...].astype(f32) + 0.5 * acc_ref[...]
        mid_ref[...] = mid
        vh, _ = norm(mid)
        n = (vh * gain_ref[1:2, :]).astype(bf16)
        for b in range(3):
            at = slice(16 * b, 16 * b + 16)
            w = join(side, wi_s, hpa_ref[:, at, :], hpb_ref[:, at, :])
            hp_ref[b] = w
            q_ref[:, D * b : D * b + D] = mm(n, w).astype(bf16)
        width = 3 * D // nh
        for i in range(nh):
            qkv_ref[i] = q_ref[:, width * i : width * i + width]


def up_kernel(
    micro, frames, mid_ref, gain_ref, ggate_ref, gu_ref,
    zl_ref, gp_ref, gn_ref, rs_ref, fe_ref, le_ref, n_ref, zr_ref,
):
    j = pl.program_id(0)

    @pl.when(j == 0)
    def _():
        vh, _ = norm(mid_ref[...])
        n_ref[...] = (vh * gain_ref[2:3, :]).astype(bf16)

    up = mm(n_ref[...], gu_ref[...].reshape(D, D))
    phi = 0.5 + 0.5 * lax.erf(up * (1.0 / math.sqrt(2.0)))
    z = up * phi
    slope = phi + up * (jnp.exp(-0.5 * up * up) * (1.0 / math.sqrt(2.0 * math.pi)))
    gp_ref[...] = slope.astype(bf16)

    @pl.when(j < 3)
    def _():
        zl_ref[...] = z.astype(bf16)

    @pl.when(j >= 3)
    def _():
        zr_ref[:, pl.ds(pl.multiple_of((j - 3) * D, D), D)] = z

    @pl.when(j == 5)
    def _():
        vh, r = norm(zr_ref[...])
        gn = (vh * ggate_ref[...]).astype(bf16)
        gn_ref[...] = gn
        rs_ref[...] = jnp.broadcast_to(r, rs_ref.shape)
        put_edges(gn, micro, frames, fe_ref, le_ref)


def swap_halves(v):
    half = v.shape[1] // 2
    return jnp.concatenate([v[:, half:], v[:, :half]], axis=1)


def segment_ids(meta, m, count, shape, axis, start):
    pos = lax.broadcasted_iota(jnp.int32, shape, axis) + start
    ids = jnp.zeros(shape, jnp.int32)
    end = jnp.int32(0)
    for s in range(count - 1):
        end = end + meta[m * count + s]
        ids = ids + (pos >= end).astype(jnp.int32)
    return ids


SCALE = 1.0 / math.sqrt(HD)


def attend_kernel(lh, count, meta, qkv_ref, cos_ref, sin_ref, o_ref, l_ref, q_s, k_s, v_s):
    nh, _, frames, width = qkv_ref.shape
    stream = nh * frames
    m = pl.program_id(0)
    x = qkv_ref[...].reshape(stream, width)
    cos, sin = cos_ref[...], sin_ref[...]
    for h in range(lh):
        c0 = h * 3 * HD
        q = x[:, c0 : c0 + HD].astype(f32)
        k = x[:, c0 + HD : c0 + 2 * HD].astype(f32)
        q_s[h] = (q * cos + swap_halves(q) * sin).astype(bf16)
        k_s[h] = (k * cos + swap_halves(k) * sin).astype(bf16)
        v_s[h] = x[:, c0 + 2 * HD : c0 + 3 * HD]
    key_seg = segment_ids(meta, m, count, (1, stream), 1, 0)

    def body(i, c):
        at = pl.multiple_of(i * frames, frames)
        row_seg = segment_ids(meta, m, count, (frames, 1), 0, at)
        same = row_seg == key_seg
        lane = lax.broadcasted_iota(jnp.int32, (frames, 128), 1)
        pieces = []
        logs = jnp.zeros((frames, 128), f32)
        for h in range(lh):
            s = mt(q_s[h, pl.ds(at, frames), :], k_s[h])
            s = jnp.where(same, s, -1e30)
            peak = jnp.max(s, axis=1, keepdims=True)
            p = jnp.exp((s - peak) * SCALE)
            total = jnp.sum(p, axis=1, keepdims=True)
            o = mm(p.astype(bf16), v_s[h]) / total
            pieces.append(o)
            logs = jnp.where(lane == h, peak * SCALE + jnp.log(total), logs)
        o_ref[i, 0] = jnp.concatenate(pieces, axis=1).astype(bf16) if lh > 1 else pieces[0].astype(bf16)
        l_ref[0, pl.ds(at, frames), :] = logs
        return c

    lax.fori_loop(0, nh, body, 0)


def attend_back_kernel(
    lh, count, meta, qkv_ref, cos_ref, sin_ref, o_ref, l_ref, do_ref, d_ref,
    q_s, k_s, v_s, do_s, qt_s, dot_s, dq_s, dk_s, dv_s,
):
    nh, _, frames, width = qkv_ref.shape
    stream = nh * frames
    m = pl.program_id(0)
    x = qkv_ref[...].reshape(stream, width)
    do = do_ref[...].reshape(stream, lh * HD)
    cos, sin = cos_ref[...], sin_ref[...]
    for h in range(lh):
        c0 = h * 3 * HD
        q = x[:, c0 : c0 + HD].astype(f32)
        k = x[:, c0 + HD : c0 + 2 * HD].astype(f32)
        q = q * cos + swap_halves(q) * sin
        q_s[h] = q.astype(bf16)
        qt_s[h] = q.T.astype(bf16)
        k_s[h] = (k * cos + swap_halves(k) * sin).astype(bf16)
        v_s[h] = x[:, c0 + 2 * HD : c0 + 3 * HD]
        piece = do[:, h * HD : (h + 1) * HD]
        do_s[h] = piece
        dot_s[h] = piece.astype(f32).T.astype(bf16)
    dk_s[...] = jnp.zeros_like(dk_s)
    dv_s[...] = jnp.zeros_like(dv_s)
    key_seg = segment_ids(meta, m, count, (1, stream), 1, 0)

    def body(i, c):
        at = pl.multiple_of(i * frames, frames)
        row_seg = segment_ids(meta, m, count, (frames, 1), 0, at)
        same = row_seg == key_seg
        lane = lax.broadcasted_iota(jnp.int32, (frames, 128), 1)
        logs = l_ref[0, pl.ds(at, frames), :]
        o = o_ref[i, 0].astype(f32)
        for h in range(lh):
            log = jnp.sum(jnp.where(lane == h, logs, 0.0), axis=1, keepdims=True)
            dh = do_s[h, pl.ds(at, frames), :]
            delta = jnp.sum(o[:, h * HD : (h + 1) * HD] * dh.astype(f32), axis=1, keepdims=True)
            s = mt(q_s[h, pl.ds(at, frames), :], k_s[h])
            p = jnp.where(same, jnp.exp(s * SCALE - log), 0.0)
            dp = mt(dh, v_s[h])
            dr = (p * (dp - delta)).astype(bf16)
            dq_s[h, pl.ds(at, frames), :] = mm(dr, k_s[h]) * SCALE
            dk_s[h] += mm(qt_s[h, :, pl.ds(at, frames)], dr)
            dv_s[h] += mm(dot_s[h, :, pl.ds(at, frames)], p.astype(bf16))
        return c

    lax.fori_loop(0, nh, body, 0)
    pieces = []
    for h in range(lh):
        dq = dq_s[h]
        dk = dk_s[h].T * SCALE
        pieces.append(dq * cos - swap_halves(dq) * sin)
        pieces.append(dk * cos - swap_halves(dk) * sin)
        pieces.append(dv_s[h].T)
    full = jnp.concatenate(pieces, axis=1).astype(bf16)
    for i in range(nh):
        d_ref[i, 0] = full[i * frames : (i + 1) * frames]


def gate_kernel(micro, frames, count, meta, gn_ref, hb_ref, ha_ref, zl_ref, wk_ref, gd_ref, gate_ref, c_ref, buf, res, out):
    segs = [segments_of(meta, m, count, frames) for m in range(micro)]
    clear(buf)
    for g, blocks, members in channel_groups(gn_ref.shape[1], micro):
        length = segs[members[0][0]][5]
        for m, sub in members:
            stage(segs[m], gn_ref, m * frames, frames, hb_ref.at[m], ha_ref.at[m], buf, blocks, sub)
            length = jnp.maximum(length, segs[m][5])
        convolve(length, wk_ref.at[g], buf, res, False)
        for m, sub in members:
            unstage(segs[m], res, out, m * frames, blocks, sub)
    gd = gd_ref[...].reshape(gn_ref.shape[1], D)
    for m in range(micro):
        at = slice(m * frames, (m + 1) * frames)
        gate = out[at, :]
        gate_ref[at, :] = gate.astype(bf16)
        u = (zl_ref[at, :].astype(f32) * gate).astype(bf16)
        c_ref[at, :] = mm(u, gd).astype(bf16)


def join_kernel(micro, frames, o_ref, c_ref, op_ref, jn_ref, fe_ref, le_ref):
    nh = o_ref.shape[0]
    o = jnp.concatenate([o_ref[i] for i in range(nh)], axis=1)
    a = mm(o, op_ref[...].reshape(D, D)).astype(bf16)
    jn_ref[:, :D] = a
    jn_ref[:, D:] = c_ref[...]
    for m in range(micro):
        first = slice(m * frames, m * frames + 16)
        last = slice((m + 1) * frames - 16, (m + 1) * frames)
        fe_ref[m, :, :D] = a[first]
        fe_ref[m, :, D:] = c_ref[first, :]
        le_ref[m, :, :D] = a[last]
        le_ref[m, :, D:] = c_ref[last, :]


def merge_kernel(micro, frames, count, meta, jn_ref, hb_ref, ha_ref, wk_ref, mw_ref, mid_ref, m_ref, mid2_ref, buf, res, out):
    segs = [segments_of(meta, m, count, frames) for m in range(micro)]
    clear(buf)
    for g, blocks, members in channel_groups(jn_ref.shape[1], micro):
        m = members[0][0]
        stage(segs[m], jn_ref, m * frames, frames, hb_ref.at[m], ha_ref.at[m], buf, blocks, 0)
        convolve(segs[m][5], wk_ref.at[g], buf, res, False)
        unstage(segs[m], res, out, m * frames, blocks, 0)
    mw = mw_ref[...].reshape(2 * D, D)
    for m in range(micro):
        at = slice(m * frames, (m + 1) * frames)
        mixed = (jn_ref[at, :].astype(f32) + out[at, :]).astype(bf16)
        m_ref[at, :] = mixed
        mid2_ref[at, :] = mid_ref[at, :] + mm(mixed, mw)


def silu_back(p, dh):
    s = sigmoid(p)
    return (p * s).astype(bf16), (s * (1.0 + p * (1.0 - s)) * dh).astype(bf16)


def second_kernel(
    micro, frames, mid2_ref, cot_ref, gain_ref, win_ref, wout_ref, mw_ref, mixed_ref,
    out_ref, dmid2_ref, dm_ref, fe_ref, le_ref, dw_ref, dgain_ref,
    n_ref, nt_ref, p_ref, acc_ref, dmid3_ref, df_ref,
):
    j = pl.program_id(0)
    nb = pl.num_programs(0) // 2

    @pl.when(j == 0)
    def _():
        vh, _ = norm(mid2_ref[...])
        n = vh * gain_ref[3:4, :]
        n_ref[...] = n.astype(bf16)
        nt_ref[...] = n.T.astype(bf16)
        acc_ref[...] = jnp.zeros_like(acc_ref)

    @pl.when(j < nb)
    def _():
        p = mm(n_ref[...], win_ref[...].reshape(D, D))
        p_ref[j] = p
        h = (p * sigmoid(p)).astype(bf16)
        acc_ref[...] += mm(h, wout_ref[...].reshape(D, D))

    @pl.when(j == nb - 1)
    def _():
        mid3 = mid2_ref[...] + 0.5 * acc_ref[...]
        vh, r = norm(mid3)
        gain = gain_ref[4:5, :]
        out_ref[...] = (vh * gain).astype(bf16)
        dmid3, dgain = norm_back(vh, r, gain, cot_ref[...].astype(f32))
        dgain_ref[1:2, :] = dgain
        dmid3_ref[...] = dmid3
        df_ref[...] = (0.5 * dmid3).astype(bf16)
        acc_ref[...] = jnp.zeros_like(acc_ref)

    @pl.when(j >= nb)
    def _():
        win = win_ref[...].reshape(D, D)
        dh = mt(df_ref[...], wout_ref[...].reshape(D, D))
        h, dp = silu_back(p_ref[2 * nb - 1 - j], dh)
        at = 2 * nb - 1 - j
        few = D // 64
        dw_ref[pl.ds(at * few, few), 64:128, :] = tm(h, df_ref[...]).astype(bf16).reshape(few, 64, D)
        dw_ref[:, pl.ds(pl.multiple_of(at * 16, 16), 16), :] = mm(nt_ref[...], dp).astype(bf16).reshape(GROUP, 16, D)
        acc_ref[...] += mt(dp, win)

    @pl.when(j == 2 * nb - 1)
    def _():
        vh, r = norm(mid2_ref[...])
        dv, dgain = norm_back(vh, r, gain_ref[3:4, :], acc_ref[...])
        dgain_ref[0:1, :] = dgain
        dmid2 = dmid3_ref[...] + dv
        dmid2_ref[...] = dmid2
        dmg = dmid2.astype(bf16)
        dw_ref[:, 128:, :] = tm(mixed_ref[...], dmg).astype(bf16).reshape(GROUP, 32, D)
        dm = mt(dmg, mw_ref[...].reshape(2 * D, D)).astype(bf16)
        dm_ref[...] = dm
        put_edges(dm, micro, frames, fe_ref, le_ref)


def merge_back_kernel(
    micro, frames, count, meta, dm_ref, hb_ref, ha_ref, jn_ref, wk_ref, op_ref,
    da_ref, dc_ref, do_ref, dk_ref, buf, vbuf, res, out,
):
    segs = [segments_of(meta, m, count, frames) for m in range(micro)]
    clear(buf)
    clear(vbuf)
    total = [None] * KER
    for g, blocks, members in channel_groups(dm_ref.shape[1], micro):
        m = members[0][0]
        stage(segs[m], dm_ref, m * frames, frames, hb_ref.at[m], ha_ref.at[m], buf, blocks, 0)
        stage(segs[m], jn_ref, m * frames, frames, None, None, vbuf, blocks, 0)
        convolve(segs[m][5], wk_ref.at[g], buf, res, True)
        sums = tap_sums(segs[m][5], vbuf, buf)
        for k in range(KER):
            dk_ref[g, k] = sums[k] if m == 0 else dk_ref[g, k] + sums[k]
        unstage(segs[m], res, out, m * frames, blocks, 0)
    nh = do_ref.shape[0]
    width = D // nh
    for m in range(micro):
        at = slice(m * frames, (m + 1) * frames)
        djn = dm_ref[at, :].astype(f32) + out[at, :]
        da = djn[:, :D].astype(bf16)
        da_ref[at, :] = da
        dc_ref[at, :] = djn[:, D:].astype(bf16)
        do = mt(da, op_ref[...].reshape(D, D)).astype(bf16)
        for i in range(nh):
            do_ref[i, at, :] = do[:, i * width : (i + 1) * width]


def gate_pre_kernel(
    micro, frames, side, dc_ref, da_ref, o_ref, zl_ref, gate_ref, gp_ref, gd_ref,
    kept_ref, sent_ref, dup_ref, dgate_ref, fe_ref, le_ref, gd_s, dgd_s, dop_s,
):
    j = pl.program_id(0)

    @pl.when(j == 0)
    def _():
        gd_s[...] = gd_ref[...].reshape(gd_s.shape)
        width = o_ref.shape[2]
        for i in range(o_ref.shape[0]):
            few = width // 32
            at = slice(i * few, (i + 1) * few)
            kept_ref[at, :16, :], sent_ref[at, :16, :] = part(side, dop_s, tm(o_ref[i], da_ref[...]))

    du = mt(dc_ref[...], gd_s[pl.ds(pl.multiple_of(j * D, D), D), :])
    gate = gate_ref[...].astype(f32)
    left = zl_ref[...].astype(f32)
    u = (left * gate).astype(bf16)
    dgd_s[pl.ds(pl.multiple_of(j * D, D), D), :] = tm(u, dc_ref[...]).astype(bf16)

    @pl.when(j == pl.num_programs(0) - 1)
    def _():
        for i in range(GROUP // 2):
            for ref, core in ((kept_ref, side[0]), (sent_ref, 1 - side[0])):
                ref[i, 16:, :] = dgd_s[pl.ds(pl.multiple_of((2 * i + core) * 48, 16), 48), :]

    dup_ref[...] = (gp_ref[...].astype(f32) * (du * gate)).astype(bf16)
    dgate = (du * left).astype(bf16)
    dgate_ref[...] = dgate
    put_edges(dgate, micro, frames, fe_ref, le_ref)


def gate_back_kernel(
    micro, frames, count, meta, dg_ref, hb_ref, ha_ref, gn_ref, rs_ref, ggate_ref, wk_ref, gp_ref,
    dup_ref, dk_ref, dgain_ref, buf, vbuf, res, out,
):
    segs = [segments_of(meta, m, count, frames) for m in range(micro)]
    clear(buf)
    clear(vbuf)
    seen = set()
    for g, blocks, members in channel_groups(dg_ref.shape[1], micro):
        length = segs[members[0][0]][5]
        if len(members) > 1:
            clear(buf)
            clear(vbuf)
        for m, sub in members:
            stage(segs[m], dg_ref, m * frames, frames, hb_ref.at[m], ha_ref.at[m], buf, blocks, sub)
            stage(segs[m], gn_ref, m * frames, frames, None, None, vbuf, blocks, sub)
            length = jnp.maximum(length, segs[m][5])
        convolve(length, wk_ref.at[g], buf, res, True)
        sums = tap_sums(length, vbuf, buf)
        for k in range(KER):
            dk_ref[g, k] = dk_ref[g, k] + sums[k] if g in seen else sums[k]
        seen.add(g)
        for m, sub in members:
            unstage(segs[m], res, out, m * frames, blocks, sub)
    gain = ggate_ref[...]
    inverse = 1.0 / gain
    for m in range(micro):
        at = slice(m * frames, (m + 1) * frames)
        vh = gn_ref[at, :].astype(f32) * inverse
        dv, dgain = norm_back(vh, rs_ref[at, 0:1], gain, out[at, :])
        dgain_ref[...] = dgain if m == 0 else dgain_ref[...] + dgain
        dup_ref[at, :] = (gp_ref[at, :].astype(f32) * dv).astype(bf16)


def up_back_kernel(
    side, mid_ref, dmid2_ref, gain_ref, dl_ref, dr_ref, gu_ref,
    dmid_ref, kept_ref, sent_ref, dgain_ref, nt_ref, acc_ref, pair_s,
):
    j = pl.program_id(0)

    @pl.when(j == 0)
    def _():
        vh, _ = norm(mid_ref[...])
        nt_ref[...] = (vh * gain_ref[2:3, :]).T.astype(bf16)
        acc_ref[...] = jnp.zeros_like(acc_ref)

    dup = jnp.where(j < 3, dl_ref[...], dr_ref[...])
    kept_ref[...], sent_ref[...] = part(side, pair_s, mm(nt_ref[...], dup))
    acc_ref[...] += mt(dup, gu_ref[...].reshape(D, D))

    @pl.when(j == pl.num_programs(0) - 1)
    def _():
        vh, r = norm(mid_ref[...])
        dv, dgain = norm_back(vh, r, gain_ref[2:3, :], acc_ref[...])
        dgain_ref[...] = dgain
        dmid_ref[...] = dmid2_ref[...] + dv


def first_back_kernel(
    side, x_ref, mid_ref, dml_ref, dq_ref, gain_ref, hp_ref, win_ref, wout_ref,
    dx_ref, dhpk_ref, dhps_ref, dwik_ref, dwis_ref, dwok_ref, dwos_ref, dgain_ref,
    dq_s, n_ref, nt_ref, dmid_ref, df_ref, acc_ref, pi_s, po_s,
):
    j = pl.program_id(0)

    @pl.when(j == 0)
    def _():
        nh, _, width = dq_ref.shape
        for i in range(nh):
            dq_s[:, i * width : (i + 1) * width] = dq_ref[i]
        vh, r = norm(mid_ref[...])
        gain = gain_ref[1:2, :]
        nt = (vh * gain).T.astype(bf16)
        dn = None
        for b in range(3):
            dq = dq_s[:, b * D : (b + 1) * D]
            at = slice(16 * b, 16 * b + 16)
            dhpk_ref[:, at, :], dhps_ref[:, at, :] = part(side, pi_s, mm(nt, dq))
            t = mt(dq, hp_ref[b])
            dn = t if dn is None else dn + t
        dv, dgain = norm_back(vh, r, gain, dn)
        dgain_ref[1:2, :] = dgain
        dmid = dml_ref[...] + dv
        dmid_ref[...] = dmid
        df_ref[...] = (0.5 * dmid).astype(bf16)
        vh, _ = norm(x_ref[...].astype(f32))
        n = vh * gain_ref[0:1, :]
        n_ref[...] = n.astype(bf16)
        nt_ref[...] = n.T.astype(bf16)
        acc_ref[...] = jnp.zeros_like(acc_ref)

    win = win_ref[0]
    p = mm(n_ref[...], win)
    dh = mt(df_ref[...], wout_ref[0])
    h, dp = silu_back(p, dh)
    dwok_ref[...], dwos_ref[...] = part(side, po_s, tm(h, df_ref[...]))
    dwik_ref[...], dwis_ref[...] = part(side, pi_s, mm(nt_ref[...], dp))
    acc_ref[...] += mt(dp, win)

    @pl.when(j == pl.num_programs(0) - 1)
    def _():
        vh, r = norm(x_ref[...].astype(f32))
        dv, dgain = norm_back(vh, r, gain_ref[0:1, :], acc_ref[...])
        dgain_ref[0:1, :] = dgain
        dx_ref[...] = dmid_ref[...] + dv


def to_rows(shard):
    rows, cols = shard.shape
    if cols == D:
        return shard
    return shard.reshape(rows, cols // D, D).transpose(1, 0, 2).reshape(rows * cols // D, D)


def canonical(part, name):
    count = part.shape[0]
    q = count // GROUP
    if q == 1:
        return part
    blocks = BLOCKS[name]
    rows = part.shape[1] // blocks
    part = part.reshape(GROUP, q, blocks, rows, D).transpose(0, 2, 1, 3, 4)
    return part.reshape(GROUP, blocks * q * rows, D)


def by_device(part, name, count):
    q = count // GROUP
    if q == 1:
        return part
    blocks = BLOCKS[name]
    rows = part.shape[1] // blocks // q
    part = part.reshape(GROUP, blocks, q, rows, D).transpose(0, 2, 1, 3, 4)
    return part.reshape(count, blocks * rows, D)


def bit_of(index, bit):
    return (index >> bit) & 1


def swap(v, bit, count):
    return lax.ppermute(v, AXES, [(i, i ^ (1 << bit)) for i in range(count)])


def exchange_gather(shards, count, waiting):
    me = lax.axis_index(AXES)
    bits = count.bit_length() - 1
    top, rest = [bits - 2, bits - 1], list(range(1, bits - 2))
    out = []
    for v, order in zip(shards, (rest[::-1] + top, rest[::-1] + top[::-1])):
        held = []
        for bit in order:
            other = swap(v, bit, count)
            mine = bit_of(me, bit) == 1
            held = sorted(held + [bit], reverse=True)
            if waiting is not None and not out:
                other, waiting = lax.optimization_barrier((other, waiting))
                released, waiting = waiting, None
            v = jnp.stack([jnp.where(mine, other, v), jnp.where(mine, v, other)], axis=held.index(bit))
        v = v.reshape((count // 2,) + v.shape[-2:])
        out.append((v, swap(v, 0, count)))
    return out, released


def whole_pack(own, other):
    mine = bit_of(lax.axis_index(AXES), 0) == 1
    both = jnp.stack([jnp.where(mine, other, own), jnp.where(mine, own, other)], axis=1)
    return both.reshape((-1,) + own.shape[1:])


def unpack(raw, pack):
    q = raw.shape[0] // GROUP
    if q == 1:
        return raw
    return jnp.concatenate(
        [canonical(raw[:, OFFSET[n] // q : (OFFSET[n] + SIZE[n]) // q], n) for n, r, b in PACKS[pack]], axis=1
    )


def gather_weights(shards, count):
    q = count // GROUP
    tiny = jnp.concatenate([shards[n].reshape(-1) for n in GAINS + KERNELS])
    tiny = jnp.pad(tiny, (0, SIZE["tiny"] // q * D - tiny.shape[0])).reshape(-1, D)
    rows = {n: tiny if n == "tiny" else to_rows(shards[n]) for n in SIZE}
    packed = {k: jnp.concatenate([rows[n] for n, r, b in pack], axis=0) for k, pack in PACKS.items()}
    pairs, released = exchange_gather([packed["a"], packed["b"]], count, packed["rest"])
    pairs = dict(zip("ab", pairs))
    raw = {"rest": lax.all_gather(released, AXES, axis=0, tiled=False)}
    full = {"rest": unpack(raw["rest"], "rest"), "last": packed["last"]}
    for k in pairs:
        if q == 1:
            full[k] = pairs[k]
        else:
            v = unpack(whole_pack(*pairs[k]), k)
            full[k] = (v[0::2], v[1::2])
    tiny = whole_pack(*(v[:, OFFSET["tiny"] // q :] for v in pairs["b"])).reshape(count, -1)
    unit = shards["gain_first"].shape[0]
    gains = tiny[:, : 5 * unit].astype(f32).reshape(count, 5, unit).transpose(1, 0, 2).reshape(5, D)
    gains = jnp.pad(gains, ((0, 3), (0, 0)))
    at = 5 * unit
    size = shards["gain_gate"].shape[0]
    gate_gain = tiny[:, at : at + size].astype(f32).reshape(1, -1)
    at += size
    kernels = []
    for n in KERNELS:
        taps, cols = shards[n].shape
        part = tiny[:, at : at + taps * cols].reshape(count, taps, cols)
        kernels.append(tap_layout(part.transpose(1, 0, 2).reshape(taps, count * cols)))
        at += taps * cols
    return full, gains, gate_gain, kernels


class Exchange:
    def __init__(self, pieces, count):
        self.count = count
        self.names = [n for names, _ in pieces for n in names]
        self.me = lax.axis_index(AXES)
        self.bits = count.bit_length() - 1
        core = bit_of(self.me, 0)
        self.kept, self.sent = [], []
        for names, arrays in pieces:
            if names == ("tiny",):
                arrays = [arrays]
            elif count == GROUP:
                self.kept.append(arrays[0])
                self.sent.append(arrays[1])
                continue
            else:
                packed = jnp.stack(arrays, axis=1).reshape(GROUP, -1, D)
                arrays = [by_pieces(packed, names, count)]
            for p in arrays:
                p = p.reshape(count // 2, 2, p.shape[1], D)
                self.kept.append(self.pick(p, 1, core))
                self.sent.append(self.pick(p, 1, 1 - core))

    def pick(self, v, axis, at):
        return lax.dynamic_index_in_dim(v, at, axis, keepdims=False)

    def pair(self):
        sums = [p + swap(v, 0, self.count) for p, v in zip(self.kept, self.sent)]
        at = sum(p.shape[1] for p in sums)
        half = at // 2 // 16 * 16
        rows = jnp.concatenate(sums, axis=1)
        top, rest = [self.bits - 2, self.bits - 1], list(range(1, self.bits - 2))
        self.orders = [top + rest, top[::-1] + rest]
        self.left = [list(range(self.bits - 1, 0, -1)) for _ in range(2)]
        self.lanes = [
            v.reshape((2,) * (self.bits - 1) + v.shape[1:]) for v in (rows[:, :half], rows[:, half:])
        ]

    def step(self):
        for i in range(2):
            bit = self.orders[i].pop(0)
            axis = self.left[i].index(bit)
            self.left[i].remove(bit)
            mine = bit_of(self.me, bit)
            v = self.lanes[i]
            self.lanes[i] = self.pick(v, axis, mine) + swap(self.pick(v, axis, 1 - mine), bit, self.count)

    def finish(self):
        while self.orders[0]:
            self.step()
        return split_rows(jnp.concatenate(self.lanes, axis=0), self.names, self.count)


def split_rows(got, names, count):
    q = count // GROUP
    out = {}
    at = 0
    for n in names:
        size = SIZE[n] // q
        part = got[at : at + size].astype(f32)
        at += size
        if n != "tiny":
            blocks = BLOCKS[n]
            rows = part.shape[0] // blocks
            part = part.reshape(blocks, rows, D).transpose(1, 0, 2).reshape(rows, blocks * D)
        out[n] = part
    return out


EARLY = ("second_in", "second_out", "merge_weight")


def by_pieces(packed, names, count):
    if count == GROUP:
        return packed
    parts = []
    at = 0
    for n in names:
        parts.append(by_device(packed[:, at : at + SIZE[n]], n, count))
        at += SIZE[n]
    if at < packed.shape[1]:
        parts.append(packed[:, at:].reshape(count, -1, D))
    return jnp.concatenate(parts, axis=1)


def rope_tables(stream):
    half = HD // 2
    frequency = np.exp(np.arange(half, dtype=np.float32) * np.float32(-math.log(10000.0) / half))
    angles = np.arange(stream, dtype=np.float32)[:, None] * frequency.astype(np.float32)[None, :]
    cos, sin = np.cos(angles), np.sin(angles)
    return (
        jnp.asarray(np.concatenate([cos, cos], axis=1), f32),
        jnp.asarray(np.concatenate([-sin, sin], axis=1), f32),
    )


def on_device(frames, cotangent, lengths, *weights):
    shards = dict(zip(ORDER, weights))
    nh = lax.axis_size("head")
    devices = nh * lax.axis_size("seq")
    micro, _, F, _ = frames.shape
    T = micro * F
    lh = D // HD // nh
    W = 3 * D // nh
    O = lh * HD
    S = nh * F
    U = lengths.shape[2]
    FF = 4 * D
    CH = 3 * D
    meta = jnp.concatenate(
        [lengths.reshape(-1), (lax.axis_index("head") * F).astype(jnp.int32).reshape(1)]
    ).astype(jnp.int32)
    packs, gains, gate_gain, (gate_taps, merge_taps) = gather_weights(shards, devices)
    EA, EB, E = packs["a"], packs["b"], packs["rest"]
    core = lax.axis_index(AXES) & 1 if devices == GROUP else 0
    side = jnp.asarray(core, jnp.int32).reshape(1)
    x = frames.reshape(T, D)
    cot = cotangent.reshape(T, D)
    up = [(i, i + 1) for i in range(nh - 1)]
    down = [(i + 1, i) for i in range(nh - 1)]

    def halo(first, last):
        return lax.ppermute(last, "head", up), lax.ppermute(first, "head", down)

    def exchange(v):
        return lax.all_to_all(v, "head", split_axis=0, concat_axis=0, tiled=True)

    def bind(kernel, *args):
        def bound(*refs):
            return kernel(*args, *refs)

        return bound

    rows = lambda c, d: sds((T, c), d)
    full = lambda c: whole((T, c))
    edge = lambda c: sds((micro, 16, c), bf16)
    edge_spec = lambda c: whole((micro, 16, c))
    vm = pltpu.VMEM
    PR = gapped_rows(F, U)
    buf = vm((PR * 8, 128), f32)
    nb = FF // D
    same = lambda j: j

    first_in_specs = [columns_spec("first_in", same, 2)] * 2
    first_out_specs = [rows_spec("first_out", same, 2)] * 2
    head_specs = [whole_spec("head_projection", 2)] * 2
    columns_pair = vm((GROUP // 2, 2, 16, D), bf16)
    rows_pair = vm((D // 128, 2, 64, D), bf16)
    half_columns = pl.BlockSpec((GROUP // 2, 16, D), lambda j: (0, j, 0))
    half_rows = pl.BlockSpec((D // 128, 64, D), lambda j: (j, 0, 0))
    half = lambda r: sds((GROUP // 2, r, D), bf16)

    square = pl.BlockSpec((1, D, D), lambda j: (j, 0, 0))
    mid1, qkv, first_in, first_out, head = call(
        bind(first_kernel, nh), "first",
        (
            rows(D, f32), sds((nh, T, W), bf16),
            sds((nb, D, D), bf16), sds((nb, D, D), bf16), sds((3, D, D), bf16),
        ),
        [SMEM, full(D), whole((8, D)), *first_in_specs, *first_out_specs, *head_specs],
        (full(D), whole((nh, T, W)), square, square, whole((3, D, D))),
        [vm((T, D), bf16), vm((T, D), f32), vm((T, 3 * D), bf16), columns_pair, rows_pair],
        grid=(nb,), us=8,
    )(side, x, gains, *EA, *EB, *EA)
    qkv_r = exchange(qkv).reshape(nh, micro, F, W)
    mid1, last = lax.optimization_barrier((mid1, packs["last"]))
    EL = unpack(lax.all_gather(last, AXES, axis=0, tiled=False), "last")

    zl, gp, gn, rs, fe, le = call(
        bind(up_kernel, micro, F), "up",
        (rows(CH, bf16), rows(2 * CH, bf16), rows(CH, bf16), rows(128, f32), edge(CH), edge(CH)),
        [full(D), whole((8, D)), whole((1, CH)), columns_spec("gated_up", same)],
        (
            pl.BlockSpec((T, D), lambda j: (0, jnp.minimum(j, 2))),
            pl.BlockSpec((T, D), lambda j: (0, j)),
            full(CH), full(128), edge_spec(CH), edge_spec(CH),
        ),
        [vm((T, D), bf16), vm((T, CH), f32)],
        grid=(6,), us=15,
    )(mid1, gains, gate_gain, E)
    gate_b, gate_a = halo(fe, le)

    cos, sin = rope_tables(S)
    qkv_spec = pl.BlockSpec((nh, 1, F, W), lambda m: (0, m, 0, 0))
    o_spec = pl.BlockSpec((nh, 1, F, O), lambda m: (0, m, 0, 0))
    l_spec = pl.BlockSpec((1, S, 128), lambda m: (m, 0, 0))
    head_buf = vm((lh, S, HD), bf16)
    o_own, logs = call(
        bind(attend_kernel, lh, U), "attend",
        (sds((nh, micro, F, O), bf16), sds((micro, S, 128), f32)),
        [SMEM, qkv_spec, whole((S, HD)), whole((S, HD))],
        (o_spec, l_spec),
        [head_buf] * 3,
        grid=(micro,), us=12,
    )(meta, qkv_r, cos, sin)
    o_r = exchange(o_own.reshape(nh, T, O))

    gate, c = call(
        bind(gate_kernel, micro, F, U), "gate",
        (rows(CH, bf16), rows(D, bf16)),
        [SMEM, full(CH), edge_spec(CH), edge_spec(CH), full(CH), whole(gate_taps.shape), whole_spec("gated_down")],
        (full(CH), full(D)),
        [buf, buf, vm((T, CH), f32)],
        us=18,
    )(meta, gn, gate_b, gate_a, zl, gate_taps, E)

    jn, fe, le = call(
        bind(join_kernel, micro, F), "join",
        (rows(2 * D, bf16), edge(2 * D), edge(2 * D)),
        [whole((nh, T, O)), full(D), whole_spec("output_projection")],
        (full(2 * D), edge_spec(2 * D), edge_spec(2 * D)),
        us=2,
    )(o_r, c, E)
    jn_b, jn_a = halo(fe, le)

    mixed, mid2 = call(
        bind(merge_kernel, micro, F, U), "merge",
        (rows(2 * D, bf16), rows(D, f32)),
        [SMEM, full(2 * D), edge_spec(2 * D), edge_spec(2 * D), whole(merge_taps.shape), whole_spec("merge_weight"), full(D)],
        (full(2 * D), full(D)),
        [buf, buf, vm((T, 2 * D), f32)],
        us=12,
    )(meta, jn, jn_b, jn_a, merge_taps, E, mid1)

    there_back = lambda j: jnp.where(j < nb, j, 2 * nb - 1 - j)
    out_rows, dmid2, dm, fe, le, d_early, dgain2 = call(
        bind(second_kernel, micro, F), "second",
        (
            rows(D, bf16), rows(D, f32), rows(2 * D, bf16), edge(2 * D), edge(2 * D),
            sds((GROUP, 192, D), bf16), sds((8, D), f32),
        ),
        [full(D), full(D), whole((8, D)), columns_spec("second_in", there_back), rows_spec("second_out", there_back), whole_spec("merge_weight"), full(2 * D)],
        (
            full(D), full(D), full(2 * D), edge_spec(2 * D), edge_spec(2 * D),
            whole((GROUP, 160, D)),
            whole((8, D)),
        ),
        [vm((T, D), bf16), vm((D, T), bf16), vm((nb, T, D), f32), vm((T, D), f32), vm((T, D), f32), vm((T, D), bf16)],
        grid=(2 * nb,), us=25,
    )(mid2, cot, gains, EL, EL, E, mixed)
    early = lax.psum_scatter(
        by_pieces(d_early, EARLY, devices).reshape(-1, D), AXES, scatter_dimension=0, tiled=True
    )
    dm_b, dm_a = halo(fe, le)

    da, dc, do, merge_sums = call(
        bind(merge_back_kernel, micro, F, U), "merge_back",
        (rows(D, bf16), rows(D, bf16), sds((nh, T, O), bf16), sds(merge_taps.shape, f32)),
        [SMEM, full(2 * D), edge_spec(2 * D), edge_spec(2 * D), full(2 * D), whole(merge_taps.shape), whole_spec("output_projection")],
        (full(D), full(D), whole((nh, T, O)), whole(merge_taps.shape)),
        [buf, buf, buf, vm((T, 2 * D), f32)],
        us=20,
    )(meta, dm, dm_b, dm_a, jn, merge_taps, E)
    do_r = exchange(do).reshape(nh, micro, F, O)

    column = pl.BlockSpec((T, D), lambda j: (0, j))
    edge_column = pl.BlockSpec((micro, 16, D), lambda j: (0, 0, j))
    *d_down, dup_l, dgate, fe, le = call(
        bind(gate_pre_kernel, micro, F), "gate_pre",
        (half(64), half(64), rows(CH, bf16), rows(CH, bf16), edge(CH), edge(CH)),
        [SMEM, full(D), full(D), whole((nh, T, O)), column, column, column, whole_spec("gated_down")],
        (whole((GROUP // 2, 64, D)), whole((GROUP // 2, 64, D)), column, column, edge_column, edge_column),
        [vm((CH, D), bf16), vm((CH, D), bf16), vm((O // 32, 2, 16, D), bf16)],
        grid=(3,), us=8,
    )(side, dc, da, o_r, zl, gate, gp, E)
    dg_b, dg_a = halo(fe, le)

    dqkv = call(
        bind(attend_back_kernel, lh, U), "attend_back",
        sds((nh, micro, F, W), bf16),
        [SMEM, qkv_spec, whole((S, HD)), whole((S, HD)), o_spec, l_spec, o_spec],
        qkv_spec,
        [head_buf] * 4 + [vm((lh, HD, S), bf16)] * 2 + [vm((lh, S, HD), f32)] + [vm((lh, HD, S), f32)] * 2,
        grid=(micro,), us=1,
    )(meta, qkv_r, cos, sin, o_own, logs, do_r)
    dgate, dqkv, dg_b, dg_a = lax.optimization_barrier((dgate, dqkv, dg_b, dg_a))
    dqkv_r = exchange(dqkv.reshape(nh, T, W))

    dup_r, gate_sums, dgain_gate = call(
        bind(gate_back_kernel, micro, F, U), "gate_back",
        (rows(CH, bf16), sds(gate_taps.shape, f32), sds((1, CH), f32)),
        [
            SMEM, full(CH), edge_spec(CH), edge_spec(CH), full(CH), full(128), whole((1, CH)), whole(gate_taps.shape),
            pl.BlockSpec((T, CH), lambda *_: (0, 1)),
        ],
        (full(CH), whole(gate_taps.shape), whole((1, CH))),
        [buf, buf, buf, vm((T, CH), f32)],
        us=1,
    )(meta, dgate, dg_b, dg_a, gn, rs, gate_gain, gate_taps, gp)

    dup_r, dqkv_r = lax.optimization_barrier((dup_r, dqkv_r))
    dml, *d_up, dgain3 = call(
        up_back_kernel, "up_back",
        (rows(D, f32), half(96), half(96), sds((1, D), f32)),
        [
            SMEM, full(D), full(D), whole((8, D)),
            pl.BlockSpec((T, D), lambda j: (0, jnp.minimum(j, 2))),
            pl.BlockSpec((T, D), lambda j: (0, jnp.maximum(j - 3, 0))),
            columns_spec("gated_up", same),
        ],
        (full(D), half_columns, half_columns, whole((1, D))),
        [vm((D, T), bf16), vm((T, D), f32), columns_pair],
        grid=(6,), us=1,
    )(side, mid1, dmid2, gains, dup_l, dup_r, E)

    middle = Exchange([(("gated_up",), d_up), (("output_projection", "gated_down"), d_down)], devices)
    middle.pair()
    dml, middle.lanes, early = lax.optimization_barrier((dml, middle.lanes, early))

    dx, d_head_k, d_head_s, d_in_k, d_in_s, d_out_k, d_out_s, dgain1 = call(
        first_back_kernel, "first_back",
        (
            rows(D, f32), half(48), half(48), half(64), half(64), half(64), half(64), sds((8, D), f32),
        ),
        [
            SMEM, full(D), full(D), full(D), whole((nh, T, W)), whole((8, D)),
            whole((3, D, D)), square, square,
        ],
        (
            full(D), whole((GROUP // 2, 48, D)), whole((GROUP // 2, 48, D)),
            half_columns, half_columns, half_rows, half_rows, whole((8, D)),
        ),
        [
            vm((T, 3 * D), bf16), vm((T, D), bf16), vm((D, T), bf16), vm((T, D), f32), vm((T, D), bf16), vm((T, D), f32),
            columns_pair, rows_pair,
        ],
        grid=(nb,), us=1,
    )(side, x, mid1, dml, dqkv_r, gains, head, first_in, first_out)

    grads = {
        "gain_first": dgain1[0],
        "gain_attend": dgain1[1],
        "gain_gated": dgain3[0],
        "gain_second": dgain2[0],
        "gain_final": dgain2[1],
        "gain_gate": dgain_gate[0],
        "kernel_gate": tap_unlayout(gate_sums, CH),
        "kernel_merge": tap_unlayout(merge_sums, 2 * D),
    }
    tiny = [grads[n].reshape(devices, -1) for n in GAINS]
    for n in KERNELS:
        cols = grads[n].shape[1] // devices
        tiny.append(grads[n].reshape(KER, devices, cols).transpose(1, 0, 2).reshape(devices, -1))
    tiny = jnp.concatenate(tiny, axis=1).astype(bf16)
    tiny_rows = SIZE["tiny"] * GROUP // devices
    tiny = jnp.pad(tiny, ((0, 0), (0, tiny_rows * D - tiny.shape[1]))).reshape(devices, tiny_rows, D)
    late = Exchange(
        [
            (("head_projection",), (d_head_k, d_head_s)), (("first_in",), (d_in_k, d_in_s)),
            (("first_out",), (d_out_k, d_out_s)), (("tiny",), tiny),
        ],
        devices,
    )
    middle.step()
    late.sent, middle.lanes = lax.optimization_barrier((late.sent, middle.lanes))
    middle.step()
    late.pair()
    late.lanes, middle.lanes = lax.optimization_barrier((late.lanes, middle.lanes))
    late.step()
    while middle.orders[0]:
        middle.step()
    late.lanes, middle.lanes = lax.optimization_barrier((late.lanes, middle.lanes))
    late = late.finish()
    middle = middle.finish()
    early = split_rows(early, EARLY, devices)
    shares = {**early, **middle, **late}
    flat = shares["tiny"].reshape(-1)
    at = 0
    for n in GAINS + KERNELS:
        size = shards[n].size
        shares[n] = flat[at : at + size].reshape(shards[n].shape)
        at += size
    return (
        out_rows.reshape(micro, 1, F, D),
        dx.reshape(micro, 1, F, D),
        *(shares[n] for n in ORDER),
    )


def solution(mesh):
    split = P(AXES)
    split_rows = P(AXES, None)
    split_columns = P(None, AXES)
    spec = {n: split if n in GAINS else split_columns if n in KERNELS else split_rows for n in ORDER}
    weight_specs = tuple(spec[n] for n in ORDER)
    frame_spec = P(None, "seq", "head", None)
    return jax.shard_map(
        on_device,
        mesh=mesh,
        in_specs=(frame_spec, frame_spec, P(None, "seq", None)) + weight_specs,
        out_specs=(frame_spec, frame_spec) + weight_specs,
        check_vma=False,
    )
```

```python
import math

import jax
import jax.numpy as jnp
import numpy as np
from jax import lax
from jax.experimental import pallas as pl
from jax.experimental.pallas import tpu as pltpu
from jax.sharding import PartitionSpec as P

D = 512
HD = 64
KER = 31
GAP = 15
PAD = 16
EPSILON = 1e-05
AXES = ("head", "seq")
GROUP = 32
f32 = jnp.float32
bf16 = jnp.bfloat16

PACKS = {
    "a": (("head_projection", 48, 3), ("first_in", 64, 4)),
    "b": (("first_out", 64, 1), ("tiny", 16, 1)),
    "rest": (("gated_up", 96, 6), ("gated_down", 48, 1), ("output_projection", 16, 1), ("merge_weight", 32, 1)),
    "last": (("second_in", 64, 4), ("second_out", 64, 1)),
}
OFFSET = {}
SIZE = {}
BLOCKS = {}
for _pack in PACKS.values():
    _at = 0
    for _name, _rows, _blocks in _pack:
        OFFSET[_name], SIZE[_name], BLOCKS[_name] = _at, _rows, _blocks
        _at += _rows

ORDER = (
    "gain_first",
    "first_in",
    "first_out",
    "gain_attend",
    "head_projection",
    "output_projection",
    "gain_gated",
    "gated_up",
    "gain_gate",
    "kernel_gate",
    "gated_down",
    "kernel_merge",
    "merge_weight",
    "gain_second",
    "second_in",
    "second_out",
    "gain_final",
)
GAINS = ("gain_first", "gain_attend", "gain_gated", "gain_second", "gain_final", "gain_gate")
KERNELS = ("kernel_gate", "kernel_merge")


def mm(a, b):
    return jnp.dot(a, b, preferred_element_type=f32)


def mt(a, b):
    return lax.dot_general(a, b, (((1,), (1,)), ((), ())), preferred_element_type=f32)


def tm(a, b):
    return lax.dot_general(a, b, (((0,), (0,)), ((), ())), preferred_element_type=f32)


def norm(v):
    centre = v - jnp.mean(v, axis=-1, keepdims=True)
    scaling = lax.rsqrt(jnp.mean(centre * centre, axis=-1, keepdims=True) + EPSILON)
    return centre * scaling, scaling


def norm_back(vh, scaling, gain, dz):
    t = dz * gain
    dv = scaling * (
        t - jnp.mean(t, axis=-1, keepdims=True) - vh * jnp.mean(t * vh, axis=-1, keepdims=True)
    )
    return dv, jnp.sum(dz * vh, axis=0, keepdims=True)


def sigmoid(v):
    return 0.5 * jnp.tanh(0.5 * v) + 0.5


def call(kernel, name, out_shape, in_specs, out_specs, scratch=(), grid=(1,), us=10, aliases=None):
    return pl.pallas_call(
        kernel,
        name=name,
        out_shape=out_shape,
        grid=grid,
        in_specs=in_specs,
        out_specs=out_specs,
        scratch_shapes=list(scratch),
        input_output_aliases=aliases or {},
        compiler_params=pltpu.CompilerParams(
            vmem_limit_bytes=60 << 20, dimension_semantics=("arbitrary",) * len(grid)
        ),
        cost_estimate=pl.CostEstimate(
            flops=int(us * 5e8), bytes_accessed=int(us * 2.5e6), transcendentals=0
        ),
    )


def whole(shape):
    zeros = (0,) * len(shape)
    return pl.BlockSpec(shape, lambda *_: zeros)


SMEM = pl.BlockSpec(memory_space=pltpu.SMEM)


def columns_spec(name, pick, part=1):
    base = OFFSET[name] // 16
    return pl.BlockSpec((GROUP // part, 16, D), lambda j: (0, base + pick(j), 0))


def rows_spec(name, pick, part=1):
    rows = SIZE[name]
    base = OFFSET[name] // rows
    return pl.BlockSpec((D // rows // part, rows, D), lambda j: (pick(j), base, 0))


def whole_spec(name, part=1):
    rows = SIZE[name]
    base = OFFSET[name] // rows
    return pl.BlockSpec((GROUP // part, rows, D), lambda *_: (0, base, 0))


def join(side, pair, own, other):
    core = side[0]
    pair[:, pl.ds(core, 1)] = own[:, None]
    pair[:, pl.ds(1 - core, 1)] = other[:, None]
    return pair[...].reshape(D, D)


def part(side, pair, value):
    core = side[0]
    pair[...] = value.astype(bf16).reshape(pair.shape)
    return pair[:, pl.ds(core, 1)][:, 0], pair[:, pl.ds(1 - core, 1)][:, 0]


def sds(shape, dtype):
    return jax.ShapeDtypeStruct(shape, dtype)


def segments_of(meta, m, count, frames):
    base = meta[meta.shape[0] - 1]
    low, high, offset = [], [], []
    start = jnp.int32(0)
    rank = jnp.int32(0)
    before = jnp.int32(0)
    after = jnp.int32(0)
    for s in range(count):
        end = start + meta[m * count + s]
        lo = jnp.clip(start - base, 0, frames)
        hi = jnp.clip(end - base, 0, frames)
        low.append(lo)
        high.append(hi)
        offset.append(PAD + GAP * rank)
        rank = rank + (hi > lo).astype(jnp.int32)
        first = (start <= base) & (base < end)
        before = jnp.where(first, jnp.minimum(base - start, GAP), before)
        final = base + frames - 1
        last = (start <= final) & (final < end)
        after = jnp.where(last, jnp.minimum(end - final - 1, GAP), after)
        start = end
    return low, high, offset, before, after, frames + GAP * (rank - 1)


def clear(buf):
    def body(i, c):
        buf[pl.ds(pl.multiple_of(i * 64, 64), 64), :] = jnp.zeros((64, 128), f32)
        return c

    lax.fori_loop(0, buf.shape[0] // 64, body, 0)


def stage(seg, src, row0, frames, before, after, dst, blocks, sub0):
    low, high, offset, nb, na, length = seg
    for s in range(len(low)):
        lo, hi, off = low[s], high[s], offset[s]

        @pl.when(hi > lo)
        def _():
            def body(g, c):
                r = pl.multiple_of(g * 16, 16)
                for i, cb in enumerate(blocks):
                    x = src[pl.ds(row0 + r, 16), cb * 128 : (cb + 1) * 128].astype(f32)
                    dst[pl.ds((r + off) * 8 + sub0 + i, 16, stride=8), :] = x
                return c

            lax.fori_loop(lo // 16, (hi + 15) // 16, body, 0)

    n = len(blocks)
    for s in range(len(low) - 1):
        lo, hi, off = low[s], high[s], offset[s]

        @pl.when((hi > lo) & (hi < frames))
        def _():
            def body(i, c):
                q = (hi + off + i) * 8
                if n == 8:
                    dst[pl.ds(pl.multiple_of(q, 8), 8), :] = jnp.zeros((8, 128), f32)
                else:
                    dst[pl.ds(q + sub0, n), :] = jnp.zeros((n, 128), f32)
                return c

            lax.fori_loop(0, GAP, body, 0)

    if before is None:
        xb = jnp.zeros((16, 128), f32)
        for i, cb in enumerate(blocks):
            dst[pl.ds(sub0 + i, 16, stride=8), :] = xb
            dst[pl.ds((PAD + length) * 8 + sub0 + i, 16, stride=8), :] = xb
    else:
        rows = lax.broadcasted_iota(jnp.int32, (16, 128), 0)
        kb = rows >= 16 - nb
        ka = rows < na
        for i, cb in enumerate(blocks):
            xb = jnp.where(kb, before[:, cb * 128 : (cb + 1) * 128].astype(f32), 0.0)
            xa = jnp.where(ka, after[:, cb * 128 : (cb + 1) * 128].astype(f32), 0.0)
            dst[pl.ds(sub0 + i, 16, stride=8), :] = xb
            dst[pl.ds((PAD + length) * 8 + sub0 + i, 16, stride=8), :] = xa


def unstage(seg, src, dst, row0, blocks, sub0):
    low, high, offset = seg[:3]
    rows = lax.broadcasted_iota(jnp.int32, (16, 128), 0)
    for s in range(len(low)):
        lo, hi, off = low[s], high[s], offset[s]

        @pl.when(hi > lo)
        def _():
            def body(g, c):
                r = pl.multiple_of(g * 16, 16)
                keep = rows >= lo - r
                for i, cb in enumerate(blocks):
                    value = src[pl.ds((r + off) * 8 + sub0 + i, 16, stride=8), :]
                    at = (pl.ds(row0 + r, 16), slice(cb * 128, (cb + 1) * 128))
                    dst[at] = jnp.where(keep, value, dst[at])
                return c

            lax.fori_loop(lo // 16, (hi + 15) // 16, body, 0)


def convolve(length, taps, buf, out, flip):
    w = [taps[30 - k if flip else k] for k in range(KER)]

    def body(b, c):
        p0 = PAD + b * 8
        acc = [None] * 8
        for j in range(38):
            v = buf[pl.ds(pl.multiple_of((p0 - 15 + j) * 8, 8), 8), :]
            for o in range(8):
                k = j - o
                if 0 <= k < KER:
                    t = w[k] * v
                    acc[o] = t if acc[o] is None else acc[o] + t
        for o in range(8):
            out[pl.ds(pl.multiple_of((p0 + o) * 8, 8), 8), :] = acc[o]
        return c

    lax.fori_loop(0, (length + 7) // 8, body, 0)


def tap_sums(length, vbuf, gbuf):
    def body(b, acc):
        acc = list(acc)
        p0 = PAD + b * 8
        v = [vbuf[pl.ds(pl.multiple_of((p0 + o) * 8, 8), 8), :] for o in range(8)]
        for j in range(38):
            g = gbuf[pl.ds(pl.multiple_of((p0 - 15 + j) * 8, 8), 8), :]
            for o in range(8):
                k = o - j + 30
                if 0 <= k < KER:
                    acc[k] = acc[k] + v[o] * g
        return tuple(acc)

    zero = tuple(jnp.zeros((8, 128), f32) for _ in range(KER))
    return lax.fori_loop(0, (length + 7) // 8, body, zero)


def channel_groups(channels, micro):
    out = []
    for g in range(channels // 1024):
        for m in range(micro):
            out.append((g, tuple(range(8 * g, 8 * g + 8)), ((m, 0),)))
    if channels % 1024:
        blocks = tuple(range(channels // 1024 * 8, channels // 128))
        for m in range(0, micro, 2):
            out.append((channels // 1024, blocks, ((m, 0), (m + 1, 4))))
    return out


def gapped_rows(frames, count):
    return -(-(frames + GAP * (count - 1) + 2 * PAD + 16) // 8) * 8


def tap_layout(kernel):
    channels = kernel.shape[1]
    out = []
    for g in range(channels // 1024):
        out.append(kernel[:, g * 1024 : (g + 1) * 1024].reshape(KER, 8, 128))
    if channels % 1024:
        half = kernel[:, channels // 1024 * 1024 :].reshape(KER, 4, 128)
        out.append(jnp.concatenate([half, half], axis=1))
    return jnp.stack(out).astype(f32)


def tap_unlayout(taps, channels):
    out = [taps[g].reshape(KER, 1024) for g in range(channels // 1024)]
    if channels % 1024:
        out.append((taps[-1][:, :4] + taps[-1][:, 4:]).reshape(KER, 512))
    return jnp.concatenate(out, axis=1)


def put_edges(value, micro, frames, first_ref, last_ref):
    for m in range(micro):
        first_ref[m] = value[m * frames : m * frames + 16]
        last_ref[m] = value[(m + 1) * frames - 16 : (m + 1) * frames]


def first_kernel(
    nh, side, x_ref, gain_ref, wina_ref, winb_ref, wouta_ref, woutb_ref, hpa_ref, hpb_ref,
    mid_ref, qkv_ref, win_ref, wout_ref, hp_ref, n_ref, acc_ref, q_ref, wi_s, wo_s,
):
    j = pl.program_id(0)

    @pl.when(j == 0)
    def _():
        vh, _ = norm(x_ref[...].astype(f32))
        n_ref[...] = (vh * gain_ref[0:1, :]).astype(bf16)
        acc_ref[...] = jnp.zeros_like(acc_ref)

    win = join(side, wi_s, wina_ref[...], winb_ref[...])
    win_ref[0] = win
    p = mm(n_ref[...], win)
    h = (p * sigmoid(p)).astype(bf16)
    wout = join(side, wo_s, wouta_ref[...], woutb_ref[...])
    wout_ref[0] = wout
    acc_ref[...] += mm(h, wout)

    @pl.when(j == pl.num_programs(0) - 1)
    def _():
        mid = x_ref[...].astype(f32) + 0.5 * acc_ref[...]
        mid_ref[...] = mid
        vh, _ = norm(mid)
        n = (vh * gain_ref[1:2, :]).astype(bf16)
        for b in range(3):
            at = slice(16 * b, 16 * b + 16)
            w = join(side, wi_s, hpa_ref[:, at, :], hpb_ref[:, at, :])
            hp_ref[b] = w
            q_ref[:, D * b : D * b + D] = mm(n, w).astype(bf16)
        width = 3 * D // nh
        for i in range(nh):
            qkv_ref[i] = q_ref[:, width * i : width * i + width]


def up_kernel(
    micro, frames, mid_ref, gain_ref, ggate_ref, gu_ref,
    zl_ref, gp_ref, gn_ref, rs_ref, fe_ref, le_ref, n_ref, zr_ref,
):
    j = pl.program_id(0)

    @pl.when(j == 0)
    def _():
        vh, _ = norm(mid_ref[...])
        n_ref[...] = (vh * gain_ref[2:3, :]).astype(bf16)

    up = mm(n_ref[...], gu_ref[...].reshape(D, D))
    phi = 0.5 + 0.5 * lax.erf(up * (1.0 / math.sqrt(2.0)))
    z = up * phi
    slope = phi + up * (jnp.exp(-0.5 * up * up) * (1.0 / math.sqrt(2.0 * math.pi)))
    gp_ref[...] = slope.astype(bf16)

    @pl.when(j < 3)
    def _():
        zl_ref[...] = z.astype(bf16)

    @pl.when(j >= 3)
    def _():
        zr_ref[:, pl.ds(pl.multiple_of((j - 3) * D, D), D)] = z

    @pl.when(j == 5)
    def _():
        vh, r = norm(zr_ref[...])
        gn = (vh * ggate_ref[...]).astype(bf16)
        gn_ref[...] = gn
        rs_ref[...] = jnp.broadcast_to(r, rs_ref.shape)
        put_edges(gn, micro, frames, fe_ref, le_ref)


def swap_halves(v):
    half = v.shape[1] // 2
    return jnp.concatenate([v[:, half:], v[:, :half]], axis=1)


def segment_ids(meta, m, count, shape, axis, start):
    pos = lax.broadcasted_iota(jnp.int32, shape, axis) + start
    ids = jnp.zeros(shape, jnp.int32)
    end = jnp.int32(0)
    for s in range(count - 1):
        end = end + meta[m * count + s]
        ids = ids + (pos >= end).astype(jnp.int32)
    return ids


SCALE = 1.0 / math.sqrt(HD)


def attend_kernel(lh, count, meta, qkv_ref, cos_ref, sin_ref, o_ref, l_ref, q_s, k_s, v_s):
    nh, _, frames, width = qkv_ref.shape
    stream = nh * frames
    m = pl.program_id(0)
    x = qkv_ref[...].reshape(stream, width)
    cos, sin = cos_ref[...], sin_ref[...]
    for h in range(lh):
        c0 = h * 3 * HD
        q = x[:, c0 : c0 + HD].astype(f32)
        k = x[:, c0 + HD : c0 + 2 * HD].astype(f32)
        q_s[h] = (q * cos + swap_halves(q) * sin).astype(bf16)
        k_s[h] = (k * cos + swap_halves(k) * sin).astype(bf16)
        v_s[h] = x[:, c0 + 2 * HD : c0 + 3 * HD]
    key_seg = segment_ids(meta, m, count, (1, stream), 1, 0)

    def body(i, c):
        at = pl.multiple_of(i * frames, frames)
        row_seg = segment_ids(meta, m, count, (frames, 1), 0, at)
        same = row_seg == key_seg
        lane = lax.broadcasted_iota(jnp.int32, (frames, 128), 1)
        pieces = []
        logs = jnp.zeros((frames, 128), f32)
        for h in range(lh):
            s = mt(q_s[h, pl.ds(at, frames), :], k_s[h])
            s = jnp.where(same, s, -1e30)
            peak = jnp.max(s, axis=1, keepdims=True)
            p = jnp.exp((s - peak) * SCALE)
            total = jnp.sum(p, axis=1, keepdims=True)
            o = mm(p.astype(bf16), v_s[h]) / total
            pieces.append(o)
            logs = jnp.where(lane == h, peak * SCALE + jnp.log(total), logs)
        o_ref[i, 0] = jnp.concatenate(pieces, axis=1).astype(bf16) if lh > 1 else pieces[0].astype(bf16)
        l_ref[0, pl.ds(at, frames), :] = logs
        return c

    lax.fori_loop(0, nh, body, 0)


def attend_back_kernel(
    lh, count, meta, qkv_ref, cos_ref, sin_ref, o_ref, l_ref, do_ref, d_ref,
    q_s, k_s, v_s, do_s, qt_s, dot_s, dq_s, dk_s, dv_s,
):
    nh, _, frames, width = qkv_ref.shape
    stream = nh * frames
    m = pl.program_id(0)
    x = qkv_ref[...].reshape(stream, width)
    do = do_ref[...].reshape(stream, lh * HD)
    cos, sin = cos_ref[...], sin_ref[...]
    for h in range(lh):
        c0 = h * 3 * HD
        q = x[:, c0 : c0 + HD].astype(f32)
        k = x[:, c0 + HD : c0 + 2 * HD].astype(f32)
        q = q * cos + swap_halves(q) * sin
        q_s[h] = q.astype(bf16)
        qt_s[h] = q.T.astype(bf16)
        k_s[h] = (k * cos + swap_halves(k) * sin).astype(bf16)
        v_s[h] = x[:, c0 + 2 * HD : c0 + 3 * HD]
        piece = do[:, h * HD : (h + 1) * HD]
        do_s[h] = piece
        dot_s[h] = piece.astype(f32).T.astype(bf16)
    dk_s[...] = jnp.zeros_like(dk_s)
    dv_s[...] = jnp.zeros_like(dv_s)
    key_seg = segment_ids(meta, m, count, (1, stream), 1, 0)

    def body(i, c):
        at = pl.multiple_of(i * frames, frames)
        row_seg = segment_ids(meta, m, count, (frames, 1), 0, at)
        same = row_seg == key_seg
        lane = lax.broadcasted_iota(jnp.int32, (frames, 128), 1)
        logs = l_ref[0, pl.ds(at, frames), :]
        o = o_ref[i, 0].astype(f32)
        for h in range(lh):
            log = jnp.sum(jnp.where(lane == h, logs, 0.0), axis=1, keepdims=True)
            dh = do_s[h, pl.ds(at, frames), :]
            delta = jnp.sum(o[:, h * HD : (h + 1) * HD] * dh.astype(f32), axis=1, keepdims=True)
            s = mt(q_s[h, pl.ds(at, frames), :], k_s[h])
            p = jnp.where(same, jnp.exp(s * SCALE - log), 0.0)
            dp = mt(dh, v_s[h])
            dr = (p * (dp - delta)).astype(bf16)
            dq_s[h, pl.ds(at, frames), :] = mm(dr, k_s[h]) * SCALE
            dk_s[h] += mm(qt_s[h, :, pl.ds(at, frames)], dr)
            dv_s[h] += mm(dot_s[h, :, pl.ds(at, frames)], p.astype(bf16))
        return c

    lax.fori_loop(0, nh, body, 0)
    pieces = []
    for h in range(lh):
        dq = dq_s[h]
        dk = dk_s[h].T * SCALE
        pieces.append(dq * cos - swap_halves(dq) * sin)
        pieces.append(dk * cos - swap_halves(dk) * sin)
        pieces.append(dv_s[h].T)
    full = jnp.concatenate(pieces, axis=1).astype(bf16)
    for i in range(nh):
        d_ref[i, 0] = full[i * frames : (i + 1) * frames]


def gate_kernel(micro, frames, count, meta, gn_ref, hb_ref, ha_ref, zl_ref, wk_ref, gd_ref, gate_ref, c_ref, buf, res, out):
    segs = [segments_of(meta, m, count, frames) for m in range(micro)]
    clear(buf)
    for g, blocks, members in channel_groups(gn_ref.shape[1], micro):
        length = segs[members[0][0]][5]
        for m, sub in members:
            stage(segs[m], gn_ref, m * frames, frames, hb_ref.at[m], ha_ref.at[m], buf, blocks, sub)
            length = jnp.maximum(length, segs[m][5])
        convolve(length, wk_ref.at[g], buf, res, False)
        for m, sub in members:
            unstage(segs[m], res, out, m * frames, blocks, sub)
    gd = gd_ref[...].reshape(gn_ref.shape[1], D)
    for m in range(micro):
        at = slice(m * frames, (m + 1) * frames)
        gate = out[at, :]
        gate_ref[at, :] = gate.astype(bf16)
        u = (zl_ref[at, :].astype(f32) * gate).astype(bf16)
        c_ref[at, :] = mm(u, gd).astype(bf16)


def join_kernel(micro, frames, o_ref, c_ref, op_ref, jn_ref, fe_ref, le_ref):
    nh = o_ref.shape[0]
    o = jnp.concatenate([o_ref[i] for i in range(nh)], axis=1)
    a = mm(o, op_ref[...].reshape(D, D)).astype(bf16)
    jn_ref[:, :D] = a
    jn_ref[:, D:] = c_ref[...]
    for m in range(micro):
        first = slice(m * frames, m * frames + 16)
        last = slice((m + 1) * frames - 16, (m + 1) * frames)
        fe_ref[m, :, :D] = a[first]
        fe_ref[m, :, D:] = c_ref[first, :]
        le_ref[m, :, :D] = a[last]
        le_ref[m, :, D:] = c_ref[last, :]


def merge_kernel(micro, frames, count, meta, jn_ref, hb_ref, ha_ref, wk_ref, mw_ref, mid_ref, m_ref, mid2_ref, buf, res, out):
    segs = [segments_of(meta, m, count, frames) for m in range(micro)]
    clear(buf)
    for g, blocks, members in channel_groups(jn_ref.shape[1], micro):
        m = members[0][0]
        stage(segs[m], jn_ref, m * frames, frames, hb_ref.at[m], ha_ref.at[m], buf, blocks, 0)
        convolve(segs[m][5], wk_ref.at[g], buf, res, False)
        unstage(segs[m], res, out, m * frames, blocks, 0)
    mw = mw_ref[...].reshape(2 * D, D)
    for m in range(micro):
        at = slice(m * frames, (m + 1) * frames)
        mixed = (jn_ref[at, :].astype(f32) + out[at, :]).astype(bf16)
        m_ref[at, :] = mixed
        mid2_ref[at, :] = mid_ref[at, :] + mm(mixed, mw)


def silu_back(p, dh):
    s = sigmoid(p)
    return (p * s).astype(bf16), (s * (1.0 + p * (1.0 - s)) * dh).astype(bf16)


def second_kernel(
    micro, frames, mid2_ref, cot_ref, gain_ref, win_ref, wout_ref, mw_ref, mixed_ref,
    out_ref, dmid2_ref, dm_ref, fe_ref, le_ref, dw_ref, dgain_ref,
    n_ref, nt_ref, p_ref, acc_ref, dmid3_ref, df_ref,
):
    j = pl.program_id(0)
    nb = pl.num_programs(0) // 2

    @pl.when(j == 0)
    def _():
        vh, _ = norm(mid2_ref[...])
        n = vh * gain_ref[3:4, :]
        n_ref[...] = n.astype(bf16)
        nt_ref[...] = n.T.astype(bf16)
        acc_ref[...] = jnp.zeros_like(acc_ref)

    @pl.when(j < nb)
    def _():
        p = mm(n_ref[...], win_ref[...].reshape(D, D))
        p_ref[j] = p
        h = (p * sigmoid(p)).astype(bf16)
        acc_ref[...] += mm(h, wout_ref[...].reshape(D, D))

    @pl.when(j == nb - 1)
    def _():
        mid3 = mid2_ref[...] + 0.5 * acc_ref[...]
        vh, r = norm(mid3)
        gain = gain_ref[4:5, :]
        out_ref[...] = (vh * gain).astype(bf16)
        dmid3, dgain = norm_back(vh, r, gain, cot_ref[...].astype(f32))
        dgain_ref[1:2, :] = dgain
        dmid3_ref[...] = dmid3
        df_ref[...] = (0.5 * dmid3).astype(bf16)
        acc_ref[...] = jnp.zeros_like(acc_ref)

    @pl.when(j >= nb)
    def _():
        win = win_ref[...].reshape(D, D)
        dh = mt(df_ref[...], wout_ref[...].reshape(D, D))
        h, dp = silu_back(p_ref[2 * nb - 1 - j], dh)
        at = 2 * nb - 1 - j
        few = D // 64
        dw_ref[pl.ds(at * few, few), 64:128, :] = tm(h, df_ref[...]).astype(bf16).reshape(few, 64, D)
        dw_ref[:, pl.ds(pl.multiple_of(at * 16, 16), 16), :] = mm(nt_ref[...], dp).astype(bf16).reshape(GROUP, 16, D)
        acc_ref[...] += mt(dp, win)

    @pl.when(j == 2 * nb - 1)
    def _():
        vh, r = norm(mid2_ref[...])
        dv, dgain = norm_back(vh, r, gain_ref[3:4, :], acc_ref[...])
        dgain_ref[0:1, :] = dgain
        dmid2 = dmid3_ref[...] + dv
        dmid2_ref[...] = dmid2
        dmg = dmid2.astype(bf16)
        dw_ref[:, 128:, :] = tm(mixed_ref[...], dmg).astype(bf16).reshape(GROUP, 32, D)
        dm = mt(dmg, mw_ref[...].reshape(2 * D, D)).astype(bf16)
        dm_ref[...] = dm
        put_edges(dm, micro, frames, fe_ref, le_ref)


def merge_back_kernel(
    micro, frames, count, meta, dm_ref, hb_ref, ha_ref, jn_ref, wk_ref, op_ref,
    da_ref, dc_ref, do_ref, dk_ref, buf, vbuf, res, out,
):
    segs = [segments_of(meta, m, count, frames) for m in range(micro)]
    clear(buf)
    clear(vbuf)
    total = [None] * KER
    for g, blocks, members in channel_groups(dm_ref.shape[1], micro):
        m = members[0][0]
        stage(segs[m], dm_ref, m * frames, frames, hb_ref.at[m], ha_ref.at[m], buf, blocks, 0)
        stage(segs[m], jn_ref, m * frames, frames, None, None, vbuf, blocks, 0)
        convolve(segs[m][5], wk_ref.at[g], buf, res, True)
        sums = tap_sums(segs[m][5], vbuf, buf)
        for k in range(KER):
            dk_ref[g, k] = sums[k] if m == 0 else dk_ref[g, k] + sums[k]
        unstage(segs[m], res, out, m * frames, blocks, 0)
    nh = do_ref.shape[0]
    width = D // nh
    for m in range(micro):
        at = slice(m * frames, (m + 1) * frames)
        djn = dm_ref[at, :].astype(f32) + out[at, :]
        da = djn[:, :D].astype(bf16)
        da_ref[at, :] = da
        dc_ref[at, :] = djn[:, D:].astype(bf16)
        do = mt(da, op_ref[...].reshape(D, D)).astype(bf16)
        for i in range(nh):
            do_ref[i, at, :] = do[:, i * width : (i + 1) * width]


def gate_pre_kernel(
    micro, frames, side, dc_ref, da_ref, o_ref, zl_ref, gate_ref, gp_ref, gd_ref,
    kept_ref, sent_ref, dup_ref, dgate_ref, fe_ref, le_ref, gd_s, dgd_s, dop_s,
):
    j = pl.program_id(0)

    @pl.when(j == 0)
    def _():
        gd_s[...] = gd_ref[...].reshape(gd_s.shape)
        width = o_ref.shape[2]
        for i in range(o_ref.shape[0]):
            few = width // 32
            at = slice(i * few, (i + 1) * few)
            kept_ref[at, :16, :], sent_ref[at, :16, :] = part(side, dop_s, tm(o_ref[i], da_ref[...]))

    du = mt(dc_ref[...], gd_s[pl.ds(pl.multiple_of(j * D, D), D), :])
    gate = gate_ref[...].astype(f32)
    left = zl_ref[...].astype(f32)
    u = (left * gate).astype(bf16)
    dgd_s[pl.ds(pl.multiple_of(j * D, D), D), :] = tm(u, dc_ref[...]).astype(bf16)

    @pl.when(j == pl.num_programs(0) - 1)
    def _():
        for i in range(GROUP // 2):
            for ref, core in ((kept_ref, side[0]), (sent_ref, 1 - side[0])):
                ref[i, 16:, :] = dgd_s[pl.ds(pl.multiple_of((2 * i + core) * 48, 16), 48), :]

    dup_ref[...] = (gp_ref[...].astype(f32) * (du * gate)).astype(bf16)
    dgate = (du * left).astype(bf16)
    dgate_ref[...] = dgate
    put_edges(dgate, micro, frames, fe_ref, le_ref)


def gate_back_kernel(
    micro, frames, count, meta, dg_ref, hb_ref, ha_ref, gn_ref, rs_ref, ggate_ref, wk_ref, gp_ref,
    dup_ref, dk_ref, dgain_ref, buf, vbuf, res, out,
):
    segs = [segments_of(meta, m, count, frames) for m in range(micro)]
    clear(buf)
    clear(vbuf)
    seen = set()
    for g, blocks, members in channel_groups(dg_ref.shape[1], micro):
        length = segs[members[0][0]][5]
        if len(members) > 1:
            clear(buf)
            clear(vbuf)
        for m, sub in members:
            stage(segs[m], dg_ref, m * frames, frames, hb_ref.at[m], ha_ref.at[m], buf, blocks, sub)
            stage(segs[m], gn_ref, m * frames, frames, None, None, vbuf, blocks, sub)
            length = jnp.maximum(length, segs[m][5])
        convolve(length, wk_ref.at[g], buf, res, True)
        sums = tap_sums(length, vbuf, buf)
        for k in range(KER):
            dk_ref[g, k] = dk_ref[g, k] + sums[k] if g in seen else sums[k]
        seen.add(g)
        for m, sub in members:
            unstage(segs[m], res, out, m * frames, blocks, sub)
    gain = ggate_ref[...]
    inverse = 1.0 / gain
    for m in range(micro):
        at = slice(m * frames, (m + 1) * frames)
        vh = gn_ref[at, :].astype(f32) * inverse
        dv, dgain = norm_back(vh, rs_ref[at, 0:1], gain, out[at, :])
        dgain_ref[...] = dgain if m == 0 else dgain_ref[...] + dgain
        dup_ref[at, :] = (gp_ref[at, :].astype(f32) * dv).astype(bf16)


def up_back_kernel(
    side, mid_ref, dmid2_ref, gain_ref, dl_ref, dr_ref, gu_ref,
    dmid_ref, kept_ref, sent_ref, dgain_ref, nt_ref, acc_ref, pair_s,
):
    j = pl.program_id(0)

    @pl.when(j == 0)
    def _():
        vh, _ = norm(mid_ref[...])
        nt_ref[...] = (vh * gain_ref[2:3, :]).T.astype(bf16)
        acc_ref[...] = jnp.zeros_like(acc_ref)

    dup = jnp.where(j < 3, dl_ref[...], dr_ref[...])
    kept_ref[...], sent_ref[...] = part(side, pair_s, mm(nt_ref[...], dup))
    acc_ref[...] += mt(dup, gu_ref[...].reshape(D, D))

    @pl.when(j == pl.num_programs(0) - 1)
    def _():
        vh, r = norm(mid_ref[...])
        dv, dgain = norm_back(vh, r, gain_ref[2:3, :], acc_ref[...])
        dgain_ref[...] = dgain
        dmid_ref[...] = dmid2_ref[...] + dv


def first_back_kernel(
    side, x_ref, mid_ref, dml_ref, dq_ref, gain_ref, hp_ref, win_ref, wout_ref,
    dx_ref, dhpk_ref, dhps_ref, dwik_ref, dwis_ref, dwok_ref, dwos_ref, dgain_ref,
    dq_s, n_ref, nt_ref, dmid_ref, df_ref, acc_ref, pi_s, po_s,
):
    j = pl.program_id(0)

    @pl.when(j == 0)
    def _():
        nh, _, width = dq_ref.shape
        for i in range(nh):
            dq_s[:, i * width : (i + 1) * width] = dq_ref[i]
        vh, r = norm(mid_ref[...])
        gain = gain_ref[1:2, :]
        nt = (vh * gain).T.astype(bf16)
        dn = None
        for b in range(3):
            dq = dq_s[:, b * D : (b + 1) * D]
            at = slice(16 * b, 16 * b + 16)
            dhpk_ref[:, at, :], dhps_ref[:, at, :] = part(side, pi_s, mm(nt, dq))
            t = mt(dq, hp_ref[b])
            dn = t if dn is None else dn + t
        dv, dgain = norm_back(vh, r, gain, dn)
        dgain_ref[1:2, :] = dgain
        dmid = dml_ref[...] + dv
        dmid_ref[...] = dmid
        df_ref[...] = (0.5 * dmid).astype(bf16)
        vh, _ = norm(x_ref[...].astype(f32))
        n = vh * gain_ref[0:1, :]
        n_ref[...] = n.astype(bf16)
        nt_ref[...] = n.T.astype(bf16)
        acc_ref[...] = jnp.zeros_like(acc_ref)

    win = win_ref[0]
    p = mm(n_ref[...], win)
    dh = mt(df_ref[...], wout_ref[0])
    h, dp = silu_back(p, dh)
    dwok_ref[...], dwos_ref[...] = part(side, po_s, tm(h, df_ref[...]))
    dwik_ref[...], dwis_ref[...] = part(side, pi_s, mm(nt_ref[...], dp))
    acc_ref[...] += mt(dp, win)

    @pl.when(j == pl.num_programs(0) - 1)
    def _():
        vh, r = norm(x_ref[...].astype(f32))
        dv, dgain = norm_back(vh, r, gain_ref[0:1, :], acc_ref[...])
        dgain_ref[0:1, :] = dgain
        dx_ref[...] = dmid_ref[...] + dv


def to_rows(shard):
    rows, cols = shard.shape
    if cols == D:
        return shard
    return shard.reshape(rows, cols // D, D).transpose(1, 0, 2).reshape(rows * cols // D, D)


def canonical(part, name):
    count = part.shape[0]
    q = count // GROUP
    if q == 1:
        return part
    blocks = BLOCKS[name]
    rows = part.shape[1] // blocks
    part = part.reshape(GROUP, q, blocks, rows, D).transpose(0, 2, 1, 3, 4)
    return part.reshape(GROUP, blocks * q * rows, D)


def by_device(part, name, count):
    q = count // GROUP
    if q == 1:
        return part
    blocks = BLOCKS[name]
    rows = part.shape[1] // blocks // q
    part = part.reshape(GROUP, blocks, q, rows, D).transpose(0, 2, 1, 3, 4)
    return part.reshape(count, blocks * rows, D)


def bit_of(index, bit):
    return (index >> bit) & 1


def swap(v, bit, count):
    return lax.ppermute(v, AXES, [(i, i ^ (1 << bit)) for i in range(count)])


def exchange_gather(shards, count, waiting):
    me = lax.axis_index(AXES)
    bits = count.bit_length() - 1
    top, rest = [bits - 2, bits - 1], list(range(1, bits - 2))
    out = []
    for v, order in zip(shards, (rest[::-1] + top, rest[::-1] + top[::-1])):
        held = []
        for bit in order:
            other = swap(v, bit, count)
            mine = bit_of(me, bit) == 1
            held = sorted(held + [bit], reverse=True)
            if waiting is not None and not out:
                other, waiting = lax.optimization_barrier((other, waiting))
                released, waiting = waiting, None
            v = jnp.stack([jnp.where(mine, other, v), jnp.where(mine, v, other)], axis=held.index(bit))
        v = v.reshape((count // 2,) + v.shape[-2:])
        out.append((v, swap(v, 0, count)))
    return out, released


def whole_pack(own, other):
    mine = bit_of(lax.axis_index(AXES), 0) == 1
    both = jnp.stack([jnp.where(mine, other, own), jnp.where(mine, own, other)], axis=1)
    return both.reshape((-1,) + own.shape[1:])


def unpack(raw, pack):
    q = raw.shape[0] // GROUP
    if q == 1:
        return raw
    return jnp.concatenate(
        [canonical(raw[:, OFFSET[n] // q : (OFFSET[n] + SIZE[n]) // q], n) for n, r, b in PACKS[pack]], axis=1
    )


def gather_weights(shards, count):
    q = count // GROUP
    tiny = jnp.concatenate([shards[n].reshape(-1) for n in GAINS + KERNELS])
    tiny = jnp.pad(tiny, (0, SIZE["tiny"] // q * D - tiny.shape[0])).reshape(-1, D)
    rows = {n: tiny if n == "tiny" else to_rows(shards[n]) for n in SIZE}
    packed = {k: jnp.concatenate([rows[n] for n, r, b in pack], axis=0) for k, pack in PACKS.items()}
    pairs, released = exchange_gather([packed["a"], packed["b"]], count, packed["rest"])
    pairs = dict(zip("ab", pairs))
    raw = {"rest": lax.all_gather(released, AXES, axis=0, tiled=False)}
    full = {"rest": unpack(raw["rest"], "rest"), "last": packed["last"]}
    for k in pairs:
        if q == 1:
            full[k] = pairs[k]
        else:
            v = unpack(whole_pack(*pairs[k]), k)
            full[k] = (v[0::2], v[1::2])
    tiny = whole_pack(*(v[:, OFFSET["tiny"] // q :] for v in pairs["b"])).reshape(count, -1)
    unit = shards["gain_first"].shape[0]
    gains = tiny[:, : 5 * unit].astype(f32).reshape(count, 5, unit).transpose(1, 0, 2).reshape(5, D)
    gains = jnp.pad(gains, ((0, 3), (0, 0)))
    at = 5 * unit
    size = shards["gain_gate"].shape[0]
    gate_gain = tiny[:, at : at + size].astype(f32).reshape(1, -1)
    at += size
    kernels = []
    for n in KERNELS:
        taps, cols = shards[n].shape
        part = tiny[:, at : at + taps * cols].reshape(count, taps, cols)
        kernels.append(tap_layout(part.transpose(1, 0, 2).reshape(taps, count * cols)))
        at += taps * cols
    return full, gains, gate_gain, kernels


class Exchange:
    def __init__(self, pieces, count):
        self.count = count
        self.names = [n for names, _ in pieces for n in names]
        self.me = lax.axis_index(AXES)
        self.bits = count.bit_length() - 1
        core = bit_of(self.me, 0)
        self.kept, self.sent = [], []
        for names, arrays in pieces:
            if names == ("tiny",):
                arrays = [arrays]
            elif count == GROUP:
                self.kept.append(arrays[0])
                self.sent.append(arrays[1])
                continue
            else:
                packed = jnp.stack(arrays, axis=1).reshape(GROUP, -1, D)
                arrays = [by_pieces(packed, names, count)]
            for p in arrays:
                p = p.reshape(count // 2, 2, p.shape[1], D)
                self.kept.append(self.pick(p, 1, core))
                self.sent.append(self.pick(p, 1, 1 - core))

    def pick(self, v, axis, at):
        return lax.dynamic_index_in_dim(v, at, axis, keepdims=False)

    def pair(self):
        sums = [p + swap(v, 0, self.count) for p, v in zip(self.kept, self.sent)]
        at = sum(p.shape[1] for p in sums)
        half = at // 2 // 16 * 16
        rows = jnp.concatenate(sums, axis=1)
        top, rest = [self.bits - 2, self.bits - 1], list(range(1, self.bits - 2))
        self.orders = [top + rest, top[::-1] + rest]
        self.left = [list(range(self.bits - 1, 0, -1)) for _ in range(2)]
        self.lanes = [
            v.reshape((2,) * (self.bits - 1) + v.shape[1:]) for v in (rows[:, :half], rows[:, half:])
        ]

    def step(self):
        for i in range(2):
            bit = self.orders[i].pop(0)
            axis = self.left[i].index(bit)
            self.left[i].remove(bit)
            mine = bit_of(self.me, bit)
            v = self.lanes[i]
            self.lanes[i] = self.pick(v, axis, mine) + swap(self.pick(v, axis, 1 - mine), bit, self.count)

    def finish(self):
        while self.orders[0]:
            self.step()
        return split_rows(jnp.concatenate(self.lanes, axis=0), self.names, self.count)


def split_rows(got, names, count):
    q = count // GROUP
    out = {}
    at = 0
    for n in names:
        size = SIZE[n] // q
        part = got[at : at + size].astype(f32)
        at += size
        if n != "tiny":
            blocks = BLOCKS[n]
            rows = part.shape[0] // blocks
            part = part.reshape(blocks, rows, D).transpose(1, 0, 2).reshape(rows, blocks * D)
        out[n] = part
    return out


EARLY = ("second_in", "second_out", "merge_weight")


def by_pieces(packed, names, count):
    if count == GROUP:
        return packed
    parts = []
    at = 0
    for n in names:
        parts.append(by_device(packed[:, at : at + SIZE[n]], n, count))
        at += SIZE[n]
    if at < packed.shape[1]:
        parts.append(packed[:, at:].reshape(count, -1, D))
    return jnp.concatenate(parts, axis=1)


def rope_tables(stream):
    half = HD // 2
    frequency = np.exp(np.arange(half, dtype=np.float32) * np.float32(-math.log(10000.0) / half))
    angles = np.arange(stream, dtype=np.float32)[:, None] * frequency.astype(np.float32)[None, :]
    cos, sin = np.cos(angles), np.sin(angles)
    return (
        jnp.asarray(np.concatenate([cos, cos], axis=1), f32),
        jnp.asarray(np.concatenate([-sin, sin], axis=1), f32),
    )


def on_device(frames, cotangent, lengths, *weights):
    shards = dict(zip(ORDER, weights))
    nh = lax.axis_size("head")
    devices = nh * lax.axis_size("seq")
    micro, _, F, _ = frames.shape
    T = micro * F
    lh = D // HD // nh
    W = 3 * D // nh
    O = lh * HD
    S = nh * F
    U = lengths.shape[2]
    FF = 4 * D
    CH = 3 * D
    meta = jnp.concatenate(
        [lengths.reshape(-1), (lax.axis_index("head") * F).astype(jnp.int32).reshape(1)]
    ).astype(jnp.int32)
    packs, gains, gate_gain, (gate_taps, merge_taps) = gather_weights(shards, devices)
    EA, EB, E = packs["a"], packs["b"], packs["rest"]
    core = lax.axis_index(AXES) & 1 if devices == GROUP else 0
    side = jnp.asarray(core, jnp.int32).reshape(1)
    x = frames.reshape(T, D)
    cot = cotangent.reshape(T, D)
    up = [(i, i + 1) for i in range(nh - 1)]
    down = [(i + 1, i) for i in range(nh - 1)]

    def halo(first, last):
        return lax.ppermute(last, "head", up), lax.ppermute(first, "head", down)

    def exchange(v):
        return lax.all_to_all(v, "head", split_axis=0, concat_axis=0, tiled=True)

    def bind(kernel, *args):
        def bound(*refs):
            return kernel(*args, *refs)

        return bound

    rows = lambda c, d: sds((T, c), d)
    full = lambda c: whole((T, c))
    edge = lambda c: sds((micro, 16, c), bf16)
    edge_spec = lambda c: whole((micro, 16, c))
    vm = pltpu.VMEM
    PR = gapped_rows(F, U)
    buf = vm((PR * 8, 128), f32)
    nb = FF // D
    same = lambda j: j

    first_in_specs = [columns_spec("first_in", same, 2)] * 2
    first_out_specs = [rows_spec("first_out", same, 2)] * 2
    head_specs = [whole_spec("head_projection", 2)] * 2
    columns_pair = vm((GROUP // 2, 2, 16, D), bf16)
    rows_pair = vm((D // 128, 2, 64, D), bf16)
    half_columns = pl.BlockSpec((GROUP // 2, 16, D), lambda j: (0, j, 0))
    half_rows = pl.BlockSpec((D // 128, 64, D), lambda j: (j, 0, 0))
    half = lambda r: sds((GROUP // 2, r, D), bf16)

    square = pl.BlockSpec((1, D, D), lambda j: (j, 0, 0))
    mid1, qkv, first_in, first_out, head = call(
        bind(first_kernel, nh), "first",
        (
            rows(D, f32), sds((nh, T, W), bf16),
            sds((nb, D, D), bf16), sds((nb, D, D), bf16), sds((3, D, D), bf16),
        ),
        [SMEM, full(D), whole((8, D)), *first_in_specs, *first_out_specs, *head_specs],
        (full(D), whole((nh, T, W)), square, square, whole((3, D, D))),
        [vm((T, D), bf16), vm((T, D), f32), vm((T, 3 * D), bf16), columns_pair, rows_pair],
        grid=(nb,), us=8,
    )(side, x, gains, *EA, *EB, *EA)
    qkv_r = exchange(qkv).reshape(nh, micro, F, W)
    mid1, last = lax.optimization_barrier((mid1, packs["last"]))
    EL = unpack(lax.all_gather(last, AXES, axis=0, tiled=False), "last")

    zl, gp, gn, rs, fe, le = call(
        bind(up_kernel, micro, F), "up",
        (rows(CH, bf16), rows(2 * CH, bf16), rows(CH, bf16), rows(128, f32), edge(CH), edge(CH)),
        [full(D), whole((8, D)), whole((1, CH)), columns_spec("gated_up", same)],
        (
            pl.BlockSpec((T, D), lambda j: (0, jnp.minimum(j, 2))),
            pl.BlockSpec((T, D), lambda j: (0, j)),
            full(CH), full(128), edge_spec(CH), edge_spec(CH),
        ),
        [vm((T, D), bf16), vm((T, CH), f32)],
        grid=(6,), us=15,
    )(mid1, gains, gate_gain, E)
    gate_b, gate_a = halo(fe, le)

    cos, sin = rope_tables(S)
    qkv_spec = pl.BlockSpec((nh, 1, F, W), lambda m: (0, m, 0, 0))
    o_spec = pl.BlockSpec((nh, 1, F, O), lambda m: (0, m, 0, 0))
    l_spec = pl.BlockSpec((1, S, 128), lambda m: (m, 0, 0))
    head_buf = vm((lh, S, HD), bf16)
    o_own, logs = call(
        bind(attend_kernel, lh, U), "attend",
        (sds((nh, micro, F, O), bf16), sds((micro, S, 128), f32)),
        [SMEM, qkv_spec, whole((S, HD)), whole((S, HD))],
        (o_spec, l_spec),
        [head_buf] * 3,
        grid=(micro,), us=12,
    )(meta, qkv_r, cos, sin)
    o_r = exchange(o_own.reshape(nh, T, O))

    gate, c = call(
        bind(gate_kernel, micro, F, U), "gate",
        (rows(CH, bf16), rows(D, bf16)),
        [SMEM, full(CH), edge_spec(CH), edge_spec(CH), full(CH), whole(gate_taps.shape), whole_spec("gated_down")],
        (full(CH), full(D)),
        [buf, buf, vm((T, CH), f32)],
        us=18,
    )(meta, gn, gate_b, gate_a, zl, gate_taps, E)

    jn, fe, le = call(
        bind(join_kernel, micro, F), "join",
        (rows(2 * D, bf16), edge(2 * D), edge(2 * D)),
        [whole((nh, T, O)), full(D), whole_spec("output_projection")],
        (full(2 * D), edge_spec(2 * D), edge_spec(2 * D)),
        us=2,
    )(o_r, c, E)
    jn_b, jn_a = halo(fe, le)

    mixed, mid2 = call(
        bind(merge_kernel, micro, F, U), "merge",
        (rows(2 * D, bf16), rows(D, f32)),
        [SMEM, full(2 * D), edge_spec(2 * D), edge_spec(2 * D), whole(merge_taps.shape), whole_spec("merge_weight"), full(D)],
        (full(2 * D), full(D)),
        [buf, buf, vm((T, 2 * D), f32)],
        us=12,
    )(meta, jn, jn_b, jn_a, merge_taps, E, mid1)

    there_back = lambda j: jnp.where(j < nb, j, 2 * nb - 1 - j)
    out_rows, dmid2, dm, fe, le, d_early, dgain2 = call(
        bind(second_kernel, micro, F), "second",
        (
            rows(D, bf16), rows(D, f32), rows(2 * D, bf16), edge(2 * D), edge(2 * D),
            sds((GROUP, 192, D), bf16), sds((8, D), f32),
        ),
        [full(D), full(D), whole((8, D)), columns_spec("second_in", there_back), rows_spec("second_out", there_back), whole_spec("merge_weight"), full(2 * D)],
        (
            full(D), full(D), full(2 * D), edge_spec(2 * D), edge_spec(2 * D),
            whole((GROUP, 160, D)),
            whole((8, D)),
        ),
        [vm((T, D), bf16), vm((D, T), bf16), vm((nb, T, D), f32), vm((T, D), f32), vm((T, D), f32), vm((T, D), bf16)],
        grid=(2 * nb,), us=25,
    )(mid2, cot, gains, EL, EL, E, mixed)
    early = lax.psum_scatter(
        by_pieces(d_early, EARLY, devices).reshape(-1, D), AXES, scatter_dimension=0, tiled=True
    )
    dm_b, dm_a = halo(fe, le)

    da, dc, do, merge_sums = call(
        bind(merge_back_kernel, micro, F, U), "merge_back",
        (rows(D, bf16), rows(D, bf16), sds((nh, T, O), bf16), sds(merge_taps.shape, f32)),
        [SMEM, full(2 * D), edge_spec(2 * D), edge_spec(2 * D), full(2 * D), whole(merge_taps.shape), whole_spec("output_projection")],
        (full(D), full(D), whole((nh, T, O)), whole(merge_taps.shape)),
        [buf, buf, buf, vm((T, 2 * D), f32)],
        us=20,
    )(meta, dm, dm_b, dm_a, jn, merge_taps, E)
    do_r = exchange(do).reshape(nh, micro, F, O)

    column = pl.BlockSpec((T, D), lambda j: (0, j))
    edge_column = pl.BlockSpec((micro, 16, D), lambda j: (0, 0, j))
    *d_down, dup_l, dgate, fe, le = call(
        bind(gate_pre_kernel, micro, F), "gate_pre",
        (half(64), half(64), rows(CH, bf16), rows(CH, bf16), edge(CH), edge(CH)),
        [SMEM, full(D), full(D), whole((nh, T, O)), column, column, column, whole_spec("gated_down")],
        (whole((GROUP // 2, 64, D)), whole((GROUP // 2, 64, D)), column, column, edge_column, edge_column),
        [vm((CH, D), bf16), vm((CH, D), bf16), vm((O // 32, 2, 16, D), bf16)],
        grid=(3,), us=8,
    )(side, dc, da, o_r, zl, gate, gp, E)
    dg_b, dg_a = halo(fe, le)

    dqkv = call(
        bind(attend_back_kernel, lh, U), "attend_back",
        sds((nh, micro, F, W), bf16),
        [SMEM, qkv_spec, whole((S, HD)), whole((S, HD)), o_spec, l_spec, o_spec],
        qkv_spec,
        [head_buf] * 4 + [vm((lh, HD, S), bf16)] * 2 + [vm((lh, S, HD), f32)] + [vm((lh, HD, S), f32)] * 2,
        grid=(micro,), us=1,
    )(meta, qkv_r, cos, sin, o_own, logs, do_r)
    dgate, dqkv, dg_b, dg_a = lax.optimization_barrier((dgate, dqkv, dg_b, dg_a))
    dqkv_r = exchange(dqkv.reshape(nh, T, W))

    dup_r, gate_sums, dgain_gate = call(
        bind(gate_back_kernel, micro, F, U), "gate_back",
        (rows(CH, bf16), sds(gate_taps.shape, f32), sds((1, CH), f32)),
        [
            SMEM, full(CH), edge_spec(CH), edge_spec(CH), full(CH), full(128), whole((1, CH)), whole(gate_taps.shape),
            pl.BlockSpec((T, CH), lambda *_: (0, 1)),
        ],
        (full(CH), whole(gate_taps.shape), whole((1, CH))),
        [buf, buf, buf, vm((T, CH), f32)],
        us=1,
    )(meta, dgate, dg_b, dg_a, gn, rs, gate_gain, gate_taps, gp)

    dup_r, dqkv_r = lax.optimization_barrier((dup_r, dqkv_r))
    dml, *d_up, dgain3 = call(
        up_back_kernel, "up_back",
        (rows(D, f32), half(96), half(96), sds((1, D), f32)),
        [
            SMEM, full(D), full(D), whole((8, D)),
            pl.BlockSpec((T, D), lambda j: (0, jnp.minimum(j, 2))),
            pl.BlockSpec((T, D), lambda j: (0, jnp.maximum(j - 3, 0))),
            columns_spec("gated_up", same),
        ],
        (full(D), half_columns, half_columns, whole((1, D))),
        [vm((D, T), bf16), vm((T, D), f32), columns_pair],
        grid=(6,), us=1,
    )(side, mid1, dmid2, gains, dup_l, dup_r, E)

    middle = Exchange([(("gated_up",), d_up), (("output_projection", "gated_down"), d_down)], devices)
    middle.pair()
    dml, middle.lanes = lax.optimization_barrier((dml, middle.lanes))

    dx, d_head_k, d_head_s, d_in_k, d_in_s, d_out_k, d_out_s, dgain1 = call(
        first_back_kernel, "first_back",
        (
            rows(D, f32), half(48), half(48), half(64), half(64), half(64), half(64), sds((8, D), f32),
        ),
        [
            SMEM, full(D), full(D), full(D), whole((nh, T, W)), whole((8, D)),
            whole((3, D, D)), square, square,
        ],
        (
            full(D), whole((GROUP // 2, 48, D)), whole((GROUP // 2, 48, D)),
            half_columns, half_columns, half_rows, half_rows, whole((8, D)),
        ),
        [
            vm((T, 3 * D), bf16), vm((T, D), bf16), vm((D, T), bf16), vm((T, D), f32), vm((T, D), bf16), vm((T, D), f32),
            columns_pair, rows_pair,
        ],
        grid=(nb,), us=1,
    )(side, x, mid1, dml, dqkv_r, gains, head, first_in, first_out)

    grads = {
        "gain_first": dgain1[0],
        "gain_attend": dgain1[1],
        "gain_gated": dgain3[0],
        "gain_second": dgain2[0],
        "gain_final": dgain2[1],
        "gain_gate": dgain_gate[0],
        "kernel_gate": tap_unlayout(gate_sums, CH),
        "kernel_merge": tap_unlayout(merge_sums, 2 * D),
    }
    tiny = [grads[n].reshape(devices, -1) for n in GAINS]
    for n in KERNELS:
        cols = grads[n].shape[1] // devices
        tiny.append(grads[n].reshape(KER, devices, cols).transpose(1, 0, 2).reshape(devices, -1))
    tiny = jnp.concatenate(tiny, axis=1).astype(bf16)
    tiny_rows = SIZE["tiny"] * GROUP // devices
    tiny = jnp.pad(tiny, ((0, 0), (0, tiny_rows * D - tiny.shape[1]))).reshape(devices, tiny_rows, D)
    late = Exchange(
        [
            (("head_projection",), (d_head_k, d_head_s)), (("first_in",), (d_in_k, d_in_s)),
            (("first_out",), (d_out_k, d_out_s)), (("tiny",), tiny),
        ],
        devices,
    )
    middle.step()
    late.sent, middle.lanes, early = lax.optimization_barrier((late.sent, middle.lanes, early))
    middle.step()
    late.pair()
    late.lanes, middle.lanes = lax.optimization_barrier((late.lanes, middle.lanes))
    late.step()
    while middle.orders[0]:
        middle.step()
    late.lanes, middle.lanes = lax.optimization_barrier((late.lanes, middle.lanes))
    late = late.finish()
    middle = middle.finish()
    early = split_rows(early, EARLY, devices)
    shares = {**early, **middle, **late}
    flat = shares["tiny"].reshape(-1)
    at = 0
    for n in GAINS + KERNELS:
        size = shards[n].size
        shares[n] = flat[at : at + size].reshape(shards[n].shape)
        at += size
    return (
        out_rows.reshape(micro, 1, F, D),
        dx.reshape(micro, 1, F, D),
        *(shares[n] for n in ORDER),
    )


def solution(mesh):
    split = P(AXES)
    split_rows = P(AXES, None)
    split_columns = P(None, AXES)
    spec = {n: split if n in GAINS else split_columns if n in KERNELS else split_rows for n in ORDER}
    weight_specs = tuple(spec[n] for n in ORDER)
    frame_spec = P(None, "seq", "head", None)
    return jax.shard_map(
        on_device,
        mesh=mesh,
        in_specs=(frame_spec, frame_spec, P(None, "seq", None)) + weight_specs,
        out_specs=(frame_spec, frame_spec) + weight_specs,
        check_vma=False,
    )
```
